32 devices in a mesh: dp: 8 (over z, y), tensor: 4 (over x, core).
Axes of the slice: x: 2, y: 2, z: 4, core: 2. Of those that a mesh axis runs over, the one named last changes fastest.
Arguments:
- tokens: bfloat16 [8, 1536, 768], P('dp'), may hold values from -6 to 6
- timesteps: int32 [8], P('dp'), may hold values from 0 to 999
- piece_starts: int32 [8, 3], P('dp'), may hold values from 0 to 1280, as said below
- step_table: bfloat16 [1000, 768], replicated, may hold values from -4 to 4
- first_gain: float32 [768], replicated, may hold values from 0.5 to 1.5
- first_shift: float32 [768], replicated, may hold values from -2 to 2
- w_query: bfloat16 [768, 768], P(None, 'tensor'), may hold values from -0.3125 to 0.3125
- b_query: float32 [768], P('tensor'), may hold values from -2 to 2
- w_key: bfloat16 [768, 768], P(None, 'tensor'), may hold values from -0.3125 to 0.3125
- w_value: bfloat16 [768, 768], P(None, 'tensor'), may hold values from -0.21875 to 0.21875
- b_value: float32 [768], P('tensor'), may hold values from -2 to 2
- w_out: bfloat16 [768, 768], P('tensor'), may hold values from -0.875 to 0.875
- b_out: float32 [768], replicated, may hold values from -2 to 2
- second_gain: float32 [768], replicated, may hold values from 0.5 to 1.5
- second_shift: float32 [768], replicated, may hold values from -2 to 2
- w_in: bfloat16 [768, 3072], P(None, 'tensor'), may hold values from -0.21875 to 0.21875
- b_in: float32 [3072], P('tensor'), may hold values from -2 to 2
- w_down: bfloat16 [3072, 768], P('tensor'), may hold values from -0.109375 to 0.109375
- b_down: float32 [768], replicated, may hold values from -2 to 2
- cotangent: bfloat16 [8, 1536, 768], P('dp'), may hold values from -6 to 6
Outputs:
- output: bfloat16 [8, 1536, 768], P('dp')
- grad_tokens: bfloat16 [8, 1536, 768], P('dp')
- grad_step_table: float32 [1000, 768], replicated
- grad_first_gain: float32 [768], replicated
- grad_first_shift: float32 [768], replicated
- grad_w_query: float32 [768, 768], P(None, 'tensor')
- grad_b_query: float32 [768], P('tensor')
- grad_w_key: float32 [768, 768], P(None, 'tensor')
- grad_w_value: float32 [768, 768], P(None, 'tensor')
- grad_b_value: float32 [768], P('tensor')
- grad_w_out: float32 [768, 768], P('tensor')
- grad_b_out: float32 [768], replicated
- grad_second_gain: float32 [768], replicated
- grad_second_shift: float32 [768], replicated
- grad_w_in: float32 [768, 3072], P(None, 'tensor')
- grad_b_in: float32 [3072], P('tensor')
- grad_w_down: float32 [3072, 768], P('tensor')
- grad_b_down: float32 [768], replicated
The draws below stay inside these ranges and needn't reach their ends.
Inputs may be any that keep to these rules, and one draw needn't show every extreme that they name: `piece_starts`: piece k of a sequence starts between 2 * k * 256 and 2 * k * 256 + 256, so pieces of 256 tokens lie inside their sequence, in order, without intersection.
All inputs are finite; a program needn't handle non-finite values.
Results may differ from the reference program's by a relative error of at most 0.02.
Values may be sent and summed in bfloat16 or wider, within the bound.
No kernel may reach another device: no remote copies, remote signals or barrier semaphores. Data moves between devices by JAX's collectives and lax.ppermute only.
A program may use at most 128 MiB of HBM per device.

```python
import jax
import jax.numpy as jnp
from jax import lax

D = 768
H = 12
HD = 64
FF = 3072
STEPS = 1000
LEN = 1536
PIECE = 256
PIECES = 3
SEQS = 8
N_TENSOR = 4


def draw_piece_starts(key, part):
    key_off = jax.random.fold_in(key, 11)
    key_first = jax.random.fold_in(key, 12)
    key_last = jax.random.fold_in(key, 13)
    offsets = jax.random.randint(key_off, (SEQS, PIECES), 0, PIECE + 1).astype(jnp.int32)
    first_seq = jax.random.randint(key_first, (), 0, SEQS)
    last_seq = jax.random.randint(key_last, (), 0, SEQS)
    offsets = offsets.at[first_seq, 0].set(0)
    offsets = offsets.at[last_seq, PIECES - 1].set(PIECE)
    bases = jnp.arange(PIECES, dtype=jnp.int32)[None, :] * (2 * PIECE)
    return (bases + offsets).astype(jnp.int32)


def place_ends(entries, key, low, largest):
    longest = entries.shape.index(max(entries.shape))
    spots = []
    for shift in (0, 1):
        where = [jax.random.randint(jax.random.fold_in(key, axis), (), 0, length) for axis, length in enumerate(entries.shape)]
        where[longest] = (where[longest] + shift) % entries.shape[longest]
        spots.append(tuple(where))
    return entries.at[spots[0]].set(low).at[spots[1]].set(largest)


def block_scale(key, shape, pieces, smallest, high):
    level, own = 1.0, jax.random.fold_in(key, 6)
    for position, shards_of in pieces:
        heights = jnp.exp(jax.random.uniform(jax.random.fold_in(own, position), (shards_of,), jnp.float32, smallest / len(pieces), high / len(pieces)))
        level = level * jnp.repeat(heights, shape[position] // shards_of).reshape([-1 if axis == position else 1 for axis in range(len(shape))])
    return level


def bell_draw(own_key, extent, scale, reach, cuts=(), kind=jnp.bfloat16):
    values = jax.random.normal(own_key, extent, jnp.float32) * scale
    if len(cuts) > 0:
        values = block_scale(own_key, extent, cuts, -0.22, 0.18) * values
    return jnp.clip(values, min=-reach, max=reach).astype(kind)


def setup_inputs(seed: int = 0) -> dict:
    splits = jax.random.split(jax.random.key(seed), 21)
    tokens = bell_draw(splits[0], (SEQS, LEN, D), 1.0, 6.0, ((0, 8),))
    timesteps = place_ends(jax.random.randint(splits[1], (SEQS,), 0, STEPS), jax.random.fold_in(splits[1], 1), 0, STEPS - 1).astype(jnp.int32)
    piece_starts = draw_piece_starts(jax.random.fold_in(splits[20], 71), 0)
    step_table = bell_draw(splits[3], (STEPS, D), 0.5, 4.0)
    first_gain = jnp.clip(1.0 + 0.1 * jax.random.normal(splits[4], (D,), jnp.float32), 0.5, 1.5)
    first_shift = bell_draw(splits[5], (D,), 0.3, 2.0, (), jnp.float32)
    w_query = bell_draw(splits[6], (D, D), (D // 2) ** -0.5, 0.3125, ((1, 4),))
    b_query = bell_draw(splits[7], (D,), 0.3, 2.0, ((0, 4),), jnp.float32)
    w_key = bell_draw(splits[8], (D, D), (D // 2) ** -0.5, 0.3125, ((1, 4),))
    w_value = bell_draw(splits[9], (D, D), D ** -0.5, 0.21875, ((1, 4),))
    b_value = bell_draw(splits[10], (D,), 0.3, 2.0, ((0, 4),), jnp.float32)
    w_out = bell_draw(splits[11], (D, D), (D // 16) ** -0.5, 0.875, ((0, 4),))
    b_out = bell_draw(splits[12], (D,), 0.3, 2.0, (), jnp.float32)
    second_gain = jnp.clip(1.0 + 0.1 * jax.random.normal(splits[13], (D,), jnp.float32), 0.5, 1.5)
    second_shift = bell_draw(splits[14], (D,), 0.3, 2.0, (), jnp.float32)
    w_in = bell_draw(splits[15], (D, FF), D ** -0.5, 0.21875, ((1, 4),))
    b_in = bell_draw(splits[16], (FF,), 0.3, 2.0, ((0, 4),), jnp.float32)
    w_down = bell_draw(splits[17], (FF, D), FF ** -0.5, 0.109375, ((0, 4),))
    b_down = bell_draw(splits[18], (D,), 0.3, 2.0, (), jnp.float32)
    cotangent = bell_draw(splits[19], (SEQS, LEN, D), 1.0, 6.0, ((0, 8),))
    return dict(tokens=tokens, timesteps=timesteps, piece_starts=piece_starts, step_table=step_table, first_gain=first_gain, first_shift=first_shift, w_query=w_query, b_query=b_query, w_key=w_key, w_value=w_value, b_value=b_value, w_out=w_out, b_out=b_out, second_gain=second_gain, second_shift=second_shift, w_in=w_in, b_in=b_in, w_down=w_down, b_down=b_down, cotangent=cotangent)


@jax.custom_vjp
def low(v):
    return lax.optimization_barrier(v.astype(jnp.bfloat16)).astype(jnp.float32)

@jax.custom_vjp
def low_back(v):
    return v

def low_keep(v):
    return (low(v), None)

def low_pass(kept, grad):
    return (grad,)

def back_keep(v):
    return (v, None)

def back_low(kept, grad):
    return (low(grad),)
low.defvjp(low_keep, low_pass)
low_back.defvjp(back_keep, back_low)
HIGHEST = lax.Precision.HIGHEST

def matmul_high(left, right):
    return jnp.dot(left, right, precision=HIGHEST)

def normalize(values, gain, shift):
    center = values - lax.optimization_barrier(jnp.mean(values, axis=-1, keepdims=True))
    spread = lax.optimization_barrier(jnp.mean(center * center, axis=-1, keepdims=True))
    return center * lax.rsqrt(spread + 1e-05) * gain + shift

def piece_labels(starts):
    positions = jnp.arange(LEN, dtype=jnp.int32)
    inside = (positions[None, :] >= starts[:, None]) & (positions[None, :] < starts[:, None] + PIECE)
    numbers = jnp.arange(1, PIECES + 1, dtype=jnp.int32)
    return lax.optimization_barrier(jnp.sum(jnp.where(inside, numbers[:, None], 0), axis=0)).astype(jnp.int32)

def layer(stream_in, step_row, params, allowed):
    first_gain, first_shift, w_query, b_query, w_key, w_value, b_value, w_out, b_out, second_gain, second_shift, w_in, b_in, w_down, b_down = params
    stream = stream_in + step_row[None, :]
    normed_one = low(normalize(stream, first_gain, first_shift))
    span_cols = D // N_TENSOR
    heads_here = H // N_TENSOR
    span_units = FF // N_TENSOR
    scale = HD ** (-0.5)
    attn = b_out[None, :]
    for member in range(N_TENSOR):
        first_col = member * span_cols
        last_col = first_col + span_cols
        source = low_back(normed_one)
        queries = low(low_back((matmul_high(source, w_query[:, first_col:last_col]) + b_query[first_col:last_col]) * scale))
        keys_all = low(low_back(matmul_high(source, w_key[:, first_col:last_col])))
        values_all = low(low_back(matmul_high(source, w_value[:, first_col:last_col]) + b_value[first_col:last_col]))
        scores = low_back(jnp.einsum('qhd,khd->hqk', queries.reshape(LEN, heads_here, HD), keys_all.reshape(LEN, heads_here, HD), precision=HIGHEST))
        probs = jax.nn.softmax(jnp.where(allowed[None], scores, -1e+30), axis=-1)
        mixed = jnp.einsum('hqk,khd->qhd', low(probs), values_all.reshape(LEN, heads_here, HD), precision=HIGHEST).reshape(LEN, span_cols)
        mixed = low(low_back(mixed))
        attn = attn + low(low_back(matmul_high(mixed, w_out[first_col:last_col, :])))
    hidden_one = stream + attn
    normed_two = low(normalize(hidden_one, second_gain, second_shift))
    mlp = b_down[None, :]
    for member in range(N_TENSOR):
        first_unit = member * span_units
        last_unit = first_unit + span_units
        source = low_back(normed_two)
        pre_act = low_back(matmul_high(source, w_in[:, first_unit:last_unit]) + b_in[first_unit:last_unit])
        active = low(jax.nn.gelu(pre_act, approximate=True))
        mlp = mlp + low(low_back(matmul_high(active, w_down[first_unit:last_unit, :])))
    return hidden_one + mlp

def reference(tokens, timesteps, piece_starts, step_table, first_gain, first_shift, w_query, b_query, w_key, w_value, b_value, w_out, b_out, second_gain, second_shift, w_in, b_in, w_down, b_down, cotangent):
    params = tuple((item.astype(jnp.float32) for item in (first_gain, first_shift, w_query, b_query, w_key, w_value, b_value, w_out, b_out, second_gain, second_shift, w_in, b_in, w_down, b_down)))
    table_f = step_table.astype(jnp.float32)
    positions = jnp.arange(LEN, dtype=jnp.int32)

    def one_sequence(carry, items):
        seq_tokens, step, starts, seq_cot = items
        labels = piece_labels(starts)
        allowed = (positions[None, :] <= positions[:, None]) | (labels[:, None] == labels[None, :]) & (labels[:, None] > 0)
        onehot = (jnp.arange(STEPS, dtype=jnp.int32) == step).astype(jnp.float32)

        def forward(tokens_f, table_in, params_in):
            return layer(tokens_f, matmul_high(onehot, table_in), params_in, allowed)
        result, pull = jax.vjp(forward, seq_tokens.astype(jnp.float32), table_f, params)
        grad_in, grad_table, grad_params = pull(seq_cot.astype(jnp.float32))
        table_acc, param_acc = carry
        new_params = tuple((a + b for a, b in zip(param_acc, grad_params)))
        return ((table_acc + grad_table, new_params), (result.astype(jnp.bfloat16), grad_in.astype(jnp.bfloat16)))
    start = (jnp.zeros((STEPS, D), jnp.float32), tuple((jnp.zeros_like(item) for item in params)))
    (grad_table, grads), (output, grad_tokens) = lax.scan(one_sequence, start, (tokens, timesteps, piece_starts, cotangent))
    g_first_gain, g_first_shift, g_w_query, g_b_query, g_w_key, g_w_value, g_b_value, g_w_out, g_b_out, g_second_gain, g_second_shift, g_w_in, g_b_in, g_w_down, g_b_down = grads
    return (output, grad_tokens, grad_table, g_first_gain, g_first_shift, g_w_query, g_b_query, g_w_key, g_w_value, g_b_value, g_w_out, g_b_out, g_second_gain, g_second_shift, g_w_in, g_b_in, g_w_down, g_b_down)
```

```python
import functools

import jax
import jax.numpy as jnp
from jax import lax
from jax.experimental import pallas as pl
from jax.experimental.pallas import tpu as pltpu
from jax.sharding import PartitionSpec as P

HD = 64
PIECE = 256
WIN = 2 * PIECE
EPS = 1e-05
QB = 256
BT = 256
F32 = jnp.float32
BF16 = jnp.bfloat16
SDS = jax.ShapeDtypeStruct
SCALE = HD ** (-0.5)
GELU_C = 0.7978845608028654


def nn(a, b):
    return lax.dot_general(a, b, (((1,), (0,)), ((), ())), preferred_element_type=F32)


def nt(a, b):
    return lax.dot_general(a, b, (((1,), (1,)), ((), ())), preferred_element_type=F32)


def tn(a, b):
    return lax.dot_general(a, b, (((0,), (0,)), ((), ())), preferred_element_type=F32)


def norm_parts(v):
    c = v - jnp.mean(v, axis=-1, keepdims=True)
    root = lax.rsqrt(jnp.mean(c * c, axis=-1, keepdims=True) + EPS)
    return c * root, root


def norm_back(e, hat, root):
    return root * (
        e - jnp.mean(e, axis=-1, keepdims=True) - hat * jnp.mean(e * hat, axis=-1, keepdims=True)
    )


def col_sum(v):
    return jnp.sum(v, axis=0, keepdims=True)


def whole(shape):
    return pl.BlockSpec(shape, lambda i, *_: (0,) * len(shape))


def rows_at(width, offset=0, block=BT):
    return pl.BlockSpec((block, width), lambda i, *_: (offset + i, 0))


def cost(flops, nbytes, trans=0):
    return pl.CostEstimate(flops=int(flops), bytes_accessed=int(nbytes), transcendentals=int(trans))


def kept_first(width, nb, offset=0):
    return pl.BlockSpec((BT, width), lambda i, core: (offset + lax.rem(i + core[0] * (nb // 2), nb), 0))


def first_half(width, nb):
    return pl.BlockSpec((BT, width), lambda i, core: (jnp.minimum(i, nb // 2 - 1), 0))


def second_half(width, nb):
    return pl.BlockSpec((BT, width), lambda i, core: (jnp.maximum(i - nb // 2, 0), 0))


def qkv_kernel(tok, row, gain, shift, wq, wk, wv, bq, bv, n1, q, k, v):
    hat, _ = norm_parts(tok[...].astype(F32) + row[...])
    n = (hat * gain[...] + shift[...]).astype(BF16)
    n1[...] = n
    q[...] = ((nn(n, wq[...]) + bq[...]) * SCALE).astype(BF16)
    k[...] = nn(n, wk[...]).astype(BF16)
    v[...] = (nn(n, wv[...]) + bv[...]).astype(BF16)


def qkv_call(tok, row, gain, shift, wq, wk, wv, bq, bv):
    length, d = tok.shape
    c = wq.shape[1]
    return pl.pallas_call(
        qkv_kernel,
        grid=(length // BT,),
        in_specs=[rows_at(d)] + [whole((1, d))] * 3 + [whole((d, c))] * 3 + [whole((1, c))] * 2,
        out_specs=[rows_at(d)] + [rows_at(c)] * 3,
        out_shape=[SDS((length, d), BF16)] + [SDS((length, c), BF16)] * 3,
        cost_estimate=cost(6 * length * d * c, length * (4 * d + 6 * c) + 6 * d * c),
        name="norm_qkv",
    )(tok, row, gain, shift, wq, wk, wv, bq, bv)


def attn_fwd_window(win, sub, nh, starts, q, k, v, mix, lse):
    base = win * WIN
    start = starts[win]
    qpos = base + sub * QB + lax.broadcasted_iota(jnp.int32, (QB, 1), 0)
    limit = jnp.where((qpos >= start) & (qpos < start + PIECE), start + PIECE - 1, qpos)
    kpos = base + lax.broadcasted_iota(jnp.int32, (1, WIN), 1)
    allow = kpos <= limit
    for h in range(nh):
        cols = slice(h * HD, (h + 1) * HD)
        qh = q[:, cols]
        near = jnp.where(allow, nt(qh, k[base : base + WIN, cols]), -1e30)
        top = jnp.max(near, axis=-1, keepdims=True)
        if win:
            far = nt(qh, k[:base, cols])
            top = jnp.maximum(top, jnp.max(far, axis=-1, keepdims=True))
        pn = jnp.exp(near - top)
        total = jnp.sum(pn, axis=-1, keepdims=True)
        out = nn(pn.astype(BF16), v[base : base + WIN, cols])
        if win:
            pf = jnp.exp(far - top)
            total = total + jnp.sum(pf, axis=-1, keepdims=True)
            out = out + nn(pf.astype(BF16), v[:base, cols])
        mix[:, cols] = (out / total).astype(BF16)
        stat = jnp.broadcast_to(top + jnp.log(total), (QB, 128))
        lse[h : h + 1, :] = jnp.transpose(stat)[0:1, :]


def attn_fwd_kernel(wins, nh, starts, *refs):
    step = pl.program_id(0)
    per = WIN // QB
    for n, win in enumerate(wins):

        @pl.when(step // per == n)
        def _(win=win):
            attn_fwd_window(win, lax.rem(step, per), nh, starts, *refs)


def window_map(wins):
    per = WIN // QB
    return lambda i: (wins[0] - i // per) * per + lax.rem(i, per)


def attn_fwd_call(starts, q, k, v, wins):
    length, c = q.shape
    nh = c // HD
    per = WIN // QB
    kv = (wins[0] + 1) * WIN
    low = wins[-1] * per
    at = window_map(wins)
    return pl.pallas_call(
        functools.partial(attn_fwd_kernel, wins, nh),
        grid=(len(wins) * per,),
        in_specs=[
            pl.BlockSpec(memory_space=pltpu.SMEM),
            pl.BlockSpec((QB, c), lambda i: (at(i), 0)),
            whole((kv, c)),
            whole((kv, c)),
        ],
        out_specs=[
            pl.BlockSpec((QB, c), lambda i: (at(i) - low, 0)),
            pl.BlockSpec((8, QB), lambda i: (0, at(i) - low)),
        ],
        out_shape=[SDS((len(wins) * WIN, c), BF16), SDS((8, len(wins) * WIN), F32)],
        cost_estimate=cost(
            sum(4 * WIN * (w + 1) * WIN * c * 4 for w in wins),
            4 * kv * c + 4 * len(wins) * WIN * c,
            sum(WIN * (w + 1) * WIN * nh for w in wins),
        ),
        name="attn_fwd",
    )(starts, q, k, v)


def ffn_kernel(
    nb, core, m0, m1, m2, m3, tok, row, cot, wo0, wo1, wo2, wo3, b_out, gain, shift, w_in, b_in, w_down,
    hid, n2, act, gpre, mlp_keep, mlp_send, two_keep, two_send,
):
    i = pl.program_id(0)
    attn = nn(m0[...], wo0[...]) + nn(m1[...], wo1[...]) + nn(m2[...], wo2[...]) + nn(m3[...], wo3[...])
    h = tok[...].astype(F32) + row[...] + attn + b_out[...]
    hid[...] = h
    hat, _ = norm_parts(h)
    n = (hat * gain[...] + shift[...]).astype(BF16)
    n2[...] = n
    z = nn(n, w_in[...]) + b_in[...]
    z2 = z * z
    th = jnp.tanh(z * (GELU_C + (GELU_C * 0.044715) * z2))
    half = 0.5 * (1.0 + th)
    a = (z * half).astype(BF16)
    act[...] = a
    slope = half + (0.5 * z) * (1.0 - th * th) * (GELU_C + (3.0 * 0.044715 * GELU_C) * z2)
    gp = (nt(cot[...], w_down[...]) * slope).astype(BF16)
    gpre[...] = gp
    mlp = nn(a, w_down[...]).astype(BF16)
    two = nt(gp, w_in[...]).astype(BF16)

    @pl.when(i < nb // 2)
    def _():
        mlp_keep[...] = mlp
        two_keep[...] = two

    @pl.when(i >= nb // 2)
    def _():
        mlp_send[...] = mlp
        two_send[...] = two


def ffn_call(core, ms, tok, row, cot, wos, b_out, gain, shift, w_in, b_in, w_down, row0):
    n, c = ms[0].shape
    d = tok.shape[1]
    u = w_in.shape[1]
    nb = n // BT
    off = row0 // BT
    kf = functools.partial(kept_first, nb=nb)
    return pl.pallas_call(
        functools.partial(ffn_kernel, nb),
        grid_spec=pltpu.PrefetchScalarGridSpec(
            num_scalar_prefetch=1,
            grid=(nb,),
            in_specs=[kf(c)] * 4
            + [kf(d, offset=off), whole((1, d)), kf(d, offset=off)]
            + [whole((c, d))] * 4
            + [whole((1, d))] * 3
            + [whole((d, u)), whole((1, u)), whole((u, d))],
            out_specs=[kf(d), kf(d), kf(u), kf(u)] + [first_half(d, nb), second_half(d, nb)] * 2,
        ),
        out_shape=[SDS((n, d), F32), SDS((n, d), BF16), SDS((n, u), BF16), SDS((n, u), BF16)]
        + [SDS((n // 2, d), BF16)] * 4,
        cost_estimate=cost(2 * n * d * (4 * c + 4 * u), n * (8 * c + 18 * d) + 8 * d * c + 4 * d * u, n * u),
        name="ffn",
    )(core, *ms, tok, row, cot, *wos, b_out, gain, shift, w_in, b_in, w_down)


def ffn_grad_kernel(na, n2a, n2b, gpa, gpb, aca, acb, cot, g_in, g_down, sums, acc_in, acc_down):
    i = pl.program_id(0)

    @pl.when(i == 0)
    def _():
        acc_in[...] = jnp.zeros_like(acc_in)
        acc_down[...] = jnp.zeros_like(acc_down)
        sums[...] = jnp.zeros_like(sums)

    def step(n2, gp, ac):
        acc_in[...] += tn(n2[...], gp[...])
        acc_down[...] += tn(ac[...], cot[...])
        sums[0:1, :] += col_sum(gp[...].astype(F32))
        sums[1:2, :] += col_sum(cot[...].astype(F32))

    @pl.when(i < na)
    def _():
        step(n2a, gpa, aca)

    @pl.when(i >= na)
    def _():
        step(n2b, gpb, acb)

    @pl.when(i == pl.num_programs(0) - 1)
    def _():
        g_in[...] = acc_in[...].astype(BF16)
        g_down[...] = acc_down[...].astype(BF16)


def ffn_grad_call(n2a, n2b, gpa, gpb, aca, acb, cot, block=512):
    length, d = cot.shape
    u = gpa.shape[1]
    na, nb = n2a.shape[0] // block, n2b.shape[0] // block
    fa = lambda w: pl.BlockSpec((block, w), lambda i: (jnp.minimum(i, na - 1), 0))
    fb = lambda w: pl.BlockSpec((block, w), lambda i: (jnp.maximum(i - na, 0), 0))
    return pl.pallas_call(
        functools.partial(ffn_grad_kernel, na),
        grid=(na + nb,),
        in_specs=[
            fa(d), fb(d), fa(u), fb(u), fa(u), fb(u),
            pl.BlockSpec((block, d), lambda i: (lax.rem(i + nb, na + nb), 0)),
        ],
        out_specs=[whole((d, u)), whole((u, d)), whole((8, d))],
        out_shape=[SDS((d, u), BF16), SDS((u, d), BF16), SDS((8, d), F32)],
        scratch_shapes=[pltpu.VMEM((d, u), F32), pltpu.VMEM((u, d), F32)],
        cost_estimate=cost(4 * length * d * u, length * (4 * d + 4 * u) + 4 * d * u),
        name="ffn_grad",
    )(n2a, n2b, gpa, gpb, aca, acb, cot)


def halves(nb, refs):
    i = pl.program_id(0)
    ks, kx, os_, ox = refs
    return jnp.where(
        i < nb // 2,
        ks[...].astype(F32) + kx[...].astype(F32),
        os_[...].astype(F32) + ox[...].astype(F32),
    )


def norm_two_kernel(nb, core, ks, kx, os_, ox, hid, cot, gain, w_out, gh, gm, sums):
    @pl.when(pl.program_id(0) == 0)
    def _():
        sums[...] = jnp.zeros_like(sums)

    two = halves(nb, (ks, kx, os_, ox))
    hat, root = norm_parts(hid[...])
    g = cot[...].astype(F32) + norm_back(two * gain[...], hat, root)
    gh[...] = g
    gm[...] = nt(g.astype(BF16), w_out[...]).astype(BF16)
    sums[0:1, :] += col_sum(two * hat)
    sums[1:2, :] += col_sum(two)
    sums[2:3, :] += col_sum(g)


def norm_two_call(core, parts, hid, cot, gain, w_out, row0):
    n, d = hid.shape
    c = w_out.shape[0]
    nb = n // BT
    kf = functools.partial(kept_first, nb=nb)
    return pl.pallas_call(
        functools.partial(norm_two_kernel, nb),
        grid_spec=pltpu.PrefetchScalarGridSpec(
            num_scalar_prefetch=1,
            grid=(nb,),
            in_specs=[first_half(d, nb)] * 2
            + [second_half(d, nb)] * 2
            + [kf(d), kf(d, offset=row0 // BT), whole((1, d)), whole((c, d))],
            out_specs=[kf(d), kf(c), whole((8, d))],
        ),
        out_shape=[SDS((n, d), F32), SDS((n, c), BF16), SDS((8, d), F32)],
        cost_estimate=cost(2 * n * d * c, n * (14 * d + 2 * c)),
        name="norm_two_back",
    )(core, *parts, hid, cot, gain, w_out)


def attn_bwd_window(win, sub, nh, starts, q, k, v, g, lse, dq, ak, av):
    base = win * WIN
    start = starts[win]
    qpos = base + sub * QB + lax.broadcasted_iota(jnp.int32, (1, QB), 1)
    limit = jnp.where((qpos >= start) & (qpos < start + PIECE), start + PIECE - 1, qpos)
    kpos = base + lax.broadcasted_iota(jnp.int32, (WIN, 1), 0)
    allow = kpos <= limit
    near = slice(base, base + WIN)
    for h in range(nh):
        cols = slice(h * HD, (h + 1) * HD)
        qh = q[:, cols]
        gh = g[:, cols]
        ls = lse[h : h + 1, :]
        pn = jnp.exp(jnp.where(allow, nt(k[near, cols], qh), -1e30) - ls)
        dpn = nt(v[near, cols], gh)
        centre = col_sum(pn * dpn)
        if win:
            pf = jnp.exp(nt(k[:base, cols], qh) - ls)
            dpf = nt(v[:base, cols], gh)
            centre = centre + col_sum(pf * dpf)
        dsn = (pn * (dpn - centre)).astype(BF16)
        dqh = tn(dsn, k[near, cols])
        ak[near, cols] += nn(dsn, qh)
        av[near, cols] += nn(pn.astype(BF16), gh)
        if win:
            dsf = (pf * (dpf - centre)).astype(BF16)
            dqh = dqh + tn(dsf, k[:base, cols])
            ak[:base, cols] += nn(dsf, qh)
            av[:base, cols] += nn(pf.astype(BF16), gh)
        dq[:, cols] = (dqh.astype(BF16).astype(F32) * SCALE).astype(BF16)


def attn_bwd_kernel(wins, nh, carried, starts, q, k, v, g, lse, *rest):
    step = pl.program_id(0)
    per = WIN // QB
    if carried:
        dk0, dv0, dq, dk, dv, ak, av = rest
    else:
        dq, dk, dv, dkf, dvf, ak, av = rest

    @pl.when(step == 0)
    def _():
        if carried:
            ak[...] = dk0[...]
            av[...] = dv0[...]
        else:
            ak[...] = jnp.zeros_like(ak)
            av[...] = jnp.zeros_like(av)

    for n, win in enumerate(wins):

        @pl.when(step // per == n)
        def _(win=win):
            attn_bwd_window(win, lax.rem(step, per), nh, starts, q, k, v, g, lse, dq, ak, av)

    @pl.when(step == pl.num_programs(0) - 1)
    def _():
        low = wins[-1] * WIN
        dk[...] = ak[low:, :].astype(BF16)
        dv[...] = av[low:, :].astype(BF16)
        if not carried:
            dkf[...] = ak[:low, :]
            dvf[...] = av[:low, :]


def attn_bwd_call(starts, q, k, v, g, lse, carry, wins):
    c = q.shape[1]
    nh = c // HD
    per = WIN // QB
    kv = (wins[0] + 1) * WIN
    n = len(wins) * WIN
    low = wins[-1] * per
    at = window_map(wins)
    carried = carry is not None
    near = lambda w: pl.BlockSpec((QB, w), lambda i: (at(i) - low, 0))
    rest = kv - n
    return pl.pallas_call(
        functools.partial(attn_bwd_kernel, wins, nh, carried),
        grid=(len(wins) * per,),
        in_specs=[
            pl.BlockSpec(memory_space=pltpu.SMEM),
            pl.BlockSpec((QB, c), lambda i: (at(i), 0)),
            whole((kv, c)),
            whole((kv, c)),
            near(c),
            pl.BlockSpec((8, QB), lambda i: (0, at(i) - low)),
        ]
        + ([whole((kv, c))] * 2 if carried else []),
        out_specs=[near(c), whole((n, c)), whole((n, c))] + ([] if carried else [whole((rest, c))] * 2),
        out_shape=[SDS((n, c), BF16)] * 3 + ([] if carried else [SDS((rest, c), F32)] * 2),
        scratch_shapes=[pltpu.VMEM((kv, c), F32)] * 2,
        cost_estimate=cost(
            sum(10 * WIN * (w + 1) * WIN * c * 4 for w in wins),
            12 * kv * c + 8 * n * c,
            sum(WIN * (w + 1) * WIN * nh for w in wins),
        ),
        name="attn_bwd",
    )(starts, q, k, v, g, lse, *(carry if carried else ()))


def one_kernel(nb, core, dq, dk, dv, wq, wk, wv, keep, send, sums):
    i = pl.program_id(0)

    @pl.when(i == 0)
    def _():
        sums[...] = jnp.zeros_like(sums)

    part = (nt(dq[...], wq[...]) + nt(dk[...], wk[...]) + nt(dv[...], wv[...])).astype(BF16)
    sums[0:1, :] += col_sum(dq[...].astype(F32))
    sums[1:2, :] += col_sum(dv[...].astype(F32))

    @pl.when(i < nb // 2)
    def _():
        keep[...] = part

    @pl.when(i >= nb // 2)
    def _():
        send[...] = part


def one_call(core, dq, dk, dv, wq, wk, wv):
    n, c = dq.shape
    d = wq.shape[0]
    nb = n // BT
    kf = functools.partial(kept_first, nb=nb)
    return pl.pallas_call(
        functools.partial(one_kernel, nb),
        grid_spec=pltpu.PrefetchScalarGridSpec(
            num_scalar_prefetch=1,
            grid=(nb,),
            in_specs=[kf(c)] * 3 + [whole((d, c))] * 3,
            out_specs=[first_half(d, nb), second_half(d, nb), whole((8, c))],
        ),
        out_shape=[SDS((n // 2, d), BF16)] * 2 + [SDS((8, c), F32)],
        cost_estimate=cost(6 * n * d * c, n * (6 * c + 2 * d) + 6 * d * c),
        name="grad_one",
    )(core, dq, dk, dv, wq, wk, wv)


def attn_grad_kernel(na, n1, dqa, dqb, dka, dkb, dva, dvb, mxa, mxb, gha, ghb, gq, gk, gv, go, aq, ak, av, ao):
    i = pl.program_id(0)

    @pl.when(i == 0)
    def _():
        for acc in (aq, ak, av, ao):
            acc[...] = jnp.zeros_like(acc)

    def step(dq, dk, dv, mx, gh):
        n = n1[...]
        aq[...] += tn(n, dq[...])
        ak[...] += tn(n, dk[...])
        av[...] += tn(n, dv[...])
        ao[...] += tn(mx[...], gh[...].astype(BF16))

    @pl.when(i < na)
    def _():
        step(dqa, dka, dva, mxa, gha)

    @pl.when(i >= na)
    def _():
        step(dqb, dkb, dvb, mxb, ghb)

    @pl.when(i == pl.num_programs(0) - 1)
    def _():
        gq[...] = aq[...].astype(BF16)
        gk[...] = ak[...].astype(BF16)
        gv[...] = av[...].astype(BF16)
        go[...] = ao[...].astype(BF16)


def attn_grad_call(n1, dqs, dks, dvs, mxs, ghs, block=512):
    length, d = n1.shape
    c = dqs[0].shape[1]
    na, nb = dqs[0].shape[0] // block, dqs[1].shape[0] // block
    fa = lambda w: pl.BlockSpec((block, w), lambda i: (jnp.minimum(i, na - 1), 0))
    fb = lambda w: pl.BlockSpec((block, w), lambda i: (jnp.maximum(i - na, 0), 0))
    return pl.pallas_call(
        functools.partial(attn_grad_kernel, na),
        grid=(na + nb,),
        in_specs=[pl.BlockSpec((block, d), lambda i: (lax.rem(i + nb, na + nb), 0))]
        + [fa(c), fb(c)] * 4
        + [fa(d), fb(d)],
        out_specs=[whole((d, c))] * 3 + [whole((c, d))],
        out_shape=[SDS((d, c), BF16)] * 3 + [SDS((c, d), BF16)],
        scratch_shapes=[pltpu.VMEM((d, c), F32)] * 3 + [pltpu.VMEM((c, d), F32)],
        cost_estimate=cost(8 * length * d * c, length * (6 * d + 8 * c) + 8 * d * c),
        name="attn_grad",
    )(n1, *dqs, *dks, *dvs, *mxs, *ghs)


def norm_one_kernel(nb, core, ks, kx, os_, ox, tok, row, gh, gain, out, sums):
    @pl.when(pl.program_id(0) == 0)
    def _():
        sums[...] = jnp.zeros_like(sums)

    one = halves(nb, (ks, kx, os_, ox))
    hat, root = norm_parts(tok[...].astype(F32) + row[...])
    g = gh[...] + norm_back(one * gain[...], hat, root)
    out[...] = g.astype(BF16)
    sums[0:1, :] += col_sum(one * hat)
    sums[1:2, :] += col_sum(one)
    sums[2:3, :] += col_sum(g)


def norm_one_call(core, parts, tok, row, gh, gain, row0):
    n, d = gh.shape
    nb = n // BT
    kf = functools.partial(kept_first, nb=nb)
    return pl.pallas_call(
        functools.partial(norm_one_kernel, nb),
        grid_spec=pltpu.PrefetchScalarGridSpec(
            num_scalar_prefetch=1,
            grid=(nb,),
            in_specs=[first_half(d, nb)] * 2
            + [second_half(d, nb)] * 2
            + [kf(d, offset=row0 // BT), whole((1, d)), kf(d), whole((1, d))],
            out_specs=[kf(d), whole((8, d))],
        ),
        out_shape=[SDS((n, d), BF16), SDS((8, d), F32)],
        cost_estimate=cost(20 * n * d, n * 12 * d),
        name="norm_one_back",
    )(core, *parts, tok, row, gh, gain)


def out_kernel(nb, core, ks, kx, os_, ox, hid, b_down, out):
    out[...] = (hid[...] + halves(nb, (ks, kx, os_, ox)) + b_down[...]).astype(BF16)


def out_call(core, parts, hid, b_down):
    n, d = hid.shape
    nb = n // BT
    kf = functools.partial(kept_first, nb=nb)
    return pl.pallas_call(
        functools.partial(out_kernel, nb),
        grid_spec=pltpu.PrefetchScalarGridSpec(
            num_scalar_prefetch=1,
            grid=(nb,),
            in_specs=[first_half(d, nb)] * 2 + [second_half(d, nb)] * 2 + [kf(d), whole((1, d))],
            out_specs=kf(d),
        ),
        out_shape=SDS((n, d), BF16),
        cost_estimate=cost(3 * n * d, n * 10 * d),
        name="layer_out",
    )(core, *parts, hid, b_down)


def per_device(
    n_tensor,
    n_dp,
    tokens,
    timesteps,
    piece_starts,
    step_table,
    first_gain,
    first_shift,
    w_query,
    b_query,
    w_key,
    w_value,
    b_value,
    w_out,
    b_out,
    second_gain,
    second_shift,
    w_in,
    b_in,
    w_down,
    b_down,
    cotangent,
):
    tok = tokens[0]
    cot = cotangent[0]
    length, d = tok.shape
    c = w_query.shape[1]
    table_rows = step_table.shape[0]
    starts = piece_starts[0]
    rank = lax.axis_index("tensor")
    core = (rank % 2).astype(jnp.int32)[None]
    over_x = [(i, i ^ 2) for i in range(n_tensor)]
    over_core = [(i, i ^ 1) for i in range(n_tensor)]
    swap_x = lambda v: lax.ppermute(v, "tensor", over_x)
    swap_core = lambda v: lax.ppermute(v, "tensor", over_core)
    line = lambda v: v[None, :]

    row = lax.dynamic_slice(step_table, (timesteps[0], 0), (1, d)).astype(F32)
    wo0, wo2 = w_out, swap_x(w_out)
    wo1, wo3 = swap_core(wo0), swap_core(wo2)

    n1, q, k, v = qkv_call(
        tok, row, line(first_gain), line(first_shift), w_query, w_key, w_value, line(b_query), line(b_value)
    )
    top = length // WIN - 1
    groups = [[top], list(range(top - 1, -1, -1))]
    row0s = [top * WIN, 0]

    def gathered(m):
        m2 = swap_x(m)
        return [m, swap_core(m), m2, swap_core(m2)]

    def summed(keep, send):
        s = (keep.astype(F32) + swap_core(send).astype(F32)).astype(BF16)
        x = swap_x(s)
        return [s, x, swap_core(s), swap_core(x)]

    fwd = [attn_fwd_call(starts, q, k, v, wins) for wins in groups]
    ffn = [
        ffn_call(
            core, gathered(fwd[n][0]), tok, row, cot, [wo0, wo1, wo2, wo3], line(b_out), line(second_gain),
            line(second_shift), w_in, line(b_in), w_down, row0s[n],
        )
        for n in range(2)
    ]
    hid = [f[0] for f in ffn]
    g_in, g_down, ffn_sums = ffn_grad_call(
        ffn[0][1], ffn[1][1], ffn[0][3], ffn[1][3], ffn[0][2], ffn[1][2], cot
    )
    two = [summed(f[6], f[7]) for f in ffn]
    mlp = [summed(f[4], f[5]) for f in ffn]
    g_in, g_down = lax.psum((g_in, g_down), "dp")

    nt_out = [norm_two_call(core, two[n], hid[n], cot, line(second_gain), w_out, row0s[n]) for n in range(2)]
    dq0, dk0, dv0, dkf, dvf = attn_bwd_call(starts, q, k, v, nt_out[0][1], fwd[0][1], None, groups[0])
    dq1, dk1, dv1 = attn_bwd_call(starts, q, k, v, nt_out[1][1], fwd[1][1], (dkf, dvf), groups[1])
    one0 = one_call(core, dq0, dk0, dv0, w_query, w_key, w_value)
    one1 = one_call(core, dq1, dk1, dv1, w_query, w_key, w_value)
    ones = [summed(o[0], o[1]) for o in (one0, one1)]
    g_q, g_k, g_v, g_o = attn_grad_call(
        n1, (dq0, dq1), (dk0, dk1), (dv0, dv1), (fwd[0][0], fwd[1][0]), (nt_out[0][0], nt_out[1][0])
    )
    g_q, g_k, g_v, g_o = lax.psum((g_q, g_k, g_v, g_o), "dp")
    n_out = [norm_one_call(core, ones[n], tok, row, nt_out[n][0], line(first_gain), row0s[n]) for n in range(2)]
    outs = [out_call(core, mlp[n], hid[n], line(b_down)) for n in range(2)]

    me = lax.axis_index("dp")
    spot = (jnp.arange(n_dp) == me).astype(F32)
    s2 = nt_out[0][2] + nt_out[1][2]
    s1 = n_out[0][1] + n_out[1][1]
    so = one0[2] + one1[2]
    pad = (-(2 * c + n_dp)) % d
    mixed_row = jnp.concatenate([so[0], so[1], spot * timesteps[0].astype(F32), jnp.zeros((pad,), F32)])
    small = jnp.concatenate(
        [ffn_sums[0:2], s2[0:3], s1[0:2], mixed_row.reshape(-1, d), spot[:, None] * s1[2:3]], axis=0
    )
    bit = 1
    while bit < n_dp:
        small = small + lax.ppermute(small, "dp", [(i, i ^ bit) for i in range(n_dp)])
        bit *= 2
    extra = mixed_row.shape[0] // d
    mixed_row = small[7 : 7 + extra].reshape(-1)
    row_totals = small[7 + extra :]
    steps = mixed_row[2 * c : 2 * c + n_dp].astype(jnp.int32)
    hot = (jnp.arange(table_rows, dtype=jnp.int32)[:, None] == steps[None, :]).astype(F32)
    g_table = jnp.dot(hot, row_totals, precision=lax.Precision.HIGHEST)

    output = jnp.concatenate([outs[1], outs[0]], axis=0)[None]
    grad_tokens = jnp.concatenate([n_out[1][0], n_out[0][0]], axis=0)[None]
    return (
        output,
        grad_tokens,
        g_table,
        small[5],
        small[6],
        g_q.astype(F32),
        mixed_row[:c],
        g_k.astype(F32),
        g_v.astype(F32),
        mixed_row[c : 2 * c],
        g_o.astype(F32),
        small[4],
        small[2],
        small[3],
        g_in.astype(F32),
        small[0],
        g_down.astype(F32),
        small[1],
    )


def solution(mesh):
    in_specs = (
        P("dp", None, None),
        P("dp"),
        P("dp", None),
        P(),
        P(),
        P(),
        P(None, "tensor"),
        P("tensor"),
        P(None, "tensor"),
        P(None, "tensor"),
        P("tensor"),
        P("tensor", None),
        P(),
        P(),
        P(),
        P(None, "tensor"),
        P("tensor"),
        P("tensor", None),
        P(),
        P("dp", None, None),
    )
    out_specs = (
        P("dp", None, None),
        P("dp", None, None),
        P(),
        P(),
        P(),
        P(None, "tensor"),
        P("tensor"),
        P(None, "tensor"),
        P(None, "tensor"),
        P("tensor"),
        P("tensor", None),
        P(),
        P(),
        P(),
        P(None, "tensor"),
        P("tensor"),
        P("tensor", None),
        P(),
    )
    return jax.shard_map(
        functools.partial(per_device, mesh.shape["tensor"], mesh.shape["dp"]),
        mesh=mesh,
        in_specs=in_specs,
        out_specs=out_specs,
        check_vma=False,
    )
```

```python
import functools

import jax
import jax.numpy as jnp
from jax import lax
from jax.experimental import pallas as pl
from jax.experimental.pallas import tpu as pltpu
from jax.sharding import PartitionSpec as P

HD = 64
PIECE = 256
WIN = 2 * PIECE
EPS = 1e-05
QB = 256
BT = 256
F32 = jnp.float32
BF16 = jnp.bfloat16
SDS = jax.ShapeDtypeStruct
SCALE = HD ** (-0.5)
GELU_C = 0.7978845608028654


def nn(a, b):
    return lax.dot_general(a, b, (((1,), (0,)), ((), ())), preferred_element_type=F32)


def nt(a, b):
    return lax.dot_general(a, b, (((1,), (1,)), ((), ())), preferred_element_type=F32)


def tn(a, b):
    return lax.dot_general(a, b, (((0,), (0,)), ((), ())), preferred_element_type=F32)


def norm_parts(v):
    c = v - jnp.mean(v, axis=-1, keepdims=True)
    root = lax.rsqrt(jnp.mean(c * c, axis=-1, keepdims=True) + EPS)
    return c * root, root


def norm_back(e, hat, root):
    return root * (
        e - jnp.mean(e, axis=-1, keepdims=True) - hat * jnp.mean(e * hat, axis=-1, keepdims=True)
    )


def col_sum(v):
    return jnp.sum(v, axis=0, keepdims=True)


def whole(shape):
    return pl.BlockSpec(shape, lambda i, *_: (0,) * len(shape))


def rows_at(width, offset=0, block=BT):
    return pl.BlockSpec((block, width), lambda i, *_: (offset + i, 0))


def cost(flops, nbytes, trans=0):
    return pl.CostEstimate(flops=int(flops), bytes_accessed=int(nbytes), transcendentals=int(trans))


def kept_first(width, nb, offset=0):
    return pl.BlockSpec((BT, width), lambda i, core: (offset + lax.rem(i + core[0] * (nb // 2), nb), 0))


def first_half(width, nb):
    return pl.BlockSpec((BT, width), lambda i, core: (jnp.minimum(i, nb // 2 - 1), 0))


def second_half(width, nb):
    return pl.BlockSpec((BT, width), lambda i, core: (jnp.maximum(i - nb // 2, 0), 0))


def params(mib=12):
    return pltpu.CompilerParams(vmem_limit_bytes=mib * 1024 * 1024)


SMEM = pl.BlockSpec(memory_space=pltpu.SMEM)


def qkv_kernel(steps, tok, table, gain, shift, wq, wk, wv, bq, bv, n1, q, k, v, row):
    rows = table[...].astype(F32)
    at = lax.broadcasted_iota(jnp.int32, rows.shape, 0) == lax.rem(steps[0], 8)
    step_row = col_sum(jnp.where(at, rows, 0.0))
    row[...] = step_row
    hat, _ = norm_parts(tok[...].astype(F32) + step_row)
    n = (hat * gain[...] + shift[...]).astype(BF16)
    n1[...] = n
    q[...] = ((nt(n, wq[...]) + bq[...]) * SCALE).astype(BF16)
    k[...] = nt(n, wk[...]).astype(BF16)
    v[...] = (nt(n, wv[...]) + bv[...]).astype(BF16)


def qkv_call(steps, tok, table, gain, shift, wq, wk, wv, bq, bv):
    length, d = tok.shape
    c = wq.shape[0]
    return pl.pallas_call(
        qkv_kernel,
        grid_spec=pltpu.PrefetchScalarGridSpec(
            num_scalar_prefetch=1,
            grid=(length // BT,),
            in_specs=[rows_at(d), pl.BlockSpec((8, d), lambda i, steps: (steps[0] // 8, 0))]
            + [whole((d,))] * 2
            + [whole((c, d))] * 3
            + [whole((c,))] * 2,
            out_specs=[rows_at(d)] + [rows_at(c)] * 3 + [whole((1, d))],
        ),
        out_shape=[SDS((length, d), BF16)] + [SDS((length, c), BF16)] * 3 + [SDS((1, d), F32)],
        cost_estimate=cost(6 * length * d * c, length * (4 * d + 6 * c) + 6 * d * c),
        compiler_params=params(),
        name="norm_qkv",
    )(steps, tok, table, gain, shift, wq, wk, wv, bq, bv)


def attn_fwd_window(win, sub, nh, starts, q, k, v, mix, lse):
    base = win * WIN
    start = starts[win]
    qpos = base + sub * QB + lax.broadcasted_iota(jnp.int32, (QB, 1), 0)
    limit = jnp.where((qpos >= start) & (qpos < start + PIECE), start + PIECE - 1, qpos)
    kpos = base + lax.broadcasted_iota(jnp.int32, (1, WIN), 1)
    allow = kpos <= limit
    for h in range(nh):
        cols = slice(h * HD, (h + 1) * HD)
        qh = q[:, cols]
        near = jnp.where(allow, nt(qh, k[base : base + WIN, cols]), -1e30)
        top = jnp.max(near, axis=-1, keepdims=True)
        if win:
            far = nt(qh, k[:base, cols])
            top = jnp.maximum(top, jnp.max(far, axis=-1, keepdims=True))
        pn = jnp.exp(near - top)
        total = jnp.sum(pn, axis=-1, keepdims=True)
        out = nn(pn.astype(BF16), v[base : base + WIN, cols])
        if win:
            pf = jnp.exp(far - top)
            total = total + jnp.sum(pf, axis=-1, keepdims=True)
            out = out + nn(pf.astype(BF16), v[:base, cols])
        mix[:, cols] = (out / total).astype(BF16)
        stat = jnp.broadcast_to(top + jnp.log(total), (QB, 128))
        lse[h : h + 1, :] = jnp.transpose(stat)[0:1, :]


def attn_fwd_kernel(wins, nh, starts, *refs):
    step = pl.program_id(0)
    per = WIN // QB
    for n, win in enumerate(wins):

        @pl.when(step // per == n)
        def _(win=win):
            attn_fwd_window(win, lax.rem(step, per), nh, starts, *refs)


def window_map(wins):
    per = WIN // QB
    return lambda i: (wins[0] - i // per) * per + lax.rem(i, per)


def attn_fwd_call(starts, q, k, v, wins):
    length, c = q.shape
    nh = c // HD
    per = WIN // QB
    kv = (wins[0] + 1) * WIN
    low = wins[-1] * per
    at = window_map(wins)
    return pl.pallas_call(
        functools.partial(attn_fwd_kernel, wins, nh),
        grid=(len(wins) * per,),
        in_specs=[
            SMEM,
            pl.BlockSpec((QB, c), lambda i: (at(i), 0)),
            whole((kv, c)),
            whole((kv, c)),
        ],
        out_specs=[
            pl.BlockSpec((QB, c), lambda i: (at(i) - low, 0)),
            pl.BlockSpec((8, QB), lambda i: (0, at(i) - low)),
        ],
        out_shape=[SDS((len(wins) * WIN, c), BF16), SDS((8, len(wins) * WIN), F32)],
        cost_estimate=cost(
            sum(4 * WIN * (w + 1) * WIN * c * 4 for w in wins),
            4 * kv * c + 4 * len(wins) * WIN * c,
            sum(WIN * (w + 1) * WIN * nh for w in wins),
        ),
        compiler_params=params(),
        name="attn_fwd",
    )(starts, q, k, v)


def ffn_kernel(
    nb, core, m0, m1, m2, m3, tok, row, cot, wo0, wo1, wo2, wo3, b_out, gain, shift, w_in, b_in, w_down,
    hid, n2, act, gpre, keep, send,
):
    i = pl.program_id(0)
    attn = nn(m0[...], wo0[...]) + nn(m1[...], wo1[...]) + nn(m2[...], wo2[...]) + nn(m3[...], wo3[...])
    h = tok[...].astype(F32) + row[...] + attn + b_out[...]
    hat, _ = norm_parts(h)
    n = (hat * gain[...] + shift[...]).astype(BF16)
    n2[...] = n
    z = nn(n, w_in[...]) + b_in[...]
    z2 = z * z
    th = jnp.tanh(z * (GELU_C + (GELU_C * 0.044715) * z2))
    half = 0.5 * (1.0 + th)
    a = (z * half).astype(BF16)
    act[...] = a
    slope = half + (0.5 * z) * (1.0 - th * th) * (GELU_C + (3.0 * 0.044715 * GELU_C) * z2)
    gp = (nt(cot[...], w_down[...]) * slope).astype(BF16)
    gpre[...] = gp
    mlp = nn(a, w_down[...]).astype(BF16)
    two = nt(gp, w_in[...]).astype(BF16)

    @pl.when(i < nb // 2)
    def _():
        hid[...] = h
        keep[0] = two
        keep[1] = mlp

    @pl.when(i >= nb // 2)
    def _():
        send[0] = two
        send[1] = mlp


def ffn_call(core, ms, tok, row, cot, wos, b_out, gain, shift, w_in, b_in, w_down, row0):
    n, c = ms[0].shape
    d = tok.shape[1]
    u = w_in.shape[1]
    nb = n // BT
    off = row0 // BT
    kf = functools.partial(kept_first, nb=nb)
    both = lambda at: pl.BlockSpec((2, BT, d), lambda i, core: (0, at(i), 0))
    return pl.pallas_call(
        functools.partial(ffn_kernel, nb),
        grid_spec=pltpu.PrefetchScalarGridSpec(
            num_scalar_prefetch=1,
            grid=(nb,),
            in_specs=[kf(c)] * 4
            + [kf(d, offset=off), whole((1, d)), kf(d, offset=off)]
            + [whole((c, d))] * 4
            + [whole((d,))] * 3
            + [whole((d, u)), whole((u,)), whole((u, d))],
            out_specs=[first_half(d, nb), kf(d), kf(u), kf(u)]
            + [both(lambda i: jnp.minimum(i, nb // 2 - 1)), both(lambda i: jnp.maximum(i - nb // 2, 0))],
        ),
        out_shape=[SDS((n // 2, d), F32), SDS((n, d), BF16), SDS((n, u), BF16), SDS((n, u), BF16)]
        + [SDS((2, n // 2, d), BF16)] * 2,
        cost_estimate=cost(2 * n * d * (4 * c + 4 * u), n * (8 * c + 16 * d) + 8 * d * c + 4 * d * u, n * u),
        compiler_params=params(20),
        name="ffn",
    )(core, *ms, tok, row, cot, *wos, b_out, gain, shift, w_in, b_in, w_down)


def split_store(acc, first, rows, bit, keep, send):
    half = rows // 2
    keep[...] = acc[pl.ds(pl.multiple_of(first + bit * half, 16), half), :].astype(BF16)
    send[...] = acc[pl.ds(pl.multiple_of(first + (1 - bit) * half, 16), half), :].astype(BF16)


def halve_kernel(bits, ka, ra, kb, rb, oka, osa, okb, osb, acc):
    for part, (k, r, ok, os_) in enumerate(((ka, ra, oka, osa), (kb, rb, okb, osb))):
        acc[...] = k[...].astype(F32) + r[...].astype(F32)
        split_store(acc, 0, k.shape[0], bits[2 + part], ok, os_)


def halve_call(bits, ka, ra, kb, rb):
    n, d = ka.shape
    o = SDS((n // 2, d), BF16)
    return pl.pallas_call(
        halve_kernel,
        in_specs=[SMEM] + [pl.BlockSpec((n, d))] * 4,
        out_specs=[pl.BlockSpec((n // 2, d))] * 4,
        out_shape=[o] * 4,
        scratch_shapes=[pltpu.VMEM((n, d), F32)],
        cost_estimate=cost(2 * n * d, 12 * n * d),
        compiler_params=params(8),
        name="halve",
    )(bits, ka, ra, kb, rb)


def add_kernel(ka, ra, kb, rb, oa, ob):
    oa[...] = (ka[...].astype(F32) + ra[...].astype(F32)).astype(BF16)
    ob[...] = (kb[...].astype(F32) + rb[...].astype(F32)).astype(BF16)


def add_call(ka, ra, kb, rb):
    n, d = ka.shape
    return pl.pallas_call(
        add_kernel,
        in_specs=[pl.BlockSpec((n, d))] * 4,
        out_specs=[pl.BlockSpec((n, d))] * 2,
        out_shape=[SDS((n, d), BF16)] * 2,
        cost_estimate=cost(2 * n * d, 12 * n * d),
        compiler_params=params(8),
        name="pair_add",
    )(ka, ra, kb, rb)


def join_kernel(sa, ra, sb, rb, oa, ob):
    n = sa.shape[0]
    for s, r, o in ((sa, ra, oa), (sb, rb, ob)):
        o[:n, :] = s[...]
        o[n:, :] = r[...]


def join_call(sa, ra, sb, rb):
    n, d = sa.shape
    return pl.pallas_call(
        join_kernel,
        in_specs=[pl.BlockSpec((n, d))] * 4,
        out_specs=[pl.BlockSpec((2 * n, d))] * 2,
        out_shape=[SDS((2 * n, d), BF16)] * 2,
        cost_estimate=cost(0, 16 * n * d),
        compiler_params=params(8),
        name="join",
    )(sa, ra, sb, rb)


def place_kernel(bits, pa, ra, pb, rb, *outs):
    n = pa.shape[0] // 2
    for part, (p, r) in enumerate(((pa, ra), (pb, rb))):
        b0, b1 = bits[part], bits[2 + part]
        for src, first in ((p, b0), (r, 1 - b0)):
            for sub, second in ((0, b1), (1, 1 - b1)):
                value = src[sub * n : (sub + 1) * n, :].astype(F32)
                if len(outs) == 2:
                    outs[part][pl.ds(pl.multiple_of((2 * first + second) * n, 8), n), :] = value
                else:
                    for which in range(2):

                        @pl.when(first == which)
                        def _(out=outs[2 * part + which]):
                            out[pl.ds(pl.multiple_of(second * n, 8), n), :] = value


def place_call(bits, pa, ra, pb, rb, pieces):
    n, d = pa.shape
    m = 4 * n // pieces
    return pl.pallas_call(
        place_kernel,
        in_specs=[SMEM] + [pl.BlockSpec((n, d))] * 4,
        out_specs=[pl.BlockSpec((m, d))] * pieces,
        out_shape=[SDS((m, d), F32)] * pieces,
        cost_estimate=cost(0, 24 * n * d),
        compiler_params=params(14),
        name="place",
    )(bits, pa, ra, pb, rb)


def half_sum_kernel(keep, got, out):
    out[...] = (keep[0].astype(F32) + got[0].astype(F32)).astype(BF16)


def half_sum(keep, got, which):
    _, n, d = keep.shape
    part = pl.BlockSpec((1, n, d), lambda i: (which, 0, 0))
    return pl.pallas_call(
        half_sum_kernel,
        grid=(1,),
        in_specs=[part, part],
        out_specs=whole((n, d)),
        out_shape=SDS((n, d), BF16),
        cost_estimate=cost(n * d, 6 * n * d),
        compiler_params=params(8),
        name="half_sum",
    )(keep, got)


def ffn_grad_kernel(na, bits, n2a, n2b, gpa, gpb, aca, acb, cot, ka, sa, kb, sb, sums, acc_in, acc_down):
    i = pl.program_id(0)

    @pl.when(i == 0)
    def _():
        acc_in[...] = jnp.zeros_like(acc_in)
        acc_down[...] = jnp.zeros_like(acc_down)
        sums[...] = jnp.zeros_like(sums)

    def step(n2, gp, ac):
        acc_in[...] += tn(n2[...], gp[...])
        acc_down[...] += tn(ac[...], cot[...])
        sums[0:1, :] += col_sum(gp[...].astype(F32))
        sums[1:2, :] += col_sum(cot[...].astype(F32))

    @pl.when(i < na)
    def _():
        step(n2a, gpa, aca)

    @pl.when(i >= na)
    def _():
        step(n2b, gpb, acb)

    @pl.when(i == pl.num_programs(0) - 1)
    def _():
        split_store(acc_in, 0, acc_in.shape[0], bits[0], ka, sa)
        split_store(acc_down, 0, acc_down.shape[0], bits[1], kb, sb)


def ffn_grad_call(bits, n2a, n2b, gpa, gpb, aca, acb, cot, block=512):
    length, d = cot.shape
    u = gpa.shape[1]
    na, nb = n2a.shape[0] // block, n2b.shape[0] // block
    fa = lambda w: pl.BlockSpec((block, w), lambda i: (jnp.minimum(i, na - 1), 0))
    fb = lambda w: pl.BlockSpec((block, w), lambda i: (jnp.maximum(i - na, 0), 0))
    return pl.pallas_call(
        functools.partial(ffn_grad_kernel, na),
        grid=(na + nb,),
        in_specs=[
            SMEM, fa(d), fb(d), fa(u), fb(u), fa(u), fb(u),
            pl.BlockSpec((block, d), lambda i: (lax.rem(i + nb, na + nb), 0)),
        ],
        out_specs=[whole((d // 2, u))] * 2 + [whole((u // 2, d))] * 2 + [whole((8, d))],
        out_shape=[SDS((d // 2, u), BF16)] * 2 + [SDS((u // 2, d), BF16)] * 2 + [SDS((8, d), F32)],
        scratch_shapes=[pltpu.VMEM((d, u), F32), pltpu.VMEM((u, d), F32)],
        cost_estimate=cost(4 * length * d * u, length * (4 * d + 4 * u) + 4 * d * u),
        compiler_params=params(22),
        name="ffn_grad",
    )(bits, n2a, n2b, gpa, gpb, aca, acb, cot)


def norm_two_kernel(core, s, x, hid, cot, gain, gh, ghb, sums):
    @pl.when(pl.program_id(0) == 0)
    def _():
        sums[...] = jnp.zeros_like(sums)

    two = s[...].astype(F32) + x[...].astype(F32)
    hat, root = norm_parts(hid[...])
    g = cot[...].astype(F32) + norm_back(two * gain[...], hat, root)
    gh[...] = g
    ghb[...] = g.astype(BF16)
    sums[0:1, :] += col_sum(two * hat)
    sums[1:2, :] += col_sum(two)
    sums[2:3, :] += col_sum(g)


def half_rows(d, n, row0):
    return pl.BlockSpec((BT, d), lambda i, core: (row0 // BT + core[0] * (n // BT) + i, 0))


def norm_two_call(core, s, x, hid, cot, gain, row0):
    n, d = hid.shape
    return pl.pallas_call(
        norm_two_kernel,
        grid_spec=pltpu.PrefetchScalarGridSpec(
            num_scalar_prefetch=1,
            grid=(n // BT,),
            in_specs=[rows_at(d)] * 3 + [half_rows(d, n, row0), whole((d,))],
            out_specs=[rows_at(d)] * 2 + [whole((8, d))],
        ),
        out_shape=[SDS((n, d), F32), SDS((n, d), BF16), SDS((8, d), F32)],
        cost_estimate=cost(20 * n * d, n * 16 * d),
        compiler_params=params(16),
        name="norm_two_back",
    )(core, s, x, hid, cot, gain)


def attn_bwd_window(win, sub, nh, starts, q, k, v, g, lse, dq, ak, av):
    base = win * WIN
    start = starts[win]
    qpos = base + sub * QB + lax.broadcasted_iota(jnp.int32, (1, QB), 1)
    limit = jnp.where((qpos >= start) & (qpos < start + PIECE), start + PIECE - 1, qpos)
    kpos = base + lax.broadcasted_iota(jnp.int32, (WIN, 1), 0)
    allow = kpos <= limit
    near = slice(base, base + WIN)
    for h in range(nh):
        cols = slice(h * HD, (h + 1) * HD)
        qh = q[:, cols]
        gh = g[:, cols]
        ls = lse[h : h + 1, :]
        pn = jnp.exp(jnp.where(allow, nt(k[near, cols], qh), -1e30) - ls)
        dpn = nt(v[near, cols], gh)
        centre = col_sum(pn * dpn)
        if win:
            pf = jnp.exp(nt(k[:base, cols], qh) - ls)
            dpf = nt(v[:base, cols], gh)
            centre = centre + col_sum(pf * dpf)
        dsn = (pn * (dpn - centre)).astype(BF16)
        dqh = tn(dsn, k[near, cols])
        ak[near, cols] += nn(dsn, qh)
        av[near, cols] += nn(pn.astype(BF16), gh)
        if win:
            dsf = (pf * (dpf - centre)).astype(BF16)
            dqh = dqh + tn(dsf, k[:base, cols])
            ak[:base, cols] += nn(dsf, qh)
            av[:base, cols] += nn(pf.astype(BF16), gh)
        dq[:, cols] = (dqh.astype(BF16).astype(F32) * SCALE).astype(BF16)


def attn_bwd_kernel(wins, nh, carried, starts, core, q, k, v, mine, other, w_out, lse, *rest):
    step = pl.program_id(0)
    per = WIN // QB
    if carried:
        dk0, dv0, dq, dk, dv, ak, av, gm = rest
    else:
        dq, dk, dv, dkf, dvf, ak, av, gm = rest

    @pl.when(step == 0)
    def _():
        if carried:
            ak[...] = dk0[...]
            av[...] = dv0[...]
        else:
            ak[...] = jnp.zeros_like(ak)
            av[...] = jnp.zeros_like(av)

    half = len(wins) * per // 2
    spot = window_map(wins)(step) - wins[-1] * per
    own = spot // half == core[0]

    @pl.when(own)
    def _():
        gm[...] = nt(mine[...], w_out[...]).astype(BF16)

    @pl.when(jnp.logical_not(own))
    def _():
        gm[...] = nt(other[...], w_out[...]).astype(BF16)

    for n, win in enumerate(wins):

        @pl.when(step // per == n)
        def _(win=win):
            attn_bwd_window(win, lax.rem(step, per), nh, starts, q, k, v, gm, lse, dq, ak, av)

    @pl.when(step == pl.num_programs(0) - 1)
    def _():
        low = wins[-1] * WIN
        dk[...] = ak[low:, :].astype(BF16)
        dv[...] = av[low:, :].astype(BF16)
        if not carried:
            dkf[...] = ak[:low, :]
            dvf[...] = av[:low, :]


def attn_bwd_call(starts, core, q, k, v, mine, other, w_out, lse, carry, wins):
    c, d = w_out.shape
    nh = c // HD
    per = WIN // QB
    kv = (wins[0] + 1) * WIN
    n = len(wins) * WIN
    low = wins[-1] * per
    half = len(wins) * per // 2
    at = window_map(wins)
    carried = carry is not None
    near = pl.BlockSpec((QB, c), lambda i: (at(i) - low, 0))
    part = pl.BlockSpec((QB, d), lambda i: (lax.rem(at(i) - low, half), 0))
    rest = kv - n
    return pl.pallas_call(
        functools.partial(attn_bwd_kernel, wins, nh, carried),
        grid=(len(wins) * per,),
        in_specs=[
            SMEM,
            SMEM,
            pl.BlockSpec((QB, c), lambda i: (at(i), 0)),
            whole((kv, c)),
            whole((kv, c)),
            part,
            part,
            whole((c, d)),
            pl.BlockSpec((8, QB), lambda i: (0, at(i) - low)),
        ]
        + ([whole((kv, c))] * 2 if carried else []),
        out_specs=[near, whole((n, c)), whole((n, c))] + ([] if carried else [whole((rest, c))] * 2),
        out_shape=[SDS((n, c), BF16)] * 3 + ([] if carried else [SDS((rest, c), F32)] * 2),
        scratch_shapes=[pltpu.VMEM((kv, c), F32)] * 2 + [pltpu.VMEM((QB, c), BF16)],
        cost_estimate=cost(
            sum(10 * WIN * (w + 1) * WIN * c * 4 for w in wins),
            12 * kv * c + 8 * n * c,
            sum(WIN * (w + 1) * WIN * nh for w in wins),
        ),
        compiler_params=params(20),
        name="attn_bwd",
    )(starts, core, q, k, v, mine, other, w_out, lse, *(carry if carried else ()))


def one_kernel(nb, core, dq, dk, dv, wq, wk, wv, keep, send, sums):
    i = pl.program_id(0)

    @pl.when(i == 0)
    def _():
        sums[...] = jnp.zeros_like(sums)

    part = (nn(dq[...], wq[...]) + nn(dk[...], wk[...]) + nn(dv[...], wv[...])).astype(BF16)
    sums[0:1, :] += col_sum(dq[...].astype(F32))
    sums[1:2, :] += col_sum(dv[...].astype(F32))

    @pl.when(i < nb // 2)
    def _():
        keep[0] = part

    @pl.when(i >= nb // 2)
    def _():
        send[0] = part


def one_call(core, dq, dk, dv, wq, wk, wv):
    n, c = dq.shape
    d = wq.shape[1]
    nb = n // BT
    kf = functools.partial(kept_first, nb=nb)
    return pl.pallas_call(
        functools.partial(one_kernel, nb),
        grid_spec=pltpu.PrefetchScalarGridSpec(
            num_scalar_prefetch=1,
            grid=(nb,),
            in_specs=[kf(c)] * 3 + [whole((c, d))] * 3,
            out_specs=[
                pl.BlockSpec((1, BT, d), lambda i, core: (0, jnp.minimum(i, nb // 2 - 1), 0)),
                pl.BlockSpec((1, BT, d), lambda i, core: (0, jnp.maximum(i - nb // 2, 0), 0)),
                whole((8, c)),
            ],
        ),
        out_shape=[SDS((1, n // 2, d), BF16)] * 2 + [SDS((8, c), F32)],
        cost_estimate=cost(6 * n * d * c, n * (6 * c + 2 * d) + 6 * d * c),
        compiler_params=params(16),
        name="grad_one",
    )(core, dq, dk, dv, wq, wk, wv)


def attn_grad_kernel(bits, core, n1a, n1b, dqa, dqb, dka, dkb, dva, dvb, mxa, mxb, ga0, ga1, gb0, gb1,
                     ka, sa, kb, sb, acc):
    i = pl.program_id(0)
    c = mxa.shape[1]

    @pl.when(i == 0)
    def _():
        acc[...] = jnp.zeros_like(acc)

    def step(n1, dq, dk, dv, mx, gh):
        n = n1[...]
        acc[:c, :] += tn(dq[...], n)
        acc[c : 2 * c, :] += tn(dk[...], n)
        acc[2 * c : 3 * c, :] += tn(dv[...], n)
        acc[3 * c :, :] += tn(mx[...], gh[...])

    for at, args in enumerate(
        ((n1a, dqa, dka, dva, mxa, ga0), (n1a, dqa, dka, dva, mxa, ga1),
         (n1b, dqb, dkb, dvb, mxb, gb0), (n1b, dqb, dkb, dvb, mxb, gb1))
    ):

        @pl.when(i == at)
        def _(args=args):
            step(*args)

    @pl.when(i == 3)
    def _():
        rows = acc.shape[0] // 2
        split_store(acc, 0, rows, bits[0], ka, sa)
        split_store(acc, rows, rows, bits[1], kb, sb)


def attn_grad_call(bits, core, n1, dqs, dks, dvs, mxs, ghs):
    length, d = n1.shape
    c = dqs[0].shape[1]
    na, nb = dqs[0].shape[0] // 2, dqs[1].shape[0] // 2
    fa = lambda w, o=0: pl.BlockSpec((na, w), lambda i, bits, core: (o + lax.rem(jnp.minimum(i, 1) + core[0], 2), 0))
    fb = lambda w: pl.BlockSpec((nb, w), lambda i, bits, core: (lax.rem(jnp.maximum(i - 2, 0) + core[0], 2), 0))
    pairs = [s for _ in range(4) for s in (fa(c), fb(c))]
    return pl.pallas_call(
        attn_grad_kernel,
        grid_spec=pltpu.PrefetchScalarGridSpec(
            num_scalar_prefetch=2,
            grid=(4,),
            in_specs=[fa(d, 2 * nb // na), fb(d)] + pairs + [whole((na, d))] * 2 + [whole((nb, d))] * 2,
            out_specs=[whole((c, d))] * 4,
            scratch_shapes=[pltpu.VMEM((4 * c, d), F32)],
        ),
        out_shape=[SDS((c, d), BF16)] * 4,
        cost_estimate=cost(8 * length * d * c, length * (6 * d + 8 * c) + 8 * d * c),
        compiler_params=params(18),
        name="attn_grad",
    )(bits, core, n1, n1, dqs[0], dqs[1], dks[0], dks[1], dvs[0], dvs[1], mxs[0], mxs[1], *ghs[0], *ghs[1])


def norm_one_kernel(core, s, x, tok, row, gh, gain, out, sums):
    @pl.when(pl.program_id(0) == 0)
    def _():
        sums[...] = jnp.zeros_like(sums)

    one = s[...].astype(F32) + x[...].astype(F32)
    hat, root = norm_parts(tok[...].astype(F32) + row[...])
    g = gh[...] + norm_back(one * gain[...], hat, root)
    out[...] = g.astype(BF16)
    sums[0:1, :] += col_sum(one * hat)
    sums[1:2, :] += col_sum(one)
    sums[2:3, :] += col_sum(g)


def norm_one_call(core, s, x, tok, row, gh, gain, row0):
    n, d = gh.shape
    return pl.pallas_call(
        norm_one_kernel,
        grid_spec=pltpu.PrefetchScalarGridSpec(
            num_scalar_prefetch=1,
            grid=(n // BT,),
            in_specs=[rows_at(d)] * 2 + [half_rows(d, n, row0), whole((1, d)), rows_at(d), whole((d,))],
            out_specs=[rows_at(d), whole((8, d))],
        ),
        out_shape=[SDS((n, d), BF16), SDS((8, d), F32)],
        cost_estimate=cost(20 * n * d, n * 12 * d),
        compiler_params=params(16),
        name="norm_one_back",
    )(core, s, x, tok, row, gh, gain)


def out_kernel(s, x, hid, b_down, out):
    out[...] = (hid[...] + s[...].astype(F32) + x[...].astype(F32) + b_down[...]).astype(BF16)


def out_call(s, x, hid, b_down):
    n, d = hid.shape
    return pl.pallas_call(
        out_kernel,
        grid=(n // BT,),
        in_specs=[rows_at(d)] * 3 + [whole((d,))],
        out_specs=rows_at(d),
        out_shape=SDS((n, d), BF16),
        cost_estimate=cost(3 * n * d, n * 10 * d),
        compiler_params=params(12),
        name="layer_out",
    )(s, x, hid, b_down)


def rows_kernel(core, ao, at, bo, bt, out):
    na, nb = ao.shape[0], bo.shape[0]
    c = core[0]
    for src, base, n, half in ((bo, 0, nb, c), (bt, 0, nb, 1 - c), (ao, 2 * nb, na, c), (at, 2 * nb, na, 1 - c)):
        out[pl.ds(pl.multiple_of(base + half * n, 16), n), :] = src[...]


def rows_call(core, ao, at, bo, bt):
    na, d = ao.shape
    nb = bo.shape[0]
    return pl.pallas_call(
        rows_kernel,
        in_specs=[SMEM] + [pl.BlockSpec((na, d))] * 2 + [pl.BlockSpec((nb, d))] * 2,
        out_specs=pl.BlockSpec((2 * (na + nb), d)),
        out_shape=SDS((2 * (na + nb), d), BF16),
        cost_estimate=cost(0, 8 * (na + nb) * d),
        compiler_params=params(12),
        name="in_order",
    )(core, ao, at, bo, bt)


VALUE_AT = 256
STEP_AT = 512


def pack_kernel(scal, s2a, s2b, s1a, s1b, soa, sob, ffn, out):
    me, step = scal[0], scal[1]
    c = soa.shape[1]
    n = out.shape[0] - 8
    out[0:3, :] = s2a[0:3, :] + s2b[0:3, :]
    out[3:5, :] = s1a[0:2, :] + s1b[0:2, :]
    out[5:7, :] = ffn[0:2, :]
    out[7:8, :] = jnp.zeros((1, out.shape[1]), F32)
    so = soa[...] + sob[...]
    out[7:8, 0:c] = so[0:1, :]
    out[7:8, VALUE_AT : VALUE_AT + c] = so[1:2, :]
    lane = lax.broadcasted_iota(jnp.int32, (1, out.shape[1] - STEP_AT), 1)
    out[7:8, STEP_AT:] = jnp.where(lane == me, step.astype(F32), 0.0)
    spot = lax.broadcasted_iota(jnp.int32, (n, 1), 0) == me
    out[8:, :] = jnp.where(spot, s1a[2:3, :] + s1b[2:3, :], 0.0)


def pack_call(scal, n_dp, s2a, s2b, s1a, s1b, soa, sob, ffn):
    d = ffn.shape[1]
    rows = 8 + -(-n_dp // 8) * 8
    return pl.pallas_call(
        pack_kernel,
        in_specs=[SMEM] + [pl.BlockSpec(v.shape) for v in (s2a, s2b, s1a, s1b, soa, sob, ffn)],
        out_specs=pl.BlockSpec((rows, d)),
        out_shape=SDS((rows, d), F32),
        compiler_params=params(4),
        name="pack",
    )(scal, s2a, s2b, s1a, s1b, soa, sob, ffn)


def small_add_kernel(own_rows, a, b, out):
    out[...] = a[...] + b[...]
    if own_rows:
        out[5:8, :] = a[5:8, :]


def small_add(a, b, own_rows=False):
    return pl.pallas_call(
        functools.partial(small_add_kernel, own_rows),
        in_specs=[pl.BlockSpec(a.shape)] * 2,
        out_specs=pl.BlockSpec(a.shape),
        out_shape=SDS(a.shape, F32),
        compiler_params=params(4),
        name="small_add",
    )(a, b)


def unpack_kernel(n_dp, small, got, *outs):
    table, vecs, bq, bv, full = outs[0], outs[1:8], outs[8], outs[9], outs[10]
    full[...] = small[...] + got[...]
    for n, vec in enumerate(vecs):
        vec[...] = full[n, :]
    c = bq.shape[0]
    bq[...] = full[7, 0:c]
    bv[...] = full[7, VALUE_AT : VALUE_AT + c]
    table[...] = jnp.zeros_like(table)
    steps = full[7:8, STEP_AT:]
    lane = lax.broadcasted_iota(jnp.int32, steps.shape, 1)
    for n in range(n_dp):
        at = jnp.sum(jnp.where(lane == n, steps, 0.0)).astype(jnp.int32)
        table[pl.ds(at, 1), :] += full[8 + n : 9 + n, :]


def unpack_call(n_dp, table_rows, c, small, got):
    rows, d = small.shape
    shapes = [(table_rows, d)] + [(d,)] * 7 + [(c,)] * 2
    return pl.pallas_call(
        functools.partial(unpack_kernel, n_dp),
        in_specs=[pl.BlockSpec(small.shape)] * 2,
        out_specs=[pl.BlockSpec(s) for s in shapes],
        out_shape=[SDS(s, F32) for s in shapes],
        scratch_shapes=[pltpu.VMEM(small.shape, F32)],
        cost_estimate=cost(table_rows * d, 4 * table_rows * d),
        compiler_params=params(10),
        name="unpack",
    )(small, got)


def after(token, value):
    return lax.optimization_barrier((token, value))[1]


class Spread:
    def __init__(self, n_dp, bits, orders):
        self.n_dp, self.bits, self.orders = n_dp, bits, orders

    def swap(self, level, a, b):
        pair = lambda order: [(i, i ^ (1 << order[level])) for i in range(self.n_dp)]
        return lax.ppermute(a, "dp", pair(self.orders[0])), lax.ppermute(b, "dp", pair(self.orders[1]))

    def start(self, ka, sa, kb, sb):
        self.keep = (ka, kb)
        self.got = self.swap(0, sa, sb)

    def halve(self, token):
        ka, sa, kb, sb = halve_call(self.bits, after(token, self.keep[0]), self.got[0], self.keep[1], self.got[1])
        self.keep = (ka, kb)
        self.got = self.swap(1, sa, sb)
        self.level = 2
        return ka

    def exchange(self, token):
        self.keep = add_call(after(token, self.keep[0]), self.got[0], self.keep[1], self.got[1])
        level = self.level if self.level < len(self.orders[0]) else 1
        self.level += 1
        self.got = self.swap(level, *self.keep)
        return self.keep[0]

    def join(self, token):
        self.keep = join_call(after(token, self.keep[0]), self.got[0], self.keep[1], self.got[1])
        self.got = self.swap(0, *self.keep)
        return self.keep[0]

    def place(self, token, pieces):
        return place_call(self.bits, after(token, self.keep[0]), self.got[0], self.keep[1], self.got[1], pieces)


def per_device(
    n_tensor,
    n_dp,
    tokens,
    timesteps,
    piece_starts,
    step_table,
    first_gain,
    first_shift,
    w_query,
    b_query,
    w_key,
    w_value,
    b_value,
    w_out,
    b_out,
    second_gain,
    second_shift,
    w_in,
    b_in,
    w_down,
    b_down,
    cotangent,
):
    length, d = tokens.shape[1:]
    c = w_query.shape[1]
    rank = lax.axis_index("tensor").astype(jnp.int32)
    me = lax.axis_index("dp").astype(jnp.int32)
    over_x = [(i, i ^ 2) for i in range(n_tensor)]
    over_core = [(i, i ^ 1) for i in range(n_tensor)]
    swap_x = lambda v: lax.ppermute(v, "tensor", over_x)
    swap_core = lambda v: lax.ppermute(v, "tensor", over_core)
    n_bits = n_dp.bit_length() - 1
    orders = (list(range(n_bits)), list(range(1, n_bits)) + [0])
    bit = lambda b: (me >> b) & 1
    bits = jnp.stack([bit(orders[0][0]), bit(orders[1][0]), bit(orders[0][1]), bit(orders[1][1])])
    scal = jnp.stack([me, timesteps[0]])
    core = (rank & 1)[None]
    tok, bits, scal, core, starts, w_out0 = lax.optimization_barrier(
        (tokens[0], bits, scal, core, piece_starts[0], w_out)
    )
    cot = cotangent[0]
    wq, wk, wv = w_query.T, w_key.T, w_value.T
    wo0, wo2 = w_out, swap_x(w_out0)
    wo1, wo3 = swap_core(wo0), swap_core(wo2)

    top = length // WIN - 1
    groups = [[top], list(range(top - 1, -1, -1))]
    row0s = [top * WIN, 0]

    def gathered(m):
        m2 = swap_x(m)
        return [m, swap_core(m), m2, swap_core(m2)]

    n1, q, k, v, row = qkv_call(timesteps, tok, step_table, first_gain, first_shift, wq, wk, wv, b_query, b_value)

    def ffn_of(ms, n, token):
        return ffn_call(
            core, [after(token, ms[0])] + ms[1:], tok, row, cot, [wo0, wo1, wo2, wo3], b_out, second_gain,
            second_shift, w_in, b_in, w_down, row0s[n],
        )

    mix_a, lse_a = attn_fwd_call(starts, q, k, v, groups[0])
    ms_a = gathered(mix_a)
    mix_b, lse_b = attn_fwd_call(starts, after(mix_a, q), k, v, groups[1])
    ms_b = gathered(mix_b)

    hid_a, n2_a, act_a, gpre_a, keep_a, send_a = ffn_of(ms_a, 0, mix_b)
    got_a = swap_core(send_a)
    two_a = half_sum(keep_a, got_a, 0)
    twox_a = swap_x(two_a)
    hid_b, n2_b, act_b, gpre_b, keep_b, send_b = ffn_of(ms_b, 1, two_a)
    got_b = swap_core(send_b)
    gh_a, ghb_a, s2_a = norm_two_call(core, after(n2_b, two_a), twox_a, hid_a, cot, second_gain, row0s[0])
    gho_a = swap_core(ghb_a)
    two_b = half_sum(after(ghb_a, keep_b), got_b, 0)
    twox_b = swap_x(two_b)
    ka, sa, kb, sb, ffn_sums = ffn_grad_call(bits, after(two_b, n2_a), n2_b, gpre_a, gpre_b, act_a, act_b, cot)
    gff = Spread(n_dp, bits, orders)
    gff.start(ka, sa, kb, sb)
    dq_a, dk_a, dv_a, dkf, dvf = attn_bwd_call(
        starts, core, after(ka, q), k, v, ghb_a, gho_a, w_out, lse_a, None, groups[0]
    )
    one_a, osend_a, so_a = one_call(core, dq_a, dk_a, dv_a, wq, wk, wv)
    ogot_a = swap_core(osend_a)
    t = gff.halve(one_a)
    gh_b, ghb_b, s2_b = norm_two_call(core, after(t, two_b), twox_b, hid_b, cot, second_gain, row0s[1])
    gho_b = swap_core(ghb_b)
    os_a = half_sum(after(ghb_b, one_a), ogot_a, 0)
    ox_a = swap_x(os_a)
    dq_b, dk_b, dv_b = attn_bwd_call(
        starts, core, after(os_a, q), k, v, ghb_b, gho_b, w_out, lse_b, (dkf, dvf), groups[1]
    )
    t = gff.exchange(dq_b)
    one_b, osend_b, so_b = one_call(core, after(t, dq_b), dk_b, dv_b, wq, wk, wv)
    ogot_b = swap_core(osend_b)
    ka, sa, kb, sb = attn_grad_call(
        bits, core, after(one_b, n1), (dq_a, dq_b), (dk_a, dk_b), (dv_a, dv_b), (mix_a, mix_b),
        ((ghb_a, gho_a), (ghb_b, gho_b)),
    )
    os_b = half_sum(after(ka, one_b), ogot_b, 0)
    ox_b = swap_x(os_b)
    t = os_b
    for _ in range(n_bits - 2):
        t = gff.exchange(t)
    gat = Spread(n_dp, bits, orders)
    gat.start(ka, sa, kb, sb)
    gt_a, s1_a = norm_one_call(core, after(t, os_a), ox_a, tok, row, gh_a, first_gain, row0s[0])
    gto_a = swap_core(gt_a)
    t = gff.join(gt_a)
    mlp_a = half_sum(after(t, keep_a), got_a, 1)
    mlp_b = half_sum(after(mlp_a, keep_b), got_b, 1)
    gt_b, s1_b = norm_one_call(core, after(mlp_b, os_b), ox_b, tok, row, gh_b, first_gain, row0s[1])
    mlpx_a = swap_x(mlp_a)
    mlpx_b = swap_x(mlp_b)
    gto_b = swap_core(gt_b)
    small = pack_call(after(gt_b, scal), n_dp, s2_a, s2_b, s1_a, s1_b, so_a, so_b, ffn_sums)
    t = gat.halve(small)
    small = small_add(after(t, small), swap_core(small), True)
    for b in range(n_bits - 1):
        small = small_add(small, lax.ppermute(small, "dp", [(i, i ^ (1 << b)) for i in range(n_dp)]))
    last = lax.ppermute(small, "dp", [(i, i ^ (1 << (n_bits - 1))) for i in range(n_dp)])
    g_in, g_down = gff.place(small, 2)
    t = gat.exchange(g_in)
    g_table, g_sg, g_ss, g_bo, g_fg, g_fs, g_bi, g_bd, g_bq, g_bv = unpack_call(
        n_dp, step_table.shape[0], c, after(t, small), last
    )
    grad_tokens = rows_call(core, after(g_sg, gt_a), gto_a, gt_b, gto_b)
    t = grad_tokens
    for _ in range(n_bits - 2):
        t = gat.exchange(t)
    o_a = out_call(after(t, mlp_a), mlpx_a, hid_a, b_down)
    oo_a = swap_core(o_a)
    o_b = out_call(after(o_a, mlp_b), mlpx_b, hid_b, b_down)
    oo_b = swap_core(o_b)
    t = gat.join(o_b)
    output = rows_call(core, after(t, o_a), oo_a, o_b, oo_b)
    g_q, g_k, g_v, g_o = gat.place(output, 4)
    return (
        output[None],
        grad_tokens[None],
        g_table,
        g_fg,
        g_fs,
        g_q.T,
        g_bq,
        g_k.T,
        g_v.T,
        g_bv,
        g_o,
        g_bo,
        g_sg,
        g_ss,
        g_in,
        g_bi,
        g_down,
        g_bd,
    )


def solution(mesh):
    in_specs = (
        P("dp", None, None),
        P("dp"),
        P("dp", None),
        P(),
        P(),
        P(),
        P(None, "tensor"),
        P("tensor"),
        P(None, "tensor"),
        P(None, "tensor"),
        P("tensor"),
        P("tensor", None),
        P(),
        P(),
        P(),
        P(None, "tensor"),
        P("tensor"),
        P("tensor", None),
        P(),
        P("dp", None, None),
    )
    out_specs = (
        P("dp", None, None),
        P("dp", None, None),
        P(),
        P(),
        P(),
        P(None, "tensor"),
        P("tensor"),
        P(None, "tensor"),
        P(None, "tensor"),
        P("tensor"),
        P("tensor", None),
        P(),
        P(),
        P(),
        P(None, "tensor"),
        P("tensor"),
        P("tensor", None),
        P(),
    )
    return jax.shard_map(
        functools.partial(per_device, mesh.shape["tensor"], mesh.shape["dp"]),
        mesh=mesh,
        in_specs=in_specs,
        out_specs=out_specs,
        check_vma=False,
    )
```

```python
import functools

import jax
import jax.numpy as jnp
from jax import lax
from jax.experimental import pallas as pl
from jax.experimental.pallas import tpu as pltpu
from jax.sharding import PartitionSpec as P

HD = 64
PIECE = 256
WIN = 2 * PIECE
EPS = 1e-05
QB = 256
BT = 256
F32 = jnp.float32
BF16 = jnp.bfloat16
SDS = jax.ShapeDtypeStruct
SCALE = HD ** (-0.5)
GELU_C = 0.7978845608028654


def nn(a, b):
    return lax.dot_general(a, b, (((1,), (0,)), ((), ())), preferred_element_type=F32)


def nt(a, b):
    return lax.dot_general(a, b, (((1,), (1,)), ((), ())), preferred_element_type=F32)


def tn(a, b):
    return lax.dot_general(a, b, (((0,), (0,)), ((), ())), preferred_element_type=F32)


def norm_parts(v):
    c = v - jnp.mean(v, axis=-1, keepdims=True)
    root = lax.rsqrt(jnp.mean(c * c, axis=-1, keepdims=True) + EPS)
    return c * root, root


def norm_back(e, hat, root):
    return root * (
        e - jnp.mean(e, axis=-1, keepdims=True) - hat * jnp.mean(e * hat, axis=-1, keepdims=True)
    )


def col_sum(v):
    return jnp.sum(v, axis=0, keepdims=True)


def whole(shape):
    return pl.BlockSpec(shape, lambda i, *_: (0,) * len(shape))


def rows_at(width, offset=0, block=BT):
    return pl.BlockSpec((block, width), lambda i, *_: (offset + i, 0))


LONG = pl.CostEstimate(flops=10**11, bytes_accessed=1000, transcendentals=0)
SHORT = pl.CostEstimate(flops=1000, bytes_accessed=1000, transcendentals=0)


def kept_first(width, nb, offset=0):
    return pl.BlockSpec((BT, width), lambda i, core: (offset + lax.rem(i + core[0] * (nb // 2), nb), 0))


def first_half(width, nb):
    return pl.BlockSpec((BT, width), lambda i, core: (jnp.minimum(i, nb // 2 - 1), 0))


def second_half(width, nb):
    return pl.BlockSpec((BT, width), lambda i, core: (jnp.maximum(i - nb // 2, 0), 0))


def params(mib=12):
    return pltpu.CompilerParams(vmem_limit_bytes=mib * 1024 * 1024)


SMEM = pl.BlockSpec(memory_space=pltpu.SMEM)


def qkv_kernel(steps, tok, table, gain, shift, wq, wk, wv, bq, bv, n1, q, k, v, row):
    rows = table[...].astype(F32)
    at = lax.broadcasted_iota(jnp.int32, rows.shape, 0) == lax.rem(steps[0], 8)
    step_row = col_sum(jnp.where(at, rows, 0.0))
    row[...] = step_row
    hat, _ = norm_parts(tok[...].astype(F32) + step_row)
    n = (hat * gain[...] + shift[...]).astype(BF16)
    n1[...] = n
    q[...] = ((nt(n, wq[...]) + bq[...]) * SCALE).astype(BF16)
    k[...] = nt(n, wk[...]).astype(BF16)
    v[...] = (nt(n, wv[...]) + bv[...]).astype(BF16)


def qkv_call(steps, tok, table, gain, shift, wq, wk, wv, bq, bv):
    length, d = tok.shape
    c = wq.shape[0]
    return pl.pallas_call(
        qkv_kernel,
        grid_spec=pltpu.PrefetchScalarGridSpec(
            num_scalar_prefetch=1,
            grid=(length // BT,),
            in_specs=[rows_at(d), pl.BlockSpec((8, d), lambda i, steps: (steps[0] // 8, 0))]
            + [whole((d,))] * 2
            + [whole((c, d))] * 3
            + [whole((c,))] * 2,
            out_specs=[rows_at(d)] + [rows_at(c)] * 3 + [whole((1, d))],
        ),
        out_shape=[SDS((length, d), BF16)] + [SDS((length, c), BF16)] * 3 + [SDS((1, d), F32)],
        cost_estimate=LONG,
        compiler_params=params(),
        name="norm_qkv",
    )(steps, tok, table, gain, shift, wq, wk, wv, bq, bv)


def attn_fwd_window(win, sub, nh, starts, q, k, v, mix, lse):
    base = win * WIN
    start = starts[win]
    qpos = base + sub * QB + lax.broadcasted_iota(jnp.int32, (QB, 1), 0)
    limit = jnp.where((qpos >= start) & (qpos < start + PIECE), start + PIECE - 1, qpos)
    kpos = base + lax.broadcasted_iota(jnp.int32, (1, WIN), 1)
    allow = kpos <= limit
    for h in range(nh):
        cols = slice(h * HD, (h + 1) * HD)
        qh = q[:, cols]
        near = jnp.where(allow, nt(qh, k[base : base + WIN, cols]), -1e30)
        top = jnp.max(near, axis=-1, keepdims=True)
        if win:
            far = nt(qh, k[:base, cols])
            top = jnp.maximum(top, jnp.max(far, axis=-1, keepdims=True))
        pn = jnp.exp(near - top)
        total = jnp.sum(pn, axis=-1, keepdims=True)
        out = nn(pn.astype(BF16), v[base : base + WIN, cols])
        if win:
            pf = jnp.exp(far - top)
            total = total + jnp.sum(pf, axis=-1, keepdims=True)
            out = out + nn(pf.astype(BF16), v[:base, cols])
        mix[:, cols] = (out / total).astype(BF16)
        stat = jnp.broadcast_to(top + jnp.log(total), (QB, 128))
        lse[h : h + 1, :] = jnp.transpose(stat)[0:1, :]


def attn_fwd_kernel(wins, nh, starts, *refs):
    step = pl.program_id(0)
    per = WIN // QB
    for n, win in enumerate(wins):

        @pl.when(step // per == n)
        def _(win=win):
            attn_fwd_window(win, lax.rem(step, per), nh, starts, *refs)


def window_map(wins):
    per = WIN // QB
    return lambda i: (wins[0] - i // per) * per + lax.rem(i, per)


def attn_fwd_call(starts, q, k, v, wins):
    length, c = q.shape
    nh = c // HD
    per = WIN // QB
    kv = (wins[0] + 1) * WIN
    low = wins[-1] * per
    at = window_map(wins)
    return pl.pallas_call(
        functools.partial(attn_fwd_kernel, wins, nh),
        grid=(len(wins) * per,),
        in_specs=[
            SMEM,
            pl.BlockSpec((QB, c), lambda i: (at(i), 0)),
            whole((kv, c)),
            whole((kv, c)),
        ],
        out_specs=[
            pl.BlockSpec((QB, c), lambda i: (at(i) - low, 0)),
            pl.BlockSpec((8, QB), lambda i: (0, at(i) - low)),
        ],
        out_shape=[SDS((len(wins) * WIN, c), BF16), SDS((8, len(wins) * WIN), F32)],
        cost_estimate=LONG,
        compiler_params=params(),
        name="attn_fwd",
    )(starts, q, k, v)


def ffn_kernel(
    nb, core, m0, m1, m2, m3, tok, row, cot, wo0, wo1, wo2, wo3, b_out, gain, shift, w_in, b_in, w_down,
    hid, n2, act, gpre, keep, send,
):
    i = pl.program_id(0)
    attn = nn(m0[...], wo0[...]) + nn(m1[...], wo1[...]) + nn(m2[...], wo2[...]) + nn(m3[...], wo3[...])
    h = tok[...].astype(F32) + row[...] + attn + b_out[...]
    hat, _ = norm_parts(h)
    n = (hat * gain[...] + shift[...]).astype(BF16)
    n2[...] = n
    z = nn(n, w_in[...]) + b_in[...]
    z2 = z * z
    th = jnp.tanh(z * (GELU_C + (GELU_C * 0.044715) * z2))
    half = 0.5 * (1.0 + th)
    a = (z * half).astype(BF16)
    act[...] = a
    slope = half + (0.5 * z) * (1.0 - th * th) * (GELU_C + (3.0 * 0.044715 * GELU_C) * z2)
    gp = (nt(cot[...], w_down[...]) * slope).astype(BF16)
    gpre[...] = gp
    mlp = nn(a, w_down[...]).astype(BF16)
    two = nt(gp, w_in[...]).astype(BF16)

    @pl.when(i < nb // 2)
    def _():
        hid[...] = h
        keep[0] = two
        keep[1] = mlp

    @pl.when(i >= nb // 2)
    def _():
        send[0] = two
        send[1] = mlp


def ffn_call(core, ms, tok, row, cot, wos, b_out, gain, shift, w_in, b_in, w_down, row0):
    n, c = ms[0].shape
    d = tok.shape[1]
    u = w_in.shape[1]
    nb = n // BT
    off = row0 // BT
    kf = functools.partial(kept_first, nb=nb)
    both = lambda at: pl.BlockSpec((2, BT, d), lambda i, core: (0, at(i), 0))
    return pl.pallas_call(
        functools.partial(ffn_kernel, nb),
        grid_spec=pltpu.PrefetchScalarGridSpec(
            num_scalar_prefetch=1,
            grid=(nb,),
            in_specs=[kf(c)] * 4
            + [kf(d, offset=off), whole((1, d)), kf(d, offset=off)]
            + [whole((c, d))] * 4
            + [whole((d,))] * 3
            + [whole((d, u)), whole((u,)), whole((u, d))],
            out_specs=[first_half(d, nb), kf(d), kf(u), kf(u)]
            + [both(lambda i: jnp.minimum(i, nb // 2 - 1)), both(lambda i: jnp.maximum(i - nb // 2, 0))],
        ),
        out_shape=[SDS((n // 2, d), F32), SDS((n, d), BF16), SDS((n, u), BF16), SDS((n, u), BF16)]
        + [SDS((2, n // 2, d), BF16)] * 2,
        cost_estimate=LONG,
        compiler_params=params(20),
        name="ffn",
    )(core, *ms, tok, row, cot, *wos, b_out, gain, shift, w_in, b_in, w_down)


def split_store(acc, first, rows, bit, keep, send):
    half = rows // 2
    keep[...] = acc[pl.ds(pl.multiple_of(first + bit * half, 16), half), :].astype(BF16)
    send[...] = acc[pl.ds(pl.multiple_of(first + (1 - bit) * half, 16), half), :].astype(BF16)


def halve_kernel(bits, ka, ra, kb, rb, oka, osa, okb, osb, acc):
    for part, (k, r, ok, os_) in enumerate(((ka, ra, oka, osa), (kb, rb, okb, osb))):
        acc[...] = k[...].astype(F32) + r[...].astype(F32)
        split_store(acc, 0, k.shape[0], bits[2 + part], ok, os_)


def halve_call(bits, ka, ra, kb, rb):
    n, d = ka.shape
    o = SDS((n // 2, d), BF16)
    return pl.pallas_call(
        halve_kernel,
        in_specs=[SMEM] + [pl.BlockSpec((n, d))] * 4,
        out_specs=[pl.BlockSpec((n // 2, d))] * 4,
        out_shape=[o] * 4,
        scratch_shapes=[pltpu.VMEM((n, d), F32)],
        cost_estimate=SHORT,
        compiler_params=params(8),
        name="halve",
    )(bits, ka, ra, kb, rb)


def add_kernel(ka, ra, kb, rb, oa, ob):
    oa[...] = (ka[...].astype(F32) + ra[...].astype(F32)).astype(BF16)
    ob[...] = (kb[...].astype(F32) + rb[...].astype(F32)).astype(BF16)


def add_call(ka, ra, kb, rb, hint=SHORT):
    n, d = ka.shape
    return pl.pallas_call(
        add_kernel,
        in_specs=[pl.BlockSpec((n, d))] * 4,
        out_specs=[pl.BlockSpec((n, d))] * 2,
        out_shape=[SDS((n, d), BF16)] * 2,
        cost_estimate=hint,
        compiler_params=params(8),
        name="pair_add",
    )(ka, ra, kb, rb)


def join_kernel(sa, ra, sb, rb, oa, ob):
    n = sa.shape[0]
    for s, r, o in ((sa, ra, oa), (sb, rb, ob)):
        o[:n, :] = s[...]
        o[n:, :] = r[...]


def join_call(sa, ra, sb, rb, hint=SHORT):
    n, d = sa.shape
    return pl.pallas_call(
        join_kernel,
        in_specs=[pl.BlockSpec((n, d))] * 4,
        out_specs=[pl.BlockSpec((2 * n, d))] * 2,
        out_shape=[SDS((2 * n, d), BF16)] * 2,
        cost_estimate=hint,
        compiler_params=params(8),
        name="join",
    )(sa, ra, sb, rb)


def place_kernel(bits, pa, ra, pb, rb, *outs):
    n = pa.shape[0] // 2
    for part, (p, r) in enumerate(((pa, ra), (pb, rb))):
        b0, b1 = bits[part], bits[2 + part]
        for src, first in ((p, b0), (r, 1 - b0)):
            for sub, second in ((0, b1), (1, 1 - b1)):
                value = src[sub * n : (sub + 1) * n, :].astype(F32)
                if len(outs) == 2:
                    outs[part][pl.ds(pl.multiple_of((2 * first + second) * n, 8), n), :] = value
                else:
                    for which in range(2):

                        @pl.when(first == which)
                        def _(out=outs[2 * part + which]):
                            out[pl.ds(pl.multiple_of(second * n, 8), n), :] = value


def place_call(bits, pa, ra, pb, rb, pieces, hint=SHORT):
    n, d = pa.shape
    m = 4 * n // pieces
    return pl.pallas_call(
        place_kernel,
        in_specs=[SMEM] + [pl.BlockSpec((n, d))] * 4,
        out_specs=[pl.BlockSpec((m, d))] * pieces,
        out_shape=[SDS((m, d), F32)] * pieces,
        cost_estimate=hint,
        compiler_params=params(14),
        name="place",
    )(bits, pa, ra, pb, rb)


def half_sum_kernel(keep, got, out):
    out[...] = (keep[0].astype(F32) + got[0].astype(F32)).astype(BF16)


def half_sum(keep, got, which, hint=SHORT):
    _, n, d = keep.shape
    part = pl.BlockSpec((1, n, d), lambda i: (which, 0, 0))
    return pl.pallas_call(
        half_sum_kernel,
        grid=(1,),
        in_specs=[part, part],
        out_specs=whole((n, d)),
        out_shape=SDS((n, d), BF16),
        cost_estimate=hint,
        compiler_params=params(8),
        name="half_sum",
    )(keep, got)


def ffn_grad_kernel(na, bits, n2a, n2b, gpa, gpb, aca, acb, cot, ka, sa, kb, sb, sums, acc_in, acc_down):
    i = pl.program_id(0)

    @pl.when(i == 0)
    def _():
        acc_in[...] = jnp.zeros_like(acc_in)
        acc_down[...] = jnp.zeros_like(acc_down)
        sums[...] = jnp.zeros_like(sums)

    def step(n2, gp, ac):
        acc_in[...] += tn(n2[...], gp[...])
        acc_down[...] += tn(ac[...], cot[...])
        sums[0:1, :] += col_sum(gp[...].astype(F32))
        sums[1:2, :] += col_sum(cot[...].astype(F32))

    @pl.when(i < na)
    def _():
        step(n2a, gpa, aca)

    @pl.when(i >= na)
    def _():
        step(n2b, gpb, acb)

    @pl.when(i == pl.num_programs(0) - 1)
    def _():
        split_store(acc_in, 0, acc_in.shape[0], bits[0], ka, sa)
        split_store(acc_down, 0, acc_down.shape[0], bits[1], kb, sb)


def ffn_grad_call(bits, n2a, n2b, gpa, gpb, aca, acb, cot, block=512):
    length, d = cot.shape
    u = gpa.shape[1]
    na, nb = n2a.shape[0] // block, n2b.shape[0] // block
    fa = lambda w: pl.BlockSpec((block, w), lambda i: (jnp.minimum(i, na - 1), 0))
    fb = lambda w: pl.BlockSpec((block, w), lambda i: (jnp.maximum(i - na, 0), 0))
    return pl.pallas_call(
        functools.partial(ffn_grad_kernel, na),
        grid=(na + nb,),
        in_specs=[
            SMEM, fa(d), fb(d), fa(u), fb(u), fa(u), fb(u),
            pl.BlockSpec((block, d), lambda i: (lax.rem(i + nb, na + nb), 0)),
        ],
        out_specs=[whole((d // 2, u))] * 2 + [whole((u // 2, d))] * 2 + [whole((8, d))],
        out_shape=[SDS((d // 2, u), BF16)] * 2 + [SDS((u // 2, d), BF16)] * 2 + [SDS((8, d), F32)],
        scratch_shapes=[pltpu.VMEM((d, u), F32), pltpu.VMEM((u, d), F32)],
        cost_estimate=LONG,
        compiler_params=params(22),
        name="ffn_grad",
    )(bits, n2a, n2b, gpa, gpb, aca, acb, cot)


def norm_two_kernel(core, s, x, hid, cot, gain, gh, ghb, sums):
    @pl.when(pl.program_id(0) == 0)
    def _():
        sums[...] = jnp.zeros_like(sums)

    two = s[...].astype(F32) + x[...].astype(F32)
    hat, root = norm_parts(hid[...])
    g = cot[...].astype(F32) + norm_back(two * gain[...], hat, root)
    gh[...] = g
    ghb[...] = g.astype(BF16)
    sums[0:1, :] += col_sum(two * hat)
    sums[1:2, :] += col_sum(two)
    sums[2:3, :] += col_sum(g)


def half_rows(d, n, row0):
    return pl.BlockSpec((BT, d), lambda i, core: (row0 // BT + core[0] * (n // BT) + i, 0))


def norm_two_call(core, s, x, hid, cot, gain, row0, hint=SHORT):
    n, d = hid.shape
    return pl.pallas_call(
        norm_two_kernel,
        grid_spec=pltpu.PrefetchScalarGridSpec(
            num_scalar_prefetch=1,
            grid=(n // BT,),
            in_specs=[rows_at(d)] * 3 + [half_rows(d, n, row0), whole((d,))],
            out_specs=[rows_at(d)] * 2 + [whole((8, d))],
        ),
        out_shape=[SDS((n, d), F32), SDS((n, d), BF16), SDS((8, d), F32)],
        cost_estimate=hint,
        compiler_params=params(16),
        name="norm_two_back",
    )(core, s, x, hid, cot, gain)


def attn_bwd_window(win, sub, nh, starts, q, k, v, g, lse, dq, ak, av):
    base = win * WIN
    start = starts[win]
    qpos = base + sub * QB + lax.broadcasted_iota(jnp.int32, (1, QB), 1)
    limit = jnp.where((qpos >= start) & (qpos < start + PIECE), start + PIECE - 1, qpos)
    kpos = base + lax.broadcasted_iota(jnp.int32, (WIN, 1), 0)
    allow = kpos <= limit
    near = slice(base, base + WIN)
    for h in range(nh):
        cols = slice(h * HD, (h + 1) * HD)
        qh = q[:, cols]
        gh = g[:, cols]
        ls = lse[h : h + 1, :]
        pn = jnp.exp(jnp.where(allow, nt(k[near, cols], qh), -1e30) - ls)
        dpn = nt(v[near, cols], gh)
        centre = col_sum(pn * dpn)
        if win:
            pf = jnp.exp(nt(k[:base, cols], qh) - ls)
            dpf = nt(v[:base, cols], gh)
            centre = centre + col_sum(pf * dpf)
        dsn = (pn * (dpn - centre)).astype(BF16)
        dqh = tn(dsn, k[near, cols])
        ak[near, cols] += nn(dsn, qh)
        av[near, cols] += nn(pn.astype(BF16), gh)
        if win:
            dsf = (pf * (dpf - centre)).astype(BF16)
            dqh = dqh + tn(dsf, k[:base, cols])
            ak[:base, cols] += nn(dsf, qh)
            av[:base, cols] += nn(pf.astype(BF16), gh)
        dq[:, cols] = (dqh.astype(BF16).astype(F32) * SCALE).astype(BF16)


def attn_bwd_kernel(win, group, nh, carried, starts, core, q, k, v, mine, other, w_out, lse, *rest):
    sub = pl.program_id(0)
    per = WIN // QB
    if carried:
        dk0, dv0, rest = rest[0], rest[1], rest[2:]
    dq, dk, dv = rest[:3]
    ak, av, gm = rest[-3:]

    @pl.when(sub == 0)
    def _():
        if carried:
            ak[...] = dk0[...]
            av[...] = dv0[...]
        else:
            ak[...] = jnp.zeros_like(ak)
            av[...] = jnp.zeros_like(av)

    half = len(group) * per // 2
    own = ((win - group[-1]) * per + sub) // half == core[0]

    @pl.when(own)
    def _():
        gm[...] = nt(mine[...], w_out[...]).astype(BF16)

    @pl.when(jnp.logical_not(own))
    def _():
        gm[...] = nt(other[...], w_out[...]).astype(BF16)

    attn_bwd_window(win, sub, nh, starts, q, k, v, gm, lse, dq, ak, av)

    @pl.when(sub == per - 1)
    def _():
        low = win * WIN
        dk[...] = ak[low:, :].astype(BF16)
        dv[...] = av[low:, :].astype(BF16)
        if win:
            rest[3][...] = ak[:low, :]
            rest[4][...] = av[:low, :]


def attn_bwd_call(starts, core, q, k, v, mine, other, w_out, lse, carry, win, group):
    c, d = w_out.shape
    nh = c // HD
    per = WIN // QB
    kv = (win + 1) * WIN
    first = (win - group[-1]) * per
    half = len(group) * per // 2
    carried = carry is not None
    near = pl.BlockSpec((QB, c), lambda i: (i, 0))
    part = pl.BlockSpec((QB, d), lambda i: (lax.rem(first + i, half), 0))
    low = win * WIN
    return pl.pallas_call(
        functools.partial(attn_bwd_kernel, win, group, nh, carried),
        grid=(per,),
        in_specs=[
            SMEM,
            SMEM,
            pl.BlockSpec((QB, c), lambda i: (win * per + i, 0)),
            whole((kv, c)),
            whole((kv, c)),
            part,
            part,
            whole((c, d)),
            pl.BlockSpec((8, QB), lambda i: (0, first + i)),
        ]
        + ([whole((kv, c))] * 2 if carried else []),
        out_specs=[near, whole((WIN, c)), whole((WIN, c))] + ([whole((low, c))] * 2 if win else []),
        out_shape=[SDS((WIN, c), BF16)] * 3 + ([SDS((low, c), F32)] * 2 if win else []),
        scratch_shapes=[pltpu.VMEM((kv, c), F32)] * 2 + [pltpu.VMEM((QB, c), BF16)],
        cost_estimate=LONG,
        compiler_params=params(20),
        name="attn_bwd",
    )(starts, core, q, k, v, mine, other, w_out, lse, *(carry if carried else ()))


def one_kernel(nb, wins, core, *refs):
    i = pl.program_id(0)
    grads = refs[: 3 * wins]
    wq, wk, wv, keep, send, sums = refs[3 * wins :]

    @pl.when(i == 0)
    def _():
        sums[...] = jnp.zeros_like(sums)

    def block(dq, dk, dv, out):
        out[0] = (nn(dq[...], wq[...]) + nn(dk[...], wk[...]) + nn(dv[...], wv[...])).astype(BF16)
        sums[0:1, :] += col_sum(dq[...].astype(F32))
        sums[1:2, :] += col_sum(dv[...].astype(F32))

    per = nb // wins
    win = lax.rem(i + core[0] * (nb // 2), nb) // per
    for w in range(wins):
        for out, here in ((keep, i < nb // 2), (send, i >= nb // 2)):

            @pl.when(here & (win == w))
            def _(w=w, out=out):
                block(*grads[3 * w : 3 * w + 3], out)


def one_call(core, grads, wq, wk, wv):
    c, d = wq.shape
    wins = len(grads)
    per = WIN // BT
    nb = wins * per
    half = nb // 2 * BT

    def window(w):
        at = lambda i, core: lax.rem(i + core[0] * (nb // 2), nb) - w * per
        return pl.BlockSpec((BT, c), lambda i, core: (jnp.clip(at(i, core), 0, per - 1), 0))

    return pl.pallas_call(
        functools.partial(one_kernel, nb, wins),
        grid_spec=pltpu.PrefetchScalarGridSpec(
            num_scalar_prefetch=1,
            grid=(nb,),
            in_specs=[window(w) for w in range(wins) for _ in range(3)] + [whole((c, d))] * 3,
            out_specs=[
                pl.BlockSpec((1, BT, d), lambda i, core: (0, jnp.minimum(i, nb // 2 - 1), 0)),
                pl.BlockSpec((1, BT, d), lambda i, core: (0, jnp.maximum(i - nb // 2, 0), 0)),
                whole((8, c)),
            ],
        ),
        out_shape=[SDS((1, half, d), BF16)] * 2 + [SDS((8, c), F32)],
        cost_estimate=SHORT,
        compiler_params=params(16),
        name="grad_one",
    )(core, *[g for window_grads in grads for g in window_grads], wq, wk, wv)


def attn_grad_kernel(bits, core, n1a, n1b, mxa, mxb, ga0, ga1, gb0, gb1, *refs):
    i = pl.program_id(0)
    c = mxa.shape[1]
    dqa, dka, dva = refs[0:3]
    lowers = (refs[3:6], refs[6:9])
    ka, sa, kb, sb, acc = refs[9:]

    @pl.when(i == 0)
    def _():
        acc[...] = jnp.zeros_like(acc)

    def step(n1, grads, mx, gh):
        n = n1[...]
        for at, g in enumerate(grads):
            acc[at * c : (at + 1) * c, :] += tn(g[...], n)
        acc[3 * c :, :] += tn(mx[...], gh[...])

    for at, gh in enumerate((ga0, ga1)):

        @pl.when(i == at)
        def _(gh=gh):
            step(n1a, (dqa, dka, dva), mxa, gh)

    for at, gh in enumerate((gb0, gb1)):
        for w in range(2):

            @pl.when((i == 2 + at) & (lax.rem(at + core[0], 2) == w))
            def _(gh=gh, w=w):
                step(n1b, lowers[w], mxb, gh)

    @pl.when(i == 3)
    def _():
        rows = acc.shape[0] // 2
        split_store(acc, 0, rows, bits[0], ka, sa)
        split_store(acc, rows, rows, bits[1], kb, sb)


def attn_grad_call(bits, core, n1, mxs, ghs, grads_a, grads_0, grads_1):
    length, d = n1.shape
    c = mxs[0].shape[1]
    na, nb = mxs[0].shape[0] // 2, mxs[1].shape[0] // 2
    fa = lambda w, o=0: pl.BlockSpec((na, w), lambda i, bits, core: (o + lax.rem(jnp.minimum(i, 1) + core[0], 2), 0))
    fb = lambda w: pl.BlockSpec((nb, w), lambda i, bits, core: (lax.rem(jnp.maximum(i - 2, 0) + core[0], 2), 0))
    return pl.pallas_call(
        attn_grad_kernel,
        grid_spec=pltpu.PrefetchScalarGridSpec(
            num_scalar_prefetch=2,
            grid=(4,),
            in_specs=[fa(d, 2 * nb // na), fb(d), fa(c), fb(c)]
            + [whole((na, d))] * 2
            + [whole((nb, d))] * 2
            + [fa(c)] * 3
            + [whole((nb, c))] * 6,
            out_specs=[whole((c, d))] * 4,
            scratch_shapes=[pltpu.VMEM((4 * c, d), F32)],
        ),
        out_shape=[SDS((c, d), BF16)] * 4,
        cost_estimate=LONG,
        compiler_params=params(18),
        name="attn_grad",
    )(bits, core, n1, n1, *mxs, *ghs[0], *ghs[1], *grads_a, *grads_0, *grads_1)


def norm_one_kernel(core, s, x, tok, row, gh, gain, out, sums):
    @pl.when(pl.program_id(0) == 0)
    def _():
        sums[...] = jnp.zeros_like(sums)

    one = s[...].astype(F32) + x[...].astype(F32)
    hat, root = norm_parts(tok[...].astype(F32) + row[...])
    g = gh[...] + norm_back(one * gain[...], hat, root)
    out[...] = g.astype(BF16)
    sums[0:1, :] += col_sum(one * hat)
    sums[1:2, :] += col_sum(one)
    sums[2:3, :] += col_sum(g)


def norm_one_call(core, s, x, tok, row, gh, gain, row0, hint=SHORT):
    n, d = gh.shape
    return pl.pallas_call(
        norm_one_kernel,
        grid_spec=pltpu.PrefetchScalarGridSpec(
            num_scalar_prefetch=1,
            grid=(n // BT,),
            in_specs=[rows_at(d)] * 2 + [half_rows(d, n, row0), whole((1, d)), rows_at(d), whole((d,))],
            out_specs=[rows_at(d), whole((8, d))],
        ),
        out_shape=[SDS((n, d), BF16), SDS((8, d), F32)],
        cost_estimate=hint,
        compiler_params=params(16),
        name="norm_one_back",
    )(core, s, x, tok, row, gh, gain)


def out_kernel(s, x, hid, b_down, out):
    out[...] = (hid[...] + s[...].astype(F32) + x[...].astype(F32) + b_down[...]).astype(BF16)


def out_call(s, x, hid, b_down, hint=SHORT):
    n, d = hid.shape
    return pl.pallas_call(
        out_kernel,
        grid=(n // BT,),
        in_specs=[rows_at(d)] * 3 + [whole((d,))],
        out_specs=rows_at(d),
        out_shape=SDS((n, d), BF16),
        cost_estimate=hint,
        compiler_params=params(12),
        name="layer_out",
    )(s, x, hid, b_down)


def rows_kernel(core, ao, at, bo, bt, out):
    na, nb = ao.shape[0], bo.shape[0]
    c = core[0]
    for src, base, n, half in ((bo, 0, nb, c), (bt, 0, nb, 1 - c), (ao, 2 * nb, na, c), (at, 2 * nb, na, 1 - c)):
        out[pl.ds(pl.multiple_of(base + half * n, 16), n), :] = src[...]


def rows_call(core, ao, at, bo, bt, hint=SHORT):
    na, d = ao.shape
    nb = bo.shape[0]
    return pl.pallas_call(
        rows_kernel,
        in_specs=[SMEM] + [pl.BlockSpec((na, d))] * 2 + [pl.BlockSpec((nb, d))] * 2,
        out_specs=pl.BlockSpec((2 * (na + nb), d)),
        out_shape=SDS((2 * (na + nb), d), BF16),
        cost_estimate=hint,
        compiler_params=params(12),
        name="in_order",
    )(core, ao, at, bo, bt)


VALUE_AT = 256
STEP_AT = 512


def pack_kernel(scal, s2a, s2b, s1a, s1b, soa, sob, ffn, out):
    me, step = scal[0], scal[1]
    c = soa.shape[1]
    n = out.shape[0] - 8
    out[0:3, :] = s2a[0:3, :] + s2b[0:3, :]
    out[3:5, :] = s1a[0:2, :] + s1b[0:2, :]
    out[5:7, :] = ffn[0:2, :]
    out[7:8, :] = jnp.zeros((1, out.shape[1]), F32)
    so = soa[...] + sob[...]
    out[7:8, 0:c] = so[0:1, :]
    out[7:8, VALUE_AT : VALUE_AT + c] = so[1:2, :]
    lane = lax.broadcasted_iota(jnp.int32, (1, out.shape[1] - STEP_AT), 1)
    out[7:8, STEP_AT:] = jnp.where(lane == me, step.astype(F32), 0.0)
    spot = lax.broadcasted_iota(jnp.int32, (n, 1), 0) == me
    out[8:, :] = jnp.where(spot, s1a[2:3, :] + s1b[2:3, :], 0.0)


def pack_call(scal, n_dp, s2a, s2b, s1a, s1b, soa, sob, ffn, hint=SHORT):
    d = ffn.shape[1]
    rows = 8 + -(-n_dp // 8) * 8
    return pl.pallas_call(
        pack_kernel,
        in_specs=[SMEM] + [pl.BlockSpec(v.shape) for v in (s2a, s2b, s1a, s1b, soa, sob, ffn)],
        out_specs=pl.BlockSpec((rows, d)),
        out_shape=SDS((rows, d), F32),
        cost_estimate=hint,
        compiler_params=params(4),
        name="pack",
    )(scal, s2a, s2b, s1a, s1b, soa, sob, ffn)


def small_add_kernel(own_rows, a, b, out):
    out[...] = a[...] + b[...]
    if own_rows:
        out[5:8, :] = a[5:8, :]


def small_add(a, b, own_rows=False):
    return pl.pallas_call(
        functools.partial(small_add_kernel, own_rows),
        in_specs=[pl.BlockSpec(a.shape)] * 2,
        out_specs=pl.BlockSpec(a.shape),
        out_shape=SDS(a.shape, F32),
        cost_estimate=SHORT,
        compiler_params=params(4),
        name="small_add",
    )(a, b)


def unpack_kernel(n_dp, small, got, *outs):
    table, vecs, bq, bv, full = outs[0], outs[1:8], outs[8], outs[9], outs[10]
    full[...] = small[...] + got[...]
    for n, vec in enumerate(vecs):
        vec[...] = full[n, :]
    c = bq.shape[0]
    bq[...] = full[7, 0:c]
    bv[...] = full[7, VALUE_AT : VALUE_AT + c]
    table[...] = jnp.zeros_like(table)
    steps = full[7:8, STEP_AT:]
    lane = lax.broadcasted_iota(jnp.int32, steps.shape, 1)
    for n in range(n_dp):
        at = jnp.sum(jnp.where(lane == n, steps, 0.0)).astype(jnp.int32)
        table[pl.ds(at, 1), :] += full[8 + n : 9 + n, :]


def unpack_call(n_dp, table_rows, c, small, got):
    rows, d = small.shape
    shapes = [(table_rows, d)] + [(d,)] * 7 + [(c,)] * 2
    return pl.pallas_call(
        functools.partial(unpack_kernel, n_dp),
        in_specs=[pl.BlockSpec(small.shape)] * 2,
        out_specs=[pl.BlockSpec(s) for s in shapes],
        out_shape=[SDS(s, F32) for s in shapes],
        scratch_shapes=[pltpu.VMEM(small.shape, F32)],
        cost_estimate=SHORT,
        compiler_params=params(10),
        name="unpack",
    )(small, got)


def after(token, value):
    return lax.optimization_barrier((token, value))[1]


class Spread:
    def __init__(self, n_dp, bits, orders):
        self.n_dp, self.bits, self.orders = n_dp, bits, orders

    def swap(self, level, a, b):
        pair = lambda order: [(i, i ^ (1 << order[level])) for i in range(self.n_dp)]
        return lax.ppermute(a, "dp", pair(self.orders[0])), lax.ppermute(b, "dp", pair(self.orders[1]))

    def start(self, ka, sa, kb, sb):
        self.keep = (ka, kb)
        self.got = self.swap(0, sa, sb)

    def halve(self, token):
        ka, sa, kb, sb = halve_call(self.bits, after(token, self.keep[0]), self.got[0], self.keep[1], self.got[1])
        self.keep = (ka, kb)
        self.got = self.swap(1, sa, sb)
        self.level = 2
        return ka

    def exchange(self, token, hint=SHORT):
        self.keep = add_call(after(token, self.keep[0]), self.got[0], self.keep[1], self.got[1], hint)
        level = self.level if self.level < len(self.orders[0]) else 1
        self.level += 1
        self.got = self.swap(level, *self.keep)
        return self.keep[0]

    def join(self, token, hint=SHORT):
        self.keep = join_call(after(token, self.keep[0]), self.got[0], self.keep[1], self.got[1], hint)
        self.got = self.swap(0, *self.keep)
        return self.keep[0]

    def place(self, token, pieces, hint=SHORT):
        return place_call(self.bits, after(token, self.keep[0]), self.got[0], self.keep[1], self.got[1], pieces, hint)


def per_device(
    n_tensor,
    n_dp,
    tokens,
    timesteps,
    piece_starts,
    step_table,
    first_gain,
    first_shift,
    w_query,
    b_query,
    w_key,
    w_value,
    b_value,
    w_out,
    b_out,
    second_gain,
    second_shift,
    w_in,
    b_in,
    w_down,
    b_down,
    cotangent,
):
    length, d = tokens.shape[1:]
    c = w_query.shape[1]
    rank = lax.axis_index("tensor").astype(jnp.int32)
    me = lax.axis_index("dp").astype(jnp.int32)
    over_x = [(i, i ^ 2) for i in range(n_tensor)]
    over_core = [(i, i ^ 1) for i in range(n_tensor)]
    swap_x = lambda v: lax.ppermute(v, "tensor", over_x)
    swap_core = lambda v: lax.ppermute(v, "tensor", over_core)
    n_bits = n_dp.bit_length() - 1
    orders = (list(range(n_bits)), list(range(1, n_bits)) + [0])
    bit = lambda b: (me >> b) & 1
    bits = jnp.stack([bit(orders[0][0]), bit(orders[1][0]), bit(orders[0][1]), bit(orders[1][1])])
    scal = jnp.stack([me, timesteps[0]])
    core = (rank & 1)[None]
    tok, bits, scal, core, starts = lax.optimization_barrier((tokens[0], bits, scal, core, piece_starts[0]))
    cot = cotangent[0]
    wq, wk, wv = w_query.T, w_key.T, w_value.T

    top = length // WIN - 1
    groups = [[top], list(range(top - 1, -1, -1))]
    row0s = [top * WIN, 0]
    hbm = lambda v: pltpu.with_memory_space_constraint(v, pltpu.HBM)

    n1, q, k, v, row = qkv_call(
        timesteps, *[hbm(z) for z in (tok, step_table, first_gain, first_shift, wq, wk, wv, b_query, b_value)]
    )
    wo0 = w_out
    wo2 = swap_x(after(n1, w_out))
    mix_a, lse_a = attn_fwd_call(starts, q, k, v, groups[0])
    wo1 = swap_core(after(mix_a, w_out))
    wo3 = swap_core(after(mix_a, wo2))
    wos = [wo0, wo1, wo2, wo3]
    m1_a, m2_a = swap_core(mix_a), swap_x(mix_a)
    mix_b, lse_b = attn_fwd_call(starts, after(mix_a, q), k, v, groups[1])
    m3_a = swap_core(after(mix_b, m2_a))
    m1_b, m2_b = swap_core(mix_b), swap_x(mix_b)

    def ffn_of(ms, n):
        return ffn_call(
            core, ms, tok, row, cot, wos, b_out, second_gain, second_shift, w_in, b_in, w_down, row0s[n]
        )

    hid_a, n2_a, act_a, gpre_a, keep_a, send_a = ffn_of([mix_a, m1_a, m2_a, m3_a], 0)
    got_a = swap_core(send_a)
    m3_b = swap_core(after(n2_a, m2_b))
    hid_b, n2_b, act_b, gpre_b, keep_b, send_b = ffn_of([after(n2_a, mix_b), m1_b, m2_b, m3_b], 1)
    got_b = swap_core(send_b)
    two_a = half_sum(after(n2_b, keep_a), got_a, 0)
    twox_a = swap_x(two_a)
    ka, sa, kb, sb, ffn_sums = ffn_grad_call(bits, after(two_a, n2_a), n2_b, gpre_a, gpre_b, act_a, act_b, cot)
    gff = Spread(n_dp, bits, orders)
    gff.start(ka, sa, kb, sb)
    two_b = half_sum(after(ka, keep_b), got_b, 0)
    twox_b = swap_x(two_b)
    gh_a, ghb_a, s2_a = norm_two_call(core, after(two_b, two_a), twox_a, hid_a, cot, second_gain, row0s[0])
    gho_a = swap_core(ghb_a)
    mlp_a = half_sum(after(ghb_a, keep_a), got_a, 1, LONG)
    mlp_b = half_sum(after(mlp_a, keep_b), got_b, 1)
    *grads_a, dkf, dvf = attn_bwd_call(
        starts, core, after(mlp_b, q), k, v, ghb_a, gho_a, w_out, lse_a, None, top, groups[0]
    )
    t = gff.halve(grads_a[0])
    one_a, osend_a, so_a = one_call(core, [(after(t, grads_a[0]), *grads_a[1:])], wq, wk, wv)
    ogot_a = swap_core(osend_a)
    gh_b, ghb_b, s2_b = norm_two_call(core, after(one_a, two_b), twox_b, hid_b, cot, second_gain, row0s[1], LONG)
    gho_b = swap_core(ghb_b)
    os_a = half_sum(after(ghb_b, one_a), ogot_a, 0, LONG)
    ox_a = swap_x(os_a)
    *grads_1, dkf, dvf = attn_bwd_call(
        starts, core, after(os_a, q), k, v, ghb_b, gho_b, w_out, lse_b, (dkf, dvf), 1, groups[1]
    )
    t = gff.exchange(grads_1[0])
    gt_a, s1_a = norm_one_call(core, after(t, os_a), ox_a, tok, row, gh_a, first_gain, row0s[0])
    mlpx_b = swap_x(after(gt_a, mlp_b))
    grads_0 = attn_bwd_call(
        starts, core, after(gt_a, q), k, v, ghb_b, gho_b, w_out, lse_b, (dkf, dvf), 0, groups[1]
    )
    one_b, osend_b, so_b = one_call(core, [grads_0, grads_1], wq, wk, wv)
    ogot_b = swap_core(osend_b)
    t = one_b
    for _ in range(n_bits - 2):
        t = gff.exchange(t, LONG)
    os_b = half_sum(after(t, one_b), ogot_b, 0)
    ox_b = swap_x(os_b)
    ka, sa, kb, sb = attn_grad_call(
        bits, core, after(os_b, n1), (mix_a, mix_b), ((ghb_a, gho_a), (ghb_b, gho_b)), grads_a, grads_0, grads_1
    )
    gat = Spread(n_dp, bits, orders)
    gat.start(ka, sa, kb, sb)
    o_b = out_call(after(ka, mlp_b), mlpx_b, hid_b, b_down)
    t = gff.join(o_b, LONG)
    t = gat.halve(t)
    t = gat.exchange(t)
    gt_b, s1_b = norm_one_call(core, after(t, os_b), ox_b, tok, row, gh_b, first_gain, row0s[1], LONG)
    small = pack_call(after(gt_b, scal), n_dp, s2_a, s2_b, s1_a, s1_b, so_a, so_b, ffn_sums)
    swapped = swap_core(small)
    t = small
    for _ in range(n_bits - 2):
        t = gat.exchange(t)
    g_in, g_down = gff.place(t, 2, LONG)
    mlpx_a = swap_x(after(g_in, mlp_a))
    small = small_add(after(g_in, small), swapped, True)
    swap_dp = lambda v, b: lax.ppermute(v, "dp", [(i, i ^ (1 << b)) for i in range(n_dp)])
    for b in range(n_bits - 2):
        small = small_add(small, swap_dp(small, b))
    got = swap_dp(small, n_bits - 2)
    t = gat.join(small, LONG)
    gto_a, gto_b = swap_core(after(t, gt_a)), swap_core(after(t, gt_b))
    small = small_add(after(t, small), got)
    got = swap_dp(small, n_bits - 1)
    grad_tokens = rows_call(core, after(small, gt_a), gto_a, gt_b, gto_b, LONG)
    o_a = out_call(after(grad_tokens, mlp_a), mlpx_a, hid_a, b_down)
    oo_a, oo_b = swap_core(o_a), swap_core(after(o_a, o_b))
    g_table, g_sg, g_ss, g_bo, g_fg, g_fs, g_bi, g_bd, g_bq, g_bv = unpack_call(
        n_dp, step_table.shape[0], c, after(o_a, small), got
    )
    output = rows_call(core, after(g_sg, o_a), oo_a, o_b, oo_b)
    g_q, g_k, g_v, g_o = gat.place(output, 4)
    return (
        output[None],
        grad_tokens[None],
        g_table,
        g_fg,
        g_fs,
        g_q.T,
        g_bq,
        g_k.T,
        g_v.T,
        g_bv,
        g_o,
        g_bo,
        g_sg,
        g_ss,
        g_in,
        g_bi,
        g_down,
        g_bd,
    )


def solution(mesh):
    in_specs = (
        P("dp", None, None),
        P("dp"),
        P("dp", None),
        P(),
        P(),
        P(),
        P(None, "tensor"),
        P("tensor"),
        P(None, "tensor"),
        P(None, "tensor"),
        P("tensor"),
        P("tensor", None),
        P(),
        P(),
        P(),
        P(None, "tensor"),
        P("tensor"),
        P("tensor", None),
        P(),
        P("dp", None, None),
    )
    out_specs = (
        P("dp", None, None),
        P("dp", None, None),
        P(),
        P(),
        P(),
        P(None, "tensor"),
        P("tensor"),
        P(None, "tensor"),
        P(None, "tensor"),
        P("tensor"),
        P("tensor", None),
        P(),
        P(),
        P(),
        P(None, "tensor"),
        P("tensor"),
        P("tensor", None),
        P(),
    )
    return jax.shard_map(
        functools.partial(per_device, mesh.shape["tensor"], mesh.shape["dp"]),
        mesh=mesh,
        in_specs=in_specs,
        out_specs=out_specs,
        check_vma=False,
    )
```

```python
import functools

import jax
import jax.numpy as jnp
from jax import lax
from jax.experimental import pallas as pl
from jax.experimental.pallas import tpu as pltpu
from jax.sharding import PartitionSpec as P

HD = 64
PIECE = 256
WIN = 2 * PIECE
EPS = 1e-05
BT = 256
F32 = jnp.float32
BF16 = jnp.bfloat16
SDS = jax.ShapeDtypeStruct
SCALE = HD ** (-0.5)
GELU_C = 0.7978845608028654


def nn(a, b):
    return lax.dot_general(a, b, (((1,), (0,)), ((), ())), preferred_element_type=F32)


def nt(a, b):
    return lax.dot_general(a, b, (((1,), (1,)), ((), ())), preferred_element_type=F32)


def tn(a, b):
    return lax.dot_general(a, b, (((0,), (0,)), ((), ())), preferred_element_type=F32)


def norm_parts(v):
    c = v - jnp.mean(v, axis=-1, keepdims=True)
    root = lax.rsqrt(jnp.mean(c * c, axis=-1, keepdims=True) + EPS)
    return c * root, root


def norm_back(e, hat, root):
    return root * (
        e - jnp.mean(e, axis=-1, keepdims=True) - hat * jnp.mean(e * hat, axis=-1, keepdims=True)
    )


def col_sum(v):
    return jnp.sum(v, axis=0, keepdims=True)


def whole(shape):
    return pl.BlockSpec(shape, lambda i, *_: (0,) * len(shape))


def rows_at(width, offset=0, block=BT):
    return pl.BlockSpec((block, width), lambda i, *_: (offset + i, 0))


LONG = pl.CostEstimate(flops=10**11, bytes_accessed=1000, transcendentals=0)
SHORT = pl.CostEstimate(flops=1000, bytes_accessed=1000, transcendentals=0)
GRAD_HINT = SHORT


def params(mib=12):
    return pltpu.CompilerParams(vmem_limit_bytes=mib * 1024 * 1024)


SMEM = pl.BlockSpec(memory_space=pltpu.SMEM)


def qkv_kernel(steps, tok, table, gain, shift, wq, wk, wv, bq, bv, n1, q, k, v, row):
    rows = table[...].astype(F32)
    at = lax.broadcasted_iota(jnp.int32, rows.shape, 0) == lax.rem(steps[0], 8)
    step_row = col_sum(jnp.where(at, rows, 0.0))
    row[...] = step_row
    hat, _ = norm_parts(tok[...].astype(F32) + step_row)
    n = (hat * gain[...] + shift[...]).astype(BF16)
    n1[...] = n
    q[...] = ((nt(n, wq[...]) + bq[...]) * SCALE).astype(BF16)
    k[...] = nt(n, wk[...]).astype(BF16)
    v[...] = (nt(n, wv[...]) + bv[...]).astype(BF16)


def qkv_call(steps, tok, table, gain, shift, wq, wk, wv, bq, bv):
    length, d = tok.shape
    c = wq.shape[0]
    return pl.pallas_call(
        qkv_kernel,
        grid_spec=pltpu.PrefetchScalarGridSpec(
            num_scalar_prefetch=1,
            grid=(length // WIN,),
            in_specs=[rows_at(d, block=WIN), pl.BlockSpec((8, d), lambda i, steps: (steps[0] // 8, 0))]
            + [whole((d,))] * 2
            + [whole((c, d))] * 3
            + [whole((c,))] * 2,
            out_specs=[rows_at(d, block=WIN)] + [rows_at(c, block=WIN)] * 3 + [whole((1, d))],
        ),
        out_shape=[SDS((length, d), BF16)] + [SDS((length, c), BF16)] * 3 + [SDS((1, d), F32)],
        cost_estimate=LONG,
        compiler_params=params(16),
        name="norm_qkv",
    )(steps, tok, table, gain, shift, wq, wk, wv, bq, bv)


def attn_fwd_window(win, nh, starts, q, k, v, mix, lse):
    base = win * WIN
    start = starts[win]
    qpos = base + lax.broadcasted_iota(jnp.int32, (WIN, 1), 0)
    limit = jnp.where((qpos >= start) & (qpos < start + PIECE), start + PIECE - 1, qpos)
    kpos = base + lax.broadcasted_iota(jnp.int32, (1, WIN), 1)
    allow = kpos <= limit
    for h in range(nh):
        cols = slice(h * HD, (h + 1) * HD)
        qh = q[:, cols]
        near = jnp.where(allow, nt(qh, k[base : base + WIN, cols]), -1e30)
        top = jnp.max(near, axis=-1, keepdims=True)
        if win:
            far = nt(qh, k[:base, cols])
            top = jnp.maximum(top, jnp.max(far, axis=-1, keepdims=True))
        pn = jnp.exp(near - top)
        total = jnp.sum(pn, axis=-1, keepdims=True)
        out = nn(pn.astype(BF16), v[base : base + WIN, cols])
        if win:
            pf = jnp.exp(far - top)
            total = total + jnp.sum(pf, axis=-1, keepdims=True)
            out = out + nn(pf.astype(BF16), v[:base, cols])
        mix[:, cols] = (out / total).astype(BF16)
        stat = jnp.broadcast_to(top + jnp.log(total), (WIN, 128))
        lse[h : h + 1, :] = jnp.transpose(stat)[0:1, :]


def attn_fwd_kernel(wins, nh, starts, *refs):
    for n, win in enumerate(wins):

        @pl.when(pl.program_id(0) == n)
        def _(win=win):
            attn_fwd_window(win, nh, starts, *refs)


def attn_fwd_call(starts, q, k, v, wins):
    c = q.shape[1]
    kv = (wins[0] + 1) * WIN
    n = len(wins) * WIN
    return pl.pallas_call(
        functools.partial(attn_fwd_kernel, wins, c // HD),
        grid=(len(wins),),
        in_specs=[SMEM, pl.BlockSpec((WIN, c), lambda i: (wins[0] - i, 0)), whole((kv, c)), whole((kv, c))],
        out_specs=[
            pl.BlockSpec((WIN, c), lambda i: (wins[0] - wins[-1] - i, 0)),
            pl.BlockSpec((8, WIN), lambda i: (0, wins[0] - wins[-1] - i)),
        ],
        out_shape=[SDS((n, c), BF16), SDS((8, n), F32)],
        cost_estimate=LONG,
        compiler_params=params(20),
        name="attn_fwd",
    )(starts, q, k, v)


def stack_kernel(a, b, out):
    c = a.shape[1]
    out[:, :c] = a[...]
    out[:, c:] = b[...]


def stack_call(a, b):
    n, c = a.shape
    return pl.pallas_call(
        stack_kernel,
        in_specs=[pl.BlockSpec((n, c))] * 2,
        out_specs=pl.BlockSpec((n, 2 * c)),
        out_shape=SDS((n, 2 * c), BF16),
        cost_estimate=LONG,
        compiler_params=params(6),
        name="stack",
    )(a, b)


def ffn_kernel(
    pieces, core, *refs
):
    kept, sent, wos = refs[:pieces], refs[pieces : 2 * pieces], refs[2 * pieces + 5 : 2 * pieces + 9]
    tok_k, tok_s, row, cot_k, cot_s = refs[2 * pieces : 2 * pieces + 5]
    b_out, gain, shift, w_in, b_in, w_down, hid, n2, act, gpre, keep, send = refs[2 * pieces + 9 :]
    rows = tok_k.shape[0]
    both = lambda a, b: jnp.concatenate([a[...], b[...]], axis=0)
    mixed = jnp.concatenate([both(a, b) for a, b in zip(kept, sent)], axis=1)
    attn = nn(mixed, jnp.concatenate([w[...] for w in wos], axis=0))
    h = both(tok_k, tok_s).astype(F32) + row[...] + attn + b_out[...]
    hid[...] = h[:rows]
    hat, _ = norm_parts(h)
    n = (hat * gain[...] + shift[...]).astype(BF16)
    z = nn(n, w_in[...]) + b_in[...]
    z2 = z * z
    th = jnp.tanh(z * (GELU_C + (GELU_C * 0.044715) * z2))
    half = 0.5 * (1.0 + th)
    a = (z * half).astype(BF16)
    slope = half + (0.5 * z) * (1.0 - th * th) * (GELU_C + (3.0 * 0.044715 * GELU_C) * z2)
    gp = (nt(both(cot_k, cot_s), w_down[...]) * slope).astype(BF16)
    mlp = nn(a, w_down[...]).astype(BF16)
    two = nt(gp, w_in[...]).astype(BF16)
    for part, at in enumerate((slice(0, rows), slice(rows, 2 * rows))):
        n2[part] = n[at]
        act[part] = a[at]
        gpre[part] = gp[at]
        out = send if part else keep
        out[0] = two[at]
        out[1] = mlp[at]


def half_spec(width, nb, own, offset=0):
    return pl.BlockSpec((BT, width), lambda i, core: (offset + (core[0] if own else 1 - core[0]) * nb + i, 0))


def stacked(width, block=BT):
    return pl.BlockSpec((2, block, width), lambda i, *_: (0, i, 0))


def ffn_call(core, ms, tok, row, cot, wos, b_out, gain, shift, w_in, b_in, w_down, row0):
    n = ms[0].shape[0]
    c, d = wos[0].shape
    u = w_in.shape[1]
    h = n // 2
    nb = h // BT
    off = row0 // BT
    kept = functools.partial(half_spec, nb=nb, own=True)
    sent = functools.partial(half_spec, nb=nb, own=False)
    return pl.pallas_call(
        functools.partial(ffn_kernel, len(ms)),
        grid_spec=pltpu.PrefetchScalarGridSpec(
            num_scalar_prefetch=1,
            grid=(nb,),
            in_specs=[kept(v.shape[1]) for v in ms]
            + [sent(v.shape[1]) for v in ms]
            + [kept(d, offset=off), sent(d, offset=off), whole((1, d)), kept(d, offset=off), sent(d, offset=off)]
            + [whole((c, d))] * 4
            + [whole((d,))] * 3
            + [whole((d, u)), whole((u,)), whole((u, d))],
            out_specs=[rows_at(d), stacked(d), stacked(u), stacked(u), stacked(d), stacked(d)],
        ),
        out_shape=[SDS((h, d), F32), SDS((2, h, d), BF16)]
        + [SDS((2, h, u), BF16)] * 2
        + [SDS((2, h, d), BF16)] * 2,
        cost_estimate=LONG,
        compiler_params=params(24),
        name="ffn",
    )(core, *ms, *ms, tok, tok, row, cot, cot, *wos, b_out, gain, shift, w_in, b_in, w_down)


def split_store(acc, first, rows, bit, keep, send):
    half = rows // 2
    keep[...] = acc[pl.ds(pl.multiple_of(first + bit * half, 16), half), :].astype(BF16)
    send[...] = acc[pl.ds(pl.multiple_of(first + (1 - bit) * half, 16), half), :].astype(BF16)


def halve_kernel(parts, bits, *refs):
    ins, outs, acc = refs[: 2 * parts], refs[2 * parts : 4 * parts], refs[4 * parts]
    for part in range(parts):
        acc[...] = ins[2 * part][...].astype(F32) + ins[2 * part + 1][...].astype(F32)
        split_store(acc, 0, acc.shape[0], bits[2 + part], outs[2 * part], outs[2 * part + 1])


def add_kernel(parts, *refs):
    for part in range(parts):
        k, r = refs[2 * part : 2 * part + 2]
        refs[2 * parts + part][...] = (k[...].astype(F32) + r[...].astype(F32)).astype(BF16)


def join_kernel(parts, *refs):
    for part in range(parts):
        s, r = refs[2 * part : 2 * part + 2]
        n = s.shape[0]
        refs[2 * parts + part][:n, :] = s[...]
        refs[2 * parts + part][n:, :] = r[...]


def place_kernel(parts, bits, *refs):
    outs = refs[2 * parts :]
    per = len(outs) // parts
    for part in range(parts):
        p, r = refs[2 * part : 2 * part + 2]
        n = p.shape[0] // 2
        b0, b1 = bits[part], bits[2 + part]
        for src, first in ((p, b0), (r, 1 - b0)):
            for which in range(2):

                @pl.when(first == which)
                def _(src=src, which=which):
                    out = outs[part if per == 1 else 2 * part + which]
                    for sub, second in ((0, b1), (1, 1 - b1)):
                        at = pl.multiple_of(second * n, 8) + (2 * n * which if per == 1 else 0)
                        out[pl.ds(at, n), :] = src[sub * n : (sub + 1) * n, :].astype(F32)


def step_call(kernel, name, bits, arrays, shapes, hint, scratch=()):
    parts = len(arrays) // 2
    return pl.pallas_call(
        functools.partial(kernel, parts),
        in_specs=([] if bits is None else [SMEM]) + [pl.BlockSpec(a.shape) for a in arrays],
        out_specs=[pl.BlockSpec(s.shape) for s in shapes],
        out_shape=shapes,
        scratch_shapes=scratch,
        cost_estimate=hint,
        compiler_params=params(14),
        name=name,
    )(*([] if bits is None else [bits]), *arrays)


def half_sum_kernel(keep, got, out):
    out[...] = (keep[0].astype(F32) + got[0].astype(F32)).astype(BF16)


def half_sum(keep, got, which, hint=SHORT):
    _, n, d = keep.shape
    part = pl.BlockSpec((1, n, d), lambda i: (which, 0, 0))
    return pl.pallas_call(
        half_sum_kernel,
        grid=(1,),
        in_specs=[part, part],
        out_specs=whole((n, d)),
        out_shape=SDS((n, d), BF16),
        cost_estimate=hint,
        compiler_params=params(8),
        name="half_sum",
    )(keep, got)


def ffn_grad_kernel(bits, core, n2a, n2b, gpa, gpb, aca, acb, cot_k, cot_s, ka, sa, kb, sb, sums, acc_in, acc_down):
    i = pl.program_id(0)

    @pl.when(i == 0)
    def _():
        acc_in[...] = jnp.zeros_like(acc_in)
        acc_down[...] = jnp.zeros_like(acc_down)
        sums[...] = jnp.zeros_like(sums)

    def step(n2, gp, ac):
        flat = lambda ref: ref[...].reshape(2 * ref.shape[1], ref.shape[2])
        cot = jnp.concatenate([cot_k[...], cot_s[...]], axis=0)
        g = flat(gp)
        acc_in[...] += tn(flat(n2), g)
        acc_down[...] += tn(flat(ac), cot)
        sums[0:1, :] += col_sum(g.astype(F32))
        sums[1:2, :] += col_sum(cot.astype(F32))

    @pl.when(i == 0)
    def _():
        step(n2a, gpa, aca)

    @pl.when(i > 0)
    def _():
        step(n2b, gpb, acb)

    @pl.when(i == pl.num_programs(0) - 1)
    def _():
        split_store(acc_in, 0, acc_in.shape[0], bits[0], ka, sa)
        split_store(acc_down, 0, acc_down.shape[0], bits[1], kb, sb)


def ffn_grad_call(bits, core, n2a, n2b, gpa, gpb, aca, acb, cot):
    length, d = cot.shape
    u = gpa.shape[2]
    ha, hb = n2a.shape[1], n2b.shape[1]
    nb = hb // ha
    fa = lambda w: pl.BlockSpec((2, ha, w), lambda i, *_: (0, 0, 0))
    fb = lambda w: pl.BlockSpec((2, ha, w), lambda i, *_: (0, jnp.maximum(i - 1, 0), 0))

    def cot_spec(own):
        def at(i, bits, core):
            c = core[0] if own else 1 - core[0]
            return (jnp.where(i == 0, 2 * nb + c, c * nb + i - 1), 0)

        return pl.BlockSpec((ha, d), at)

    return pl.pallas_call(
        ffn_grad_kernel,
        grid_spec=pltpu.PrefetchScalarGridSpec(
            num_scalar_prefetch=2,
            grid=(1 + nb,),
            in_specs=[fa(d), fb(d), fa(u), fb(u), fa(u), fb(u), cot_spec(True), cot_spec(False)],
            out_specs=[whole((d // 2, u))] * 2 + [whole((u // 2, d))] * 2 + [whole((8, d))],
            scratch_shapes=[pltpu.VMEM((d, u), F32), pltpu.VMEM((u, d), F32)],
        ),
        out_shape=[SDS((d // 2, u), BF16)] * 2 + [SDS((u // 2, d), BF16)] * 2 + [SDS((8, d), F32)],
        cost_estimate=LONG,
        compiler_params=params(22),
        name="ffn_grad",
    )(bits, core, n2a, n2b, gpa, gpb, aca, acb, cot, cot)


def norm_two_kernel(core, s, x, hid, cot, gain, gh, ghb, sums):
    @pl.when(pl.program_id(0) == 0)
    def _():
        sums[...] = jnp.zeros_like(sums)

    two = s[...].astype(F32) + x[...].astype(F32)
    hat, root = norm_parts(hid[...])
    g = cot[...].astype(F32) + norm_back(two * gain[...], hat, root)
    gh[...] = g
    ghb[...] = g.astype(BF16)
    sums[0:1, :] += col_sum(two * hat)
    sums[1:2, :] += col_sum(two)
    sums[2:3, :] += col_sum(g)


def half_rows(d, n, row0):
    return pl.BlockSpec((BT, d), lambda i, core: (row0 // BT + core[0] * (n // BT) + i, 0))


def norm_two_call(core, s, x, hid, cot, gain, row0, hint=SHORT):
    n, d = hid.shape
    return pl.pallas_call(
        norm_two_kernel,
        grid_spec=pltpu.PrefetchScalarGridSpec(
            num_scalar_prefetch=1,
            grid=(n // BT,),
            in_specs=[rows_at(d)] * 3 + [half_rows(d, n, row0), whole((d,))],
            out_specs=[rows_at(d)] * 2 + [whole((8, d))],
        ),
        out_shape=[SDS((n, d), F32), SDS((n, d), BF16), SDS((8, d), F32)],
        cost_estimate=hint,
        compiler_params=params(16),
        name="norm_two_back",
    )(core, s, x, hid, cot, gain)


def attn_bwd_kernel(win, low, wins, nh, carried, starts, core, q, k, v, mine, other, w_out, lse, *rest):
    if carried:
        dk0, dv0, rest = rest[0], rest[1], rest[2:]
    dq, dk, dv = rest[:3]
    gm = rest[-1]
    base = win * WIN
    near = slice(base, base + WIN)
    grad = lambda ref: nt(ref[...], w_out[...]).astype(BF16)
    if wins == 1:
        half = WIN // 2
        gm[pl.ds(pl.multiple_of(core[0] * half, half), half), :] = grad(mine)
        gm[pl.ds(pl.multiple_of((1 - core[0]) * half, half), half), :] = grad(other)
    else:

        @pl.when(core[0] == win - low)
        def _():
            gm[...] = grad(mine)

        @pl.when(core[0] != win - low)
        def _():
            gm[...] = grad(other)

    start = starts[win]
    qpos = base + lax.broadcasted_iota(jnp.int32, (1, WIN), 1)
    limit = jnp.where((qpos >= start) & (qpos < start + PIECE), start + PIECE - 1, qpos)
    kpos = base + lax.broadcasted_iota(jnp.int32, (WIN, 1), 0)
    allow = kpos <= limit
    for h in range(nh):
        cols = slice(h * HD, (h + 1) * HD)
        qh = q[near, cols]
        gh = gm[:, cols]
        ls = lse[h : h + 1, (win - low) * WIN : (win - low + 1) * WIN]
        pn = jnp.exp(jnp.where(allow, nt(k[near, cols], qh), -1e30) - ls)
        dpn = nt(v[near, cols], gh)
        centre = col_sum(pn * dpn)
        if win:
            pf = jnp.exp(nt(k[:base, cols], qh) - ls)
            dpf = nt(v[:base, cols], gh)
            centre = centre + col_sum(pf * dpf)
        dsn = (pn * (dpn - centre)).astype(BF16)
        dqh = tn(dsn, k[near, cols])
        dkn = nn(dsn, qh)
        dvn = nn(pn.astype(BF16), gh)
        if carried:
            dkn = dkn + dk0[near, cols]
            dvn = dvn + dv0[near, cols]
        dk[:, cols] = dkn.astype(BF16)
        dv[:, cols] = dvn.astype(BF16)
        if win:
            dsf = (pf * (dpf - centre)).astype(BF16)
            dqh = dqh + tn(dsf, k[:base, cols])
            dkf = nn(dsf, qh)
            dvf = nn(pf.astype(BF16), gh)
            if carried:
                dkf = dkf + dk0[:base, cols]
                dvf = dvf + dv0[:base, cols]
            rest[3][:, cols] = dkf
            rest[4][:, cols] = dvf
        dq[:, cols] = (dqh.astype(BF16).astype(F32) * SCALE).astype(BF16)


def attn_bwd_call(starts, core, q, k, v, mine, other, w_out, lse, carry, win, group):
    c, d = w_out.shape
    carried = carry is not None
    kv = (win + 1) * WIN
    full = lambda a: pl.BlockSpec(a.shape, lambda *_: (0,) * a.ndim)
    first = pl.BlockSpec((kv, c), lambda *_: (0, 0))
    shapes = [SDS((WIN, c), BF16)] * 3 + ([SDS((win * WIN, c), F32)] * 2 if win else [])
    return pl.pallas_call(
        functools.partial(attn_bwd_kernel, win, group[-1], len(group), c // HD, carried),
        grid=(1,),
        in_specs=[SMEM, SMEM, first, first, first, full(mine), full(other), full(w_out), full(lse)]
        + ([first] * 2 if carried else []),
        out_specs=[full(s) for s in shapes],
        out_shape=shapes,
        scratch_shapes=[pltpu.VMEM((WIN, c), BF16)],
        cost_estimate=LONG,
        compiler_params=params(24),
        name="attn_bwd",
    )(starts, core, q, k, v, mine, other, w_out, lse, *(carry if carried else ()))


def one_kernel(wins, core, *refs):
    c = core[0]
    wq, wk, wv, keep, send, sums, buf = refs[3 * wins :]
    weights = jnp.concatenate([wq[...], wk[...], wv[...]], axis=0)
    for w in range(wins):
        dq, dk, dv = refs[3 * w : 3 * w + 3]
        part = nn(jnp.concatenate([dq[...], dk[...], dv[...]], axis=1), weights).astype(BF16)
        for at, g in enumerate((dq, dv)):
            total = col_sum(g[...].astype(F32))
            sums[at : at + 1, :] = total if w == 0 else sums[at : at + 1, :] + total
        if wins == 1:
            half = keep.shape[1]
            buf[...] = part
            keep[0] = buf[pl.ds(pl.multiple_of(c * half, half), half), :]
            send[0] = buf[pl.ds(pl.multiple_of((1 - c) * half, half), half), :]
        else:

            @pl.when(c == w)
            def _():
                keep[0] = part

            @pl.when(c != w)
            def _():
                send[0] = part


def one_call(core, grads, wq, wk, wv):
    c, d = wq.shape
    wins = len(grads)
    half = wins * WIN // 2
    flat = [g for window_grads in grads for g in window_grads]
    return pl.pallas_call(
        functools.partial(one_kernel, wins),
        in_specs=[SMEM] + [pl.BlockSpec((WIN, c))] * (3 * wins) + [pl.BlockSpec((c, d))] * 3,
        out_specs=[pl.BlockSpec((1, half, d))] * 2 + [pl.BlockSpec((8, c))],
        out_shape=[SDS((1, half, d), BF16)] * 2 + [SDS((8, c), F32)],
        scratch_shapes=[pltpu.VMEM((WIN, d), BF16)],
        cost_estimate=SHORT,
        compiler_params=params(16),
        name="grad_one",
    )(core, *flat, wq, wk, wv)


def attn_grad_kernel(bits, core, n1a, n1b, mxa, mxb, ga0, ga1, gb0, gb1, *refs):
    i = pl.program_id(0)
    c = mxa.shape[1]
    lowers = (refs[3:6], refs[6:9])
    ka, sa, kb, sb, acc = refs[9:]

    @pl.when(i == 0)
    def _():
        acc[...] = jnp.zeros_like(acc)

    def step(n1, grads, mx, gh):
        acc[: 3 * c, :] += tn(jnp.concatenate([g[...] for g in grads], axis=1), n1[...])
        acc[3 * c :, :] += tn(mx[...], gh[...])

    for at, gh in enumerate((ga0, ga1)):

        @pl.when(i == at)
        def _(gh=gh):
            step(n1a, refs[:3], mxa, gh)

    for at, gh in enumerate((gb0, gb1)):
        for w in range(2):

            @pl.when((i == 2 + at) & (lax.rem(at + core[0], 2) == w))
            def _(gh=gh, w=w):
                step(n1b, lowers[w], mxb, gh)

    @pl.when(i == 3)
    def _():
        rows = acc.shape[0] // 2
        split_store(acc, 0, rows, bits[0], ka, sa)
        split_store(acc, rows, rows, bits[1], kb, sb)


def attn_grad_call(bits, core, n1, mxs, ghs, grads_a, grads_0, grads_1):
    d = n1.shape[1]
    c = mxs[0].shape[1]
    na, nb = mxs[0].shape[0] // 2, mxs[1].shape[0] // 2
    fa = lambda w, o=0: pl.BlockSpec((na, w), lambda i, bits, core: (o + lax.rem(jnp.minimum(i, 1) + core[0], 2), 0))
    fb = lambda w: pl.BlockSpec((nb, w), lambda i, bits, core: (lax.rem(jnp.maximum(i - 2, 0) + core[0], 2), 0))
    return pl.pallas_call(
        attn_grad_kernel,
        grid_spec=pltpu.PrefetchScalarGridSpec(
            num_scalar_prefetch=2,
            grid=(4,),
            in_specs=[fa(d, 2 * nb // na), fb(d), fa(c), fb(c)]
            + [whole((na, d))] * 2
            + [whole((nb, d))] * 2
            + [fa(c)] * 3
            + [whole((nb, c))] * 6,
            out_specs=[whole((c, d))] * 4,
            scratch_shapes=[pltpu.VMEM((4 * c, d), F32)],
        ),
        out_shape=[SDS((c, d), BF16)] * 4,
        cost_estimate=GRAD_HINT,
        compiler_params=params(18),
        name="attn_grad",
    )(bits, core, n1, n1, *mxs, *ghs[0], *ghs[1], *grads_a, *grads_0, *grads_1)


def norm_one_kernel(core, s, x, tok, row, gh, gain, out, sums):
    @pl.when(pl.program_id(0) == 0)
    def _():
        sums[...] = jnp.zeros_like(sums)

    one = s[...].astype(F32) + x[...].astype(F32)
    hat, root = norm_parts(tok[...].astype(F32) + row[...])
    g = gh[...] + norm_back(one * gain[...], hat, root)
    out[...] = g.astype(BF16)
    sums[0:1, :] += col_sum(one * hat)
    sums[1:2, :] += col_sum(one)
    sums[2:3, :] += col_sum(g)


def norm_one_call(core, s, x, tok, row, gh, gain, row0, hint=SHORT):
    n, d = gh.shape
    return pl.pallas_call(
        norm_one_kernel,
        grid_spec=pltpu.PrefetchScalarGridSpec(
            num_scalar_prefetch=1,
            grid=(n // BT,),
            in_specs=[rows_at(d)] * 2 + [half_rows(d, n, row0), whole((1, d)), rows_at(d), whole((d,))],
            out_specs=[rows_at(d), whole((8, d))],
        ),
        out_shape=[SDS((n, d), BF16), SDS((8, d), F32)],
        cost_estimate=hint,
        compiler_params=params(16),
        name="norm_one_back",
    )(core, s, x, tok, row, gh, gain)


def out_kernel(s, x, hid, b_down, out):
    out[...] = (hid[...] + s[...].astype(F32) + x[...].astype(F32) + b_down[...]).astype(BF16)


def out_call(s, x, hid, b_down, hint=SHORT):
    n, d = hid.shape
    return pl.pallas_call(
        out_kernel,
        grid=(n // BT,),
        in_specs=[rows_at(d)] * 3 + [whole((d,))],
        out_specs=rows_at(d),
        out_shape=SDS((n, d), BF16),
        cost_estimate=hint,
        compiler_params=params(12),
        name="layer_out",
    )(s, x, hid, b_down)


def rows_kernel(core, ao, at, bo, bt, out):
    na, nb = ao.shape[0], bo.shape[0]
    c = core[0]
    for src, base, n, half in ((bo, 0, nb, c), (bt, 0, nb, 1 - c), (ao, 2 * nb, na, c), (at, 2 * nb, na, 1 - c)):
        out[pl.ds(pl.multiple_of(base + half * n, 16), n), :] = src[...]


def rows_call(core, ao, at, bo, bt, hint=SHORT):
    na, d = ao.shape
    nb = bo.shape[0]
    return pl.pallas_call(
        rows_kernel,
        in_specs=[SMEM] + [pl.BlockSpec((na, d))] * 2 + [pl.BlockSpec((nb, d))] * 2,
        out_specs=pl.BlockSpec((2 * (na + nb), d)),
        out_shape=SDS((2 * (na + nb), d), BF16),
        cost_estimate=hint,
        compiler_params=params(12),
        name="in_order",
    )(core, ao, at, bo, bt)


VALUE_AT = 256
STEP_AT = 512


def pack_kernel(scal, s2a, s2b, s1a, s1b, soa, sob, ffn, out):
    me, step = scal[0], scal[1]
    c = soa.shape[1]
    n = out.shape[0] - 8
    out[0:3, :] = s2a[0:3, :] + s2b[0:3, :]
    out[3:5, :] = s1a[0:2, :] + s1b[0:2, :]
    out[5:7, :] = ffn[0:2, :]
    out[7:8, :] = jnp.zeros((1, out.shape[1]), F32)
    so = soa[...] + sob[...]
    out[7:8, 0:c] = so[0:1, :]
    out[7:8, VALUE_AT : VALUE_AT + c] = so[1:2, :]
    lane = lax.broadcasted_iota(jnp.int32, (1, out.shape[1] - STEP_AT), 1)
    out[7:8, STEP_AT:] = jnp.where(lane == me, step.astype(F32), 0.0)
    spot = lax.broadcasted_iota(jnp.int32, (n, 1), 0) == me
    out[8:, :] = jnp.where(spot, s1a[2:3, :] + s1b[2:3, :], 0.0)


def pack_call(scal, n_dp, s2a, s2b, s1a, s1b, soa, sob, ffn, hint=SHORT):
    d = ffn.shape[1]
    rows = 8 + -(-n_dp // 8) * 8
    return pl.pallas_call(
        pack_kernel,
        in_specs=[SMEM] + [pl.BlockSpec(v.shape) for v in (s2a, s2b, s1a, s1b, soa, sob, ffn)],
        out_specs=pl.BlockSpec((rows, d)),
        out_shape=SDS((rows, d), F32),
        cost_estimate=hint,
        compiler_params=params(4),
        name="pack",
    )(scal, s2a, s2b, s1a, s1b, soa, sob, ffn)


def small_add_kernel(own_rows, a, b, out):
    out[...] = a[...] + b[...]
    if own_rows:
        out[5:8, :] = a[5:8, :]


def small_add(a, b, own_rows=False):
    return pl.pallas_call(
        functools.partial(small_add_kernel, own_rows),
        in_specs=[pl.BlockSpec(a.shape)] * 2,
        out_specs=pl.BlockSpec(a.shape),
        out_shape=SDS(a.shape, F32),
        cost_estimate=SHORT,
        compiler_params=params(4),
        name="small_add",
    )(a, b)


def unpack_kernel(n_dp, small, got, *outs):
    table, vecs, bq, bv, full = outs[0], outs[1:8], outs[8], outs[9], outs[10]
    full[...] = small[...] + got[...]
    for n, vec in enumerate(vecs):
        vec[...] = full[n, :]
    c = bq.shape[0]
    bq[...] = full[7, 0:c]
    bv[...] = full[7, VALUE_AT : VALUE_AT + c]
    table[...] = jnp.zeros_like(table)
    steps = full[7:8, STEP_AT:]
    lane = lax.broadcasted_iota(jnp.int32, steps.shape, 1)
    for n in range(n_dp):
        at = jnp.sum(jnp.where(lane == n, steps, 0.0)).astype(jnp.int32)
        table[pl.ds(at, 1), :] += full[8 + n : 9 + n, :]


def unpack_call(n_dp, table_rows, c, small, got):
    rows, d = small.shape
    shapes = [(table_rows, d)] + [(d,)] * 7 + [(c,)] * 2
    return pl.pallas_call(
        functools.partial(unpack_kernel, n_dp),
        in_specs=[pl.BlockSpec(small.shape)] * 2,
        out_specs=[pl.BlockSpec(s) for s in shapes],
        out_shape=[SDS(s, F32) for s in shapes],
        scratch_shapes=[pltpu.VMEM(small.shape, F32)],
        cost_estimate=SHORT,
        compiler_params=params(10),
        name="unpack",
    )(small, got)


def after(token, value):
    return lax.optimization_barrier((token, value))[1]


class Spread:
    def __init__(self, n_dp, bits, orders, keep, send):
        self.n_dp, self.bits, self.orders, self.level = n_dp, bits, orders, 2
        self.keep = keep
        self.swap(0, send)

    def swap(self, level, values):
        self.got = [
            lax.ppermute(v, "dp", [(i, i ^ (1 << order[level])) for i in range(self.n_dp)])
            for v, order in zip(values, self.orders)
        ]

    def step(self, token, kernel, name, bits, shapes, hint, scratch=()):
        keep = [after(token, self.keep[0]), *self.keep[1:]]
        arrays = [a for pair in zip(keep, self.got) for a in pair]
        return step_call(kernel, name, bits, arrays, shapes, hint, scratch)

    def halve(self, token, hint=SHORT):
        n, d = self.keep[0].shape
        half = [SDS((n // 2, d), BF16)] * (2 * len(self.keep))
        out = self.step(token, halve_kernel, "halve", self.bits, half, hint, [pltpu.VMEM((n, d), F32)])
        self.keep = out[0::2]
        self.swap(1, out[1::2])
        return self.keep[0]

    def exchange(self, token, hint=SHORT):
        same = [SDS(k.shape, BF16) for k in self.keep]
        self.keep = self.step(token, add_kernel, "pair_add", None, same, hint)
        self.swap(self.level if self.level < len(self.orders[0]) else 1, self.keep)
        self.level += 1
        return self.keep[0]

    def join(self, token, hint=SHORT):
        n, d = self.keep[0].shape
        self.keep = self.step(token, join_kernel, "join", None, [SDS((2 * n, d), BF16)] * len(self.keep), hint)
        self.swap(0, self.keep)
        return self.keep[0]

    def place(self, token, pieces, hint=SHORT):
        n, d = self.keep[0].shape
        rows = 2 * n * len(self.keep) // pieces
        return self.step(token, place_kernel, "place", self.bits, [SDS((rows, d), F32)] * pieces, hint)


def per_device(
    n_tensor,
    n_dp,
    tokens,
    timesteps,
    piece_starts,
    step_table,
    first_gain,
    first_shift,
    w_query,
    b_query,
    w_key,
    w_value,
    b_value,
    w_out,
    b_out,
    second_gain,
    second_shift,
    w_in,
    b_in,
    w_down,
    b_down,
    cotangent,
):
    length, d = tokens.shape[1:]
    c = w_query.shape[1]
    rank = lax.axis_index("tensor").astype(jnp.int32)
    me = lax.axis_index("dp").astype(jnp.int32)
    over_x = [(i, i ^ 2) for i in range(n_tensor)]
    over_core = [(i, i ^ 1) for i in range(n_tensor)]
    swap_x = lambda v: lax.ppermute(v, "tensor", over_x)
    swap_core = lambda v: lax.ppermute(v, "tensor", over_core)
    n_bits = n_dp.bit_length() - 1
    orders = (list(range(n_bits)), list(range(1, n_bits)) + [0])
    bit = lambda b: (me >> b) & 1
    bits = jnp.stack([bit(orders[0][0]), bit(orders[1][0]), bit(orders[0][1]), bit(orders[1][1])])
    scal = jnp.stack([me, timesteps[0]])
    core = (rank & 1)[None]
    tok, bits, scal, core, starts = lax.optimization_barrier((tokens[0], bits, scal, core, piece_starts[0]))
    cot = cotangent[0]
    wq, wk, wv = w_query.T, w_key.T, w_value.T

    top = length // WIN - 1
    groups = [[top], list(range(top - 1, -1, -1))]
    row0s = [top * WIN, 0]
    hbm = lambda v: pltpu.with_memory_space_constraint(v, pltpu.HBM)

    n1, q, k, v, row = qkv_call(
        timesteps, *[hbm(z) for z in (tok, step_table, first_gain, first_shift, wq, wk, wv, b_query, b_value)]
    )
    wo0 = w_out
    wo2 = swap_x(after(n1, w_out))
    mix_a, lse_a = attn_fwd_call(starts, q, k, v, groups[0])
    wo1 = swap_core(after(mix_a, w_out))
    wo3 = swap_core(after(mix_a, wo2))
    wos = [wo0, wo2, wo1, wo3]
    m1_a, m2_a = swap_core(mix_a), swap_x(mix_a)
    mix_b, lse_b = attn_fwd_call(starts, after(mix_a, q), k, v, groups[1])
    m3_a = swap_core(after(mix_b, m2_a))
    m2_b = swap_x(mix_b)

    def ffn_of(ms, n):
        return ffn_call(
            core, ms, tok, row, cot, wos, b_out, second_gain, second_shift, w_in, b_in, w_down, row0s[n]
        )

    hid_a, n2_a, act_a, gpre_a, keep_a, send_a = ffn_of([mix_a, m2_a, m1_a, m3_a], 0)
    got_a = swap_core(send_a)
    pair_b = stack_call(after(n2_a, mix_b), m2_b)
    far_b = swap_core(pair_b)
    two_a = half_sum(after(pair_b, keep_a), got_a, 0)
    twox_a = swap_x(two_a)
    mlp_a = half_sum(after(two_a, keep_a), got_a, 1)
    hid_b, n2_b, act_b, gpre_b, keep_b, send_b = ffn_of([after(mlp_a, mix_b), m2_b, far_b], 1)
    got_b = swap_core(send_b)
    gh_a, ghb_a, s2_a = norm_two_call(core, after(n2_b, two_a), twox_a, hid_a, cot, second_gain, row0s[0])
    gho_a = swap_core(ghb_a)
    mlpx_a = swap_x(after(ghb_a, mlp_a))
    ka, sa, kb, sb, ffn_sums = ffn_grad_call(
        bits, core, after(ghb_a, n2_a), n2_b, gpre_a, gpre_b, act_a, act_b, cot
    )
    gff = Spread(n_dp, bits, orders, [ka, kb], [sa, sb])
    two_b = half_sum(after(ka, keep_b), got_b, 0)
    twox_b = swap_x(two_b)
    *grads_a, dkf, dvf = attn_bwd_call(
        starts, core, after((two_b, mlpx_a), q), k, v, ghb_a, gho_a, w_out, lse_a, None, top, groups[0]
    )
    t = gff.halve(grads_a[0])
    one_a, osend_a, so_a = one_call(core, [(after(t, grads_a[0]), *grads_a[1:])], wq, wk, wv)
    ogot_a = swap_core(osend_a)
    gh_b, ghb_b, s2_b = norm_two_call(core, after(one_a, two_b), twox_b, hid_b, cot, second_gain, row0s[1], LONG)
    gho_b = swap_core(ghb_b)
    os_a = half_sum(after(ghb_b, one_a), ogot_a, 0, LONG)
    ox_a = swap_x(os_a)
    mlp_b = half_sum(after(os_a, keep_b), got_b, 1)
    *grads_1, dkf, dvf = attn_bwd_call(
        starts, core, after(mlp_b, q), k, v, ghb_b, gho_b, w_out, lse_b, (dkf, dvf), 1, groups[1]
    )
    t = gff.exchange(grads_1[0])
    gt_a, s1_a = norm_one_call(core, after(t, os_a), ox_a, tok, row, gh_a, first_gain, row0s[0])
    mlpx_b = swap_x(after(gt_a, mlp_b))
    grads_0 = attn_bwd_call(
        starts, core, after(gt_a, q), k, v, ghb_b, gho_b, w_out, lse_b, (dkf, dvf), 0, groups[1]
    )
    one_b, osend_b, so_b = one_call(core, [grads_0, grads_1], wq, wk, wv)
    ogot_b = swap_core(osend_b)
    ka, sa, kb, sb = attn_grad_call(
        bits, core, after(one_b, n1), (mix_a, mix_b), ((ghb_a, gho_a), (ghb_b, gho_b)), grads_a, grads_0, grads_1
    )
    gat = Spread(n_dp, bits, orders, [ka, kb], [sa, sb])
    t = ka
    for _ in range(n_bits - 2):
        t = gff.exchange(t, LONG)
    os_b = half_sum(after(t, one_b), ogot_b, 0)
    ox_b = swap_x(os_b)
    o_b = out_call(after(os_b, mlp_b), mlpx_b, hid_b, b_down)
    o_a = out_call(after(o_b, mlp_a), mlpx_a, hid_a, b_down)
    t = gat.halve(o_a)
    t = gff.join(t)
    t = gat.exchange(t)
    gt_b, s1_b = norm_one_call(core, after(t, os_b), ox_b, tok, row, gh_b, first_gain, row0s[1], LONG)
    small = pack_call(after(gt_b, scal), n_dp, s2_a, s2_b, s1_a, s1_b, so_a, so_b, ffn_sums)
    swapped = swap_core(small)
    t = small
    for _ in range(n_bits - 2):
        t = gat.exchange(t)
    small = small_add(after(t, small), swapped, True)
    swap_dp = lambda v, b: lax.ppermute(v, "dp", [(i, i ^ (1 << b)) for i in range(n_dp)])
    got = swap_dp(small, 0)
    g_in, g_down = gff.place(small, 2, LONG)
    t = gat.join(g_in)
    gto_a, gto_b = swap_core(after(t, gt_a)), swap_core(after(t, gt_b))
    oo_a, oo_b = swap_core(after(t, o_a)), swap_core(after(t, o_b))
    small = after(t, small)
    for b in range(1, n_bits):
        small = small_add(small, got)
        got = swap_dp(small, b)
        if b == 1:
            grad_tokens = rows_call(core, after(small, gt_a), gto_a, gt_b, gto_b, LONG)
            small = after(grad_tokens, small)
    output = rows_call(core, after(small, o_a), oo_a, o_b, oo_b, LONG)
    g_table, g_sg, g_ss, g_bo, g_fg, g_fs, g_bi, g_bd, g_bq, g_bv = unpack_call(
        n_dp, step_table.shape[0], c, after(output, small), got
    )
    g_q, g_k, g_v, g_o = gat.place(g_sg, 4)
    return (
        output[None],
        grad_tokens[None],
        g_table,
        g_fg,
        g_fs,
        g_q.T,
        g_bq,
        g_k.T,
        g_v.T,
        g_bv,
        g_o,
        g_bo,
        g_sg,
        g_ss,
        g_in,
        g_bi,
        g_down,
        g_bd,
    )


def solution(mesh):
    in_specs = (
        P("dp", None, None),
        P("dp"),
        P("dp", None),
        P(),
        P(),
        P(),
        P(None, "tensor"),
        P("tensor"),
        P(None, "tensor"),
        P(None, "tensor"),
        P("tensor"),
        P("tensor", None),
        P(),
        P(),
        P(),
        P(None, "tensor"),
        P("tensor"),
        P("tensor", None),
        P(),
        P("dp", None, None),
    )
    out_specs = (
        P("dp", None, None),
        P("dp", None, None),
        P(),
        P(),
        P(),
        P(None, "tensor"),
        P("tensor"),
        P(None, "tensor"),
        P(None, "tensor"),
        P("tensor"),
        P("tensor", None),
        P(),
        P(),
        P(),
        P(None, "tensor"),
        P("tensor"),
        P("tensor", None),
        P(),
    )
    return jax.shard_map(
        functools.partial(per_device, mesh.shape["tensor"], mesh.shape["dp"]),
        mesh=mesh,
        in_specs=in_specs,
        out_specs=out_specs,
        check_vma=False,
    )
```

```python
import functools

import jax
import jax.numpy as jnp
from jax import lax
from jax.experimental import pallas as pl
from jax.experimental.pallas import tpu as pltpu
from jax.sharding import PartitionSpec as P

HD = 64
PIECE = 256
WIN = 2 * PIECE
EPS = 1e-05
BT = 256
F32 = jnp.float32
BF16 = jnp.bfloat16
SDS = jax.ShapeDtypeStruct
SCALE = HD ** (-0.5)
GELU_C = 0.7978845608028654


def nn(a, b):
    return lax.dot_general(a, b, (((1,), (0,)), ((), ())), preferred_element_type=F32)


def nt(a, b):
    return lax.dot_general(a, b, (((1,), (1,)), ((), ())), preferred_element_type=F32)


def tn(a, b):
    return lax.dot_general(a, b, (((0,), (0,)), ((), ())), preferred_element_type=F32)


def norm_parts(v):
    c = v - jnp.mean(v, axis=-1, keepdims=True)
    root = lax.rsqrt(jnp.mean(c * c, axis=-1, keepdims=True) + EPS)
    return c * root, root


def norm_back(e, hat, root):
    return root * (
        e - jnp.mean(e, axis=-1, keepdims=True) - hat * jnp.mean(e * hat, axis=-1, keepdims=True)
    )


def col_sum(v):
    return jnp.sum(v, axis=0, keepdims=True)


def whole(shape):
    return pl.BlockSpec(shape, lambda i, *_: (0,) * len(shape))


def rows_at(width, offset=0, block=BT):
    return pl.BlockSpec((block, width), lambda i, *_: (offset + i, 0))


LONG = pl.CostEstimate(flops=10**11, bytes_accessed=1000, transcendentals=0)
SHORT = pl.CostEstimate(flops=1000, bytes_accessed=1000, transcendentals=0)
GRAD_HINT = SHORT


def params(mib=12):
    return pltpu.CompilerParams(vmem_limit_bytes=mib * 1024 * 1024)


SMEM = pl.BlockSpec(memory_space=pltpu.SMEM)


def qkv_kernel(steps, tok, table, gain, shift, wq, wk, wv, bq, bv, n1, q, k, v, row):
    rows = table[...].astype(F32)
    at = lax.broadcasted_iota(jnp.int32, rows.shape, 0) == lax.rem(steps[0], 8)
    step_row = col_sum(jnp.where(at, rows, 0.0))
    row[...] = step_row
    hat, _ = norm_parts(tok[...].astype(F32) + step_row)
    n = (hat * gain[...] + shift[...]).astype(BF16)
    n1[...] = n
    q[...] = ((nt(n, wq[...]) + bq[...]) * SCALE).astype(BF16)
    k[...] = nt(n, wk[...]).astype(BF16)
    v[...] = (nt(n, wv[...]) + bv[...]).astype(BF16)


def qkv_call(steps, tok, table, gain, shift, wq, wk, wv, bq, bv):
    length, d = tok.shape
    c = wq.shape[0]
    return pl.pallas_call(
        qkv_kernel,
        grid_spec=pltpu.PrefetchScalarGridSpec(
            num_scalar_prefetch=1,
            grid=(length // WIN,),
            in_specs=[rows_at(d, block=WIN), pl.BlockSpec((8, d), lambda i, steps: (steps[0] // 8, 0))]
            + [whole((d,))] * 2
            + [whole((c, d))] * 3
            + [whole((c,))] * 2,
            out_specs=[rows_at(d, block=WIN)] + [rows_at(c, block=WIN)] * 3 + [whole((1, d))],
        ),
        out_shape=[SDS((length, d), BF16)] + [SDS((length, c), BF16)] * 3 + [SDS((1, d), F32)],
        cost_estimate=LONG,
        compiler_params=params(16),
        name="norm_qkv",
    )(steps, tok, table, gain, shift, wq, wk, wv, bq, bv)


def attn_fwd_window(win, nh, starts, q, k, v, mix, lse):
    base = win * WIN
    start = starts[win]
    qpos = base + lax.broadcasted_iota(jnp.int32, (WIN, 1), 0)
    limit = jnp.where((qpos >= start) & (qpos < start + PIECE), start + PIECE - 1, qpos)
    kpos = base + lax.broadcasted_iota(jnp.int32, (1, WIN), 1)
    allow = kpos <= limit
    for h in range(nh):
        cols = slice(h * HD, (h + 1) * HD)
        qh = q[:, cols]
        near = jnp.where(allow, nt(qh, k[base : base + WIN, cols]), -1e30)
        top = jnp.max(near, axis=-1, keepdims=True)
        if win:
            far = nt(qh, k[:base, cols])
            top = jnp.maximum(top, jnp.max(far, axis=-1, keepdims=True))
        pn = jnp.exp(near - top)
        total = jnp.sum(pn, axis=-1, keepdims=True)
        out = nn(pn.astype(BF16), v[base : base + WIN, cols])
        if win:
            pf = jnp.exp(far - top)
            total = total + jnp.sum(pf, axis=-1, keepdims=True)
            out = out + nn(pf.astype(BF16), v[:base, cols])
        mix[:, cols] = (out / total).astype(BF16)
        stat = jnp.broadcast_to(top + jnp.log(total), (WIN, 128))
        lse[h : h + 1, :] = jnp.transpose(stat)[0:1, :]


def attn_fwd_kernel(wins, nh, starts, *refs):
    for n, win in enumerate(wins):

        @pl.when(pl.program_id(0) == n)
        def _(win=win):
            attn_fwd_window(win, nh, starts, *refs)


def attn_fwd_call(starts, q, k, v, wins):
    c = q.shape[1]
    kv = (wins[0] + 1) * WIN
    n = len(wins) * WIN
    return pl.pallas_call(
        functools.partial(attn_fwd_kernel, wins, c // HD),
        grid=(len(wins),),
        in_specs=[SMEM, pl.BlockSpec((WIN, c), lambda i: (wins[0] - i, 0)), whole((kv, c)), whole((kv, c))],
        out_specs=[
            pl.BlockSpec((WIN, c), lambda i: (wins[0] - wins[-1] - i, 0)),
            pl.BlockSpec((8, WIN), lambda i: (0, wins[0] - wins[-1] - i)),
        ],
        out_shape=[SDS((n, c), BF16), SDS((8, n), F32)],
        cost_estimate=LONG,
        compiler_params=params(20),
        name="attn_fwd",
    )(starts, q, k, v)


def stack_kernel(a, b, out):
    c = a.shape[1]
    out[:, :c] = a[...]
    out[:, c:] = b[...]


def stack_call(a, b):
    n, c = a.shape
    return pl.pallas_call(
        stack_kernel,
        in_specs=[pl.BlockSpec((n, c))] * 2,
        out_specs=pl.BlockSpec((n, 2 * c)),
        out_shape=SDS((n, 2 * c), BF16),
        cost_estimate=LONG,
        compiler_params=params(6),
        name="stack",
    )(a, b)


def ffn_kernel(
    pieces, core, *refs
):
    kept, sent, wos = refs[:pieces], refs[pieces : 2 * pieces], refs[2 * pieces + 5 : 2 * pieces + 9]
    tok_k, tok_s, row, cot_k, cot_s = refs[2 * pieces : 2 * pieces + 5]
    b_out, gain, shift, w_in, b_in, w_down, hid, n2, act, gpre, keep, send = refs[2 * pieces + 9 :]
    rows = tok_k.shape[0]
    both = lambda a, b: jnp.concatenate([a[...], b[...]], axis=0)
    mixed = jnp.concatenate([both(a, b) for a, b in zip(kept, sent)], axis=1)
    attn = nn(mixed, jnp.concatenate([w[...] for w in wos], axis=0))
    h = both(tok_k, tok_s).astype(F32) + row[...] + attn + b_out[...]
    hid[...] = h[:rows]
    hat, _ = norm_parts(h)
    n = (hat * gain[...] + shift[...]).astype(BF16)
    z = nn(n, w_in[...]) + b_in[...]
    z2 = z * z
    th = jnp.tanh(z * (GELU_C + (GELU_C * 0.044715) * z2))
    half = 0.5 * (1.0 + th)
    a = (z * half).astype(BF16)
    slope = half + (0.5 * z) * (1.0 - th * th) * (GELU_C + (3.0 * 0.044715 * GELU_C) * z2)
    gp = (nt(both(cot_k, cot_s), w_down[...]) * slope).astype(BF16)
    mlp = nn(a, w_down[...]).astype(BF16)
    two = nt(gp, w_in[...]).astype(BF16)
    for part, at in enumerate((slice(0, rows), slice(rows, 2 * rows))):
        n2[part] = n[at]
        act[part] = a[at]
        gpre[part] = gp[at]
        out = send if part else keep
        out[0] = two[at]
        out[1] = mlp[at]


def half_spec(width, nb, own, offset=0):
    return pl.BlockSpec((BT, width), lambda i, core: (offset + (core[0] if own else 1 - core[0]) * nb + i, 0))


def stacked(width, block=BT):
    return pl.BlockSpec((2, block, width), lambda i, *_: (0, i, 0))


def ffn_call(core, ms, tok, row, cot, wos, b_out, gain, shift, w_in, b_in, w_down, row0):
    n = ms[0].shape[0]
    c, d = wos[0].shape
    u = w_in.shape[1]
    h = n // 2
    nb = h // BT
    off = row0 // BT
    kept = functools.partial(half_spec, nb=nb, own=True)
    sent = functools.partial(half_spec, nb=nb, own=False)
    return pl.pallas_call(
        functools.partial(ffn_kernel, len(ms)),
        grid_spec=pltpu.PrefetchScalarGridSpec(
            num_scalar_prefetch=1,
            grid=(nb,),
            in_specs=[kept(v.shape[1]) for v in ms]
            + [sent(v.shape[1]) for v in ms]
            + [kept(d, offset=off), sent(d, offset=off), whole((1, d)), kept(d, offset=off), sent(d, offset=off)]
            + [whole((c, d))] * 4
            + [whole((d,))] * 3
            + [whole((d, u)), whole((u,)), whole((u, d))],
            out_specs=[rows_at(d), stacked(d), stacked(u), stacked(u), stacked(d), stacked(d)],
        ),
        out_shape=[SDS((h, d), F32), SDS((2, h, d), BF16)]
        + [SDS((2, h, u), BF16)] * 2
        + [SDS((2, h, d), BF16)] * 2,
        cost_estimate=LONG,
        compiler_params=params(24),
        name="ffn",
    )(core, *ms, *ms, tok, tok, row, cot, cot, *wos, b_out, gain, shift, w_in, b_in, w_down)


def split_store(acc, first, rows, bit, keep, send):
    half = rows // 2
    keep[...] = acc[pl.ds(pl.multiple_of(first + bit * half, 16), half), :].astype(BF16)
    send[...] = acc[pl.ds(pl.multiple_of(first + (1 - bit) * half, 16), half), :].astype(BF16)


def halve_kernel(parts, bits, *refs):
    ins, outs, acc = refs[: 2 * parts], refs[2 * parts : 4 * parts], refs[4 * parts]
    for part in range(parts):
        acc[...] = ins[2 * part][...].astype(F32) + ins[2 * part + 1][...].astype(F32)
        split_store(acc, 0, acc.shape[0], bits[2 + part], outs[2 * part], outs[2 * part + 1])


def add_kernel(parts, *refs):
    for part in range(parts):
        k, r = refs[2 * part : 2 * part + 2]
        refs[2 * parts + part][...] = (k[...].astype(F32) + r[...].astype(F32)).astype(BF16)


def join_kernel(parts, *refs):
    for part in range(parts):
        s, r = refs[2 * part : 2 * part + 2]
        n = s.shape[0]
        refs[2 * parts + part][:n, :] = s[...]
        refs[2 * parts + part][n:, :] = r[...]


def place_kernel(parts, bits, *refs):
    outs = refs[2 * parts :]
    per = len(outs) // parts
    for part in range(parts):
        p, r = refs[2 * part : 2 * part + 2]
        n = p.shape[0] // 2
        b0, b1 = bits[part], bits[2 + part]
        for src, first in ((p, b0), (r, 1 - b0)):
            for which in range(2):

                @pl.when(first == which)
                def _(src=src, which=which):
                    out = outs[part if per == 1 else 2 * part + which]
                    for sub, second in ((0, b1), (1, 1 - b1)):
                        at = pl.multiple_of(second * n, 8) + (2 * n * which if per == 1 else 0)
                        out[pl.ds(at, n), :] = src[sub * n : (sub + 1) * n, :].astype(F32)


def step_call(kernel, name, bits, arrays, shapes, hint, scratch=()):
    parts = len(arrays) // 2
    return pl.pallas_call(
        functools.partial(kernel, parts),
        in_specs=([] if bits is None else [SMEM]) + [pl.BlockSpec(a.shape) for a in arrays],
        out_specs=[pl.BlockSpec(s.shape) for s in shapes],
        out_shape=shapes,
        scratch_shapes=scratch,
        cost_estimate=hint,
        compiler_params=params(14),
        name=name,
    )(*([] if bits is None else [bits]), *arrays)


def half_sum_kernel(keep, got, out):
    out[...] = (keep[0].astype(F32) + got[0].astype(F32)).astype(BF16)


def half_sum(keep, got, which, hint=SHORT):
    _, n, d = keep.shape
    part = pl.BlockSpec((1, n, d), lambda i: (which, 0, 0))
    return pl.pallas_call(
        half_sum_kernel,
        grid=(1,),
        in_specs=[part, part],
        out_specs=whole((n, d)),
        out_shape=SDS((n, d), BF16),
        cost_estimate=hint,
        compiler_params=params(8),
        name="half_sum",
    )(keep, got)


def ffn_grad_kernel(bits, core, n2a, n2b, gpa, gpb, aca, acb, cot_k, cot_s, ka, sa, kb, sb, sums, acc_in, acc_down):
    i = pl.program_id(0)

    @pl.when(i == 0)
    def _():
        acc_in[...] = jnp.zeros_like(acc_in)
        acc_down[...] = jnp.zeros_like(acc_down)
        sums[...] = jnp.zeros_like(sums)

    def step(n2, gp, ac):
        flat = lambda ref: ref[...].reshape(2 * ref.shape[1], ref.shape[2])
        cot = jnp.concatenate([cot_k[...], cot_s[...]], axis=0)
        g = flat(gp)
        acc_in[...] += tn(flat(n2), g)
        acc_down[...] += tn(flat(ac), cot)
        sums[0:1, :] += col_sum(g.astype(F32))
        sums[1:2, :] += col_sum(cot.astype(F32))

    @pl.when(i == 0)
    def _():
        step(n2a, gpa, aca)

    @pl.when(i > 0)
    def _():
        step(n2b, gpb, acb)

    @pl.when(i == pl.num_programs(0) - 1)
    def _():
        split_store(acc_in, 0, acc_in.shape[0], bits[0], ka, sa)
        split_store(acc_down, 0, acc_down.shape[0], bits[1], kb, sb)


def ffn_grad_call(bits, core, n2a, n2b, gpa, gpb, aca, acb, cot):
    length, d = cot.shape
    u = gpa.shape[2]
    ha, hb = n2a.shape[1], n2b.shape[1]
    nb = hb // ha
    fa = lambda w: pl.BlockSpec((2, ha, w), lambda i, *_: (0, 0, 0))
    fb = lambda w: pl.BlockSpec((2, ha, w), lambda i, *_: (0, jnp.maximum(i - 1, 0), 0))

    def cot_spec(own):
        def at(i, bits, core):
            c = core[0] if own else 1 - core[0]
            return (jnp.where(i == 0, 2 * nb + c, c * nb + i - 1), 0)

        return pl.BlockSpec((ha, d), at)

    return pl.pallas_call(
        ffn_grad_kernel,
        grid_spec=pltpu.PrefetchScalarGridSpec(
            num_scalar_prefetch=2,
            grid=(1 + nb,),
            in_specs=[fa(d), fb(d), fa(u), fb(u), fa(u), fb(u), cot_spec(True), cot_spec(False)],
            out_specs=[whole((d // 2, u))] * 2 + [whole((u // 2, d))] * 2 + [whole((8, d))],
            scratch_shapes=[pltpu.VMEM((d, u), F32), pltpu.VMEM((u, d), F32)],
        ),
        out_shape=[SDS((d // 2, u), BF16)] * 2 + [SDS((u // 2, d), BF16)] * 2 + [SDS((8, d), F32)],
        cost_estimate=LONG,
        compiler_params=params(22),
        name="ffn_grad",
    )(bits, core, n2a, n2b, gpa, gpb, aca, acb, cot, cot)


def norm_two_kernel(core, s, x, hid, cot, gain, gh, ghb, sums):
    @pl.when(pl.program_id(0) == 0)
    def _():
        sums[...] = jnp.zeros_like(sums)

    two = s[...].astype(F32) + x[...].astype(F32)
    hat, root = norm_parts(hid[...])
    g = cot[...].astype(F32) + norm_back(two * gain[...], hat, root)
    gh[...] = g
    ghb[...] = g.astype(BF16)
    sums[0:1, :] += col_sum(two * hat)
    sums[1:2, :] += col_sum(two)
    sums[2:3, :] += col_sum(g)


def half_rows(d, n, row0):
    return pl.BlockSpec((BT, d), lambda i, core: (row0 // BT + core[0] * (n // BT) + i, 0))


def norm_two_call(core, s, x, hid, cot, gain, row0, hint=SHORT):
    n, d = hid.shape
    return pl.pallas_call(
        norm_two_kernel,
        grid_spec=pltpu.PrefetchScalarGridSpec(
            num_scalar_prefetch=1,
            grid=(n // BT,),
            in_specs=[rows_at(d)] * 3 + [half_rows(d, n, row0), whole((d,))],
            out_specs=[rows_at(d)] * 2 + [whole((8, d))],
        ),
        out_shape=[SDS((n, d), F32), SDS((n, d), BF16), SDS((8, d), F32)],
        cost_estimate=hint,
        compiler_params=params(16),
        name="norm_two_back",
    )(core, s, x, hid, cot, gain)


def attn_bwd_kernel(win, low, wins, nh, carried, starts, core, q, k, v, mine, other, w_out, lse, *rest):
    if carried:
        dk0, dv0, rest = rest[0], rest[1], rest[2:]
    dq, dk, dv = rest[:3]
    gm = rest[-1]
    base = win * WIN
    near = slice(base, base + WIN)
    grad = lambda ref: nt(ref[...], w_out[...]).astype(BF16)
    if wins == 1:
        half = WIN // 2
        gm[pl.ds(pl.multiple_of(core[0] * half, half), half), :] = grad(mine)
        gm[pl.ds(pl.multiple_of((1 - core[0]) * half, half), half), :] = grad(other)
    else:

        @pl.when(core[0] == win - low)
        def _():
            gm[...] = grad(mine)

        @pl.when(core[0] != win - low)
        def _():
            gm[...] = grad(other)

    start = starts[win]
    qpos = base + lax.broadcasted_iota(jnp.int32, (1, WIN), 1)
    limit = jnp.where((qpos >= start) & (qpos < start + PIECE), start + PIECE - 1, qpos)
    kpos = base + lax.broadcasted_iota(jnp.int32, (WIN, 1), 0)
    allow = kpos <= limit
    for h in range(nh):
        cols = slice(h * HD, (h + 1) * HD)
        qh = q[near, cols]
        gh = gm[:, cols]
        ls = lse[h : h + 1, (win - low) * WIN : (win - low + 1) * WIN]
        pn = jnp.exp(jnp.where(allow, nt(k[near, cols], qh), -1e30) - ls)
        dpn = nt(v[near, cols], gh)
        centre = col_sum(pn * dpn)
        if win:
            pf = jnp.exp(nt(k[:base, cols], qh) - ls)
            dpf = nt(v[:base, cols], gh)
            centre = centre + col_sum(pf * dpf)
        dsn = (pn * (dpn - centre)).astype(BF16)
        dqh = tn(dsn, k[near, cols])
        dkn = nn(dsn, qh)
        dvn = nn(pn.astype(BF16), gh)
        if carried:
            dkn = dkn + dk0[near, cols]
            dvn = dvn + dv0[near, cols]
        dk[:, cols] = dkn.astype(BF16)
        dv[:, cols] = dvn.astype(BF16)
        if win:
            dsf = (pf * (dpf - centre)).astype(BF16)
            dqh = dqh + tn(dsf, k[:base, cols])
            dkf = nn(dsf, qh)
            dvf = nn(pf.astype(BF16), gh)
            if carried:
                dkf = dkf + dk0[:base, cols]
                dvf = dvf + dv0[:base, cols]
            rest[3][:, cols] = dkf
            rest[4][:, cols] = dvf
        dq[:, cols] = (dqh.astype(BF16).astype(F32) * SCALE).astype(BF16)


def attn_bwd_call(starts, core, q, k, v, mine, other, w_out, lse, carry, win, group):
    c, d = w_out.shape
    carried = carry is not None
    kv = (win + 1) * WIN
    full = lambda a: pl.BlockSpec(a.shape, lambda *_: (0,) * a.ndim)
    first = pl.BlockSpec((kv, c), lambda *_: (0, 0))
    shapes = [SDS((WIN, c), BF16)] * 3 + ([SDS((win * WIN, c), F32)] * 2 if win else [])
    return pl.pallas_call(
        functools.partial(attn_bwd_kernel, win, group[-1], len(group), c // HD, carried),
        grid=(1,),
        in_specs=[SMEM, SMEM, first, first, first, full(mine), full(other), full(w_out), full(lse)]
        + ([first] * 2 if carried else []),
        out_specs=[full(s) for s in shapes],
        out_shape=shapes,
        scratch_shapes=[pltpu.VMEM((WIN, c), BF16)],
        cost_estimate=LONG,
        compiler_params=params(24),
        name="attn_bwd",
    )(starts, core, q, k, v, mine, other, w_out, lse, *(carry if carried else ()))


def one_kernel(wins, core, *refs):
    c = core[0]
    wq, wk, wv, keep, send, sums, buf = refs[3 * wins :]
    weights = jnp.concatenate([wq[...], wk[...], wv[...]], axis=0)
    for w in range(wins):
        dq, dk, dv = refs[3 * w : 3 * w + 3]
        part = nn(jnp.concatenate([dq[...], dk[...], dv[...]], axis=1), weights).astype(BF16)
        for at, g in enumerate((dq, dv)):
            total = col_sum(g[...].astype(F32))
            sums[at : at + 1, :] = total if w == 0 else sums[at : at + 1, :] + total
        if wins == 1:
            half = keep.shape[1]
            buf[...] = part
            keep[0] = buf[pl.ds(pl.multiple_of(c * half, half), half), :]
            send[0] = buf[pl.ds(pl.multiple_of((1 - c) * half, half), half), :]
        else:

            @pl.when(c == w)
            def _():
                keep[0] = part

            @pl.when(c != w)
            def _():
                send[0] = part


def one_call(core, grads, wq, wk, wv):
    c, d = wq.shape
    wins = len(grads)
    half = wins * WIN // 2
    flat = [g for window_grads in grads for g in window_grads]
    return pl.pallas_call(
        functools.partial(one_kernel, wins),
        in_specs=[SMEM] + [pl.BlockSpec((WIN, c))] * (3 * wins) + [pl.BlockSpec((c, d))] * 3,
        out_specs=[pl.BlockSpec((1, half, d))] * 2 + [pl.BlockSpec((8, c))],
        out_shape=[SDS((1, half, d), BF16)] * 2 + [SDS((8, c), F32)],
        scratch_shapes=[pltpu.VMEM((WIN, d), BF16)],
        cost_estimate=SHORT,
        compiler_params=params(16),
        name="grad_one",
    )(core, *flat, wq, wk, wv)


def attn_grad_kernel(bits, core, n1a, n1b, mxa, mxb, ga0, ga1, gb0, gb1, *refs):
    i = pl.program_id(0)
    c = mxa.shape[1]
    lowers = (refs[3:6], refs[6:9])
    ka, sa, kb, sb, acc = refs[9:]

    @pl.when(i == 0)
    def _():
        acc[...] = jnp.zeros_like(acc)

    def step(n1, grads, mx, gh):
        acc[: 3 * c, :] += tn(jnp.concatenate([g[...] for g in grads], axis=1), n1[...])
        acc[3 * c :, :] += tn(mx[...], gh[...])

    for at, gh in enumerate((ga0, ga1)):

        @pl.when(i == at)
        def _(gh=gh):
            step(n1a, refs[:3], mxa, gh)

    for at, gh in enumerate((gb0, gb1)):
        for w in range(2):

            @pl.when((i == 2 + at) & (lax.rem(at + core[0], 2) == w))
            def _(gh=gh, w=w):
                step(n1b, lowers[w], mxb, gh)

    @pl.when(i == 3)
    def _():
        rows = acc.shape[0] // 2
        split_store(acc, 0, rows, bits[0], ka, sa)
        split_store(acc, rows, rows, bits[1], kb, sb)


def attn_grad_call(bits, core, n1, mxs, ghs, grads_a, grads_0, grads_1):
    d = n1.shape[1]
    c = mxs[0].shape[1]
    na, nb = mxs[0].shape[0] // 2, mxs[1].shape[0] // 2
    fa = lambda w, o=0: pl.BlockSpec((na, w), lambda i, bits, core: (o + lax.rem(jnp.minimum(i, 1) + core[0], 2), 0))
    fb = lambda w: pl.BlockSpec((nb, w), lambda i, bits, core: (lax.rem(jnp.maximum(i - 2, 0) + core[0], 2), 0))
    return pl.pallas_call(
        attn_grad_kernel,
        grid_spec=pltpu.PrefetchScalarGridSpec(
            num_scalar_prefetch=2,
            grid=(4,),
            in_specs=[fa(d, 2 * nb // na), fb(d), fa(c), fb(c)]
            + [whole((na, d))] * 2
            + [whole((nb, d))] * 2
            + [fa(c)] * 3
            + [whole((nb, c))] * 6,
            out_specs=[whole((c, d))] * 4,
            scratch_shapes=[pltpu.VMEM((4 * c, d), F32)],
        ),
        out_shape=[SDS((c, d), BF16)] * 4,
        cost_estimate=GRAD_HINT,
        compiler_params=params(18),
        name="attn_grad",
    )(bits, core, n1, n1, *mxs, *ghs[0], *ghs[1], *grads_a, *grads_0, *grads_1)


def norm_one_kernel(core, s, x, tok, row, gh, gain, out, sums):
    @pl.when(pl.program_id(0) == 0)
    def _():
        sums[...] = jnp.zeros_like(sums)

    one = s[...].astype(F32) + x[...].astype(F32)
    hat, root = norm_parts(tok[...].astype(F32) + row[...])
    g = gh[...] + norm_back(one * gain[...], hat, root)
    out[...] = g.astype(BF16)
    sums[0:1, :] += col_sum(one * hat)
    sums[1:2, :] += col_sum(one)
    sums[2:3, :] += col_sum(g)


def norm_one_call(core, s, x, tok, row, gh, gain, row0, hint=SHORT):
    n, d = gh.shape
    return pl.pallas_call(
        norm_one_kernel,
        grid_spec=pltpu.PrefetchScalarGridSpec(
            num_scalar_prefetch=1,
            grid=(n // BT,),
            in_specs=[rows_at(d)] * 2 + [half_rows(d, n, row0), whole((1, d)), rows_at(d), whole((d,))],
            out_specs=[rows_at(d), whole((8, d))],
        ),
        out_shape=[SDS((n, d), BF16), SDS((8, d), F32)],
        cost_estimate=hint,
        compiler_params=params(16),
        name="norm_one_back",
    )(core, s, x, tok, row, gh, gain)


def out_kernel(nb, sb, xb, hid_b, sa, xa, hid_a, b_down, out):
    def store(s, x, hid):
        out[...] = (hid[...] + s[...].astype(F32) + x[...].astype(F32) + b_down[...]).astype(BF16)

    @pl.when(pl.program_id(0) < nb)
    def _():
        store(sb, xb, hid_b)

    @pl.when(pl.program_id(0) >= nb)
    def _():
        store(sa, xa, hid_a)


def out_call(sb, xb, hid_b, sa, xa, hid_a, b_down, hint=SHORT):
    n, d = hid_b.shape
    nb, na = n // BT, hid_a.shape[0] // BT
    lower = pl.BlockSpec((BT, d), lambda i: (jnp.minimum(i, nb - 1), 0))
    upper = pl.BlockSpec((BT, d), lambda i: (jnp.maximum(i - nb, 0), 0))
    return pl.pallas_call(
        functools.partial(out_kernel, nb),
        grid=(nb + na,),
        in_specs=[lower] * 3 + [upper] * 3 + [whole((d,))],
        out_specs=rows_at(d),
        out_shape=SDS(((nb + na) * BT, d), BF16),
        cost_estimate=hint,
        compiler_params=params(16),
        name="layer_out",
    )(sb, xb, hid_b, sa, xa, hid_a, b_down)


def rows_kernel(core, ao, at, bo, bt, out):
    na, nb = ao.shape[0], bo.shape[0]
    c = core[0]
    for src, base, n, half in ((bo, 0, nb, c), (bt, 0, nb, 1 - c), (ao, 2 * nb, na, c), (at, 2 * nb, na, 1 - c)):
        out[pl.ds(pl.multiple_of(base + half * n, 16), n), :] = src[...]


def rows_call(core, ao, at, bo, bt, hint=SHORT):
    na, d = ao.shape
    nb = bo.shape[0]
    return pl.pallas_call(
        rows_kernel,
        in_specs=[SMEM] + [pl.BlockSpec((na, d))] * 2 + [pl.BlockSpec((nb, d))] * 2,
        out_specs=pl.BlockSpec((2 * (na + nb), d)),
        out_shape=SDS((2 * (na + nb), d), BF16),
        cost_estimate=hint,
        compiler_params=params(12),
        name="in_order",
    )(core, ao, at, bo, bt)


def out_rows_kernel(core, own, other, out):
    na = WIN // 2
    nb = own.shape[0] - na
    c = core[0]
    for src, half in ((own, c), (other, 1 - c)):
        out[pl.ds(pl.multiple_of(half * nb, 16), nb), :] = src[:nb, :]
        out[pl.ds(pl.multiple_of(2 * nb + half * na, 16), na), :] = src[nb:, :]


def out_rows_call(core, own, other, hint=SHORT):
    n, d = own.shape
    return pl.pallas_call(
        out_rows_kernel,
        in_specs=[SMEM] + [pl.BlockSpec((n, d))] * 2,
        out_specs=pl.BlockSpec((2 * n, d)),
        out_shape=SDS((2 * n, d), BF16),
        cost_estimate=hint,
        compiler_params=params(12),
        name="in_order",
    )(core, own, other)


VALUE_AT = 256
STEP_AT = 512


def pack_kernel(scal, s2a, s2b, s1a, s1b, soa, sob, ffn, out):
    me, step = scal[0], scal[1]
    c = soa.shape[1]
    n = out.shape[0] - 8
    out[0:3, :] = s2a[0:3, :] + s2b[0:3, :]
    out[3:5, :] = s1a[0:2, :] + s1b[0:2, :]
    out[5:7, :] = ffn[0:2, :]
    out[7:8, :] = jnp.zeros((1, out.shape[1]), F32)
    so = soa[...] + sob[...]
    out[7:8, 0:c] = so[0:1, :]
    out[7:8, VALUE_AT : VALUE_AT + c] = so[1:2, :]
    lane = lax.broadcasted_iota(jnp.int32, (1, out.shape[1] - STEP_AT), 1)
    out[7:8, STEP_AT:] = jnp.where(lane == me, step.astype(F32), 0.0)
    spot = lax.broadcasted_iota(jnp.int32, (n, 1), 0) == me
    out[8:, :] = jnp.where(spot, s1a[2:3, :] + s1b[2:3, :], 0.0)


def pack_call(scal, n_dp, s2a, s2b, s1a, s1b, soa, sob, ffn, hint=SHORT):
    d = ffn.shape[1]
    rows = 8 + -(-n_dp // 8) * 8
    return pl.pallas_call(
        pack_kernel,
        in_specs=[SMEM] + [pl.BlockSpec(v.shape) for v in (s2a, s2b, s1a, s1b, soa, sob, ffn)],
        out_specs=pl.BlockSpec((rows, d)),
        out_shape=SDS((rows, d), F32),
        cost_estimate=hint,
        compiler_params=params(4),
        name="pack",
    )(scal, s2a, s2b, s1a, s1b, soa, sob, ffn)


def small_add_kernel(own_rows, a, b, out):
    out[...] = a[...] + b[...]
    if own_rows:
        out[5:8, :] = a[5:8, :]


def small_add(a, b, own_rows=False):
    return pl.pallas_call(
        functools.partial(small_add_kernel, own_rows),
        in_specs=[pl.BlockSpec(a.shape)] * 2,
        out_specs=pl.BlockSpec(a.shape),
        out_shape=SDS(a.shape, F32),
        cost_estimate=SHORT,
        compiler_params=params(4),
        name="small_add",
    )(a, b)


def unpack_kernel(n_dp, small, got, *outs):
    table, vecs, bq, bv, full = outs[0], outs[1:8], outs[8], outs[9], outs[10]
    full[...] = small[...] + got[...]
    for n, vec in enumerate(vecs):
        vec[...] = full[n, :]
    c = bq.shape[0]
    bq[...] = full[7, 0:c]
    bv[...] = full[7, VALUE_AT : VALUE_AT + c]
    table[...] = jnp.zeros_like(table)
    steps = full[7:8, STEP_AT:]
    lane = lax.broadcasted_iota(jnp.int32, steps.shape, 1)
    for n in range(n_dp):
        at = jnp.sum(jnp.where(lane == n, steps, 0.0)).astype(jnp.int32)
        table[pl.ds(at, 1), :] += full[8 + n : 9 + n, :]


def unpack_call(n_dp, table_rows, c, small, got):
    rows, d = small.shape
    shapes = [(table_rows, d)] + [(d,)] * 7 + [(c,)] * 2
    return pl.pallas_call(
        functools.partial(unpack_kernel, n_dp),
        in_specs=[pl.BlockSpec(small.shape)] * 2,
        out_specs=[pl.BlockSpec(s) for s in shapes],
        out_shape=[SDS(s, F32) for s in shapes],
        scratch_shapes=[pltpu.VMEM(small.shape, F32)],
        cost_estimate=SHORT,
        compiler_params=params(10),
        name="unpack",
    )(small, got)


def after(token, value):
    return lax.optimization_barrier((token, value))[1]


class Spread:
    def __init__(self, n_dp, bits, orders, keep, send):
        self.n_dp, self.bits, self.orders, self.level = n_dp, bits, orders, 2
        self.keep = keep
        self.swap(0, send)

    def swap(self, level, values):
        self.got = [
            lax.ppermute(v, "dp", [(i, i ^ (1 << order[level])) for i in range(self.n_dp)])
            for v, order in zip(values, self.orders)
        ]

    def step(self, token, kernel, name, bits, shapes, hint, scratch=()):
        keep = [after(token, self.keep[0]), *self.keep[1:]]
        arrays = [a for pair in zip(keep, self.got) for a in pair]
        return step_call(kernel, name, bits, arrays, shapes, hint, scratch)

    def halve(self, token, hint=SHORT):
        n, d = self.keep[0].shape
        half = [SDS((n // 2, d), BF16)] * (2 * len(self.keep))
        out = self.step(token, halve_kernel, "halve", self.bits, half, hint, [pltpu.VMEM((n, d), F32)])
        self.keep = out[0::2]
        self.swap(1, out[1::2])
        return self.keep[0]

    def exchange(self, token, hint=SHORT):
        same = [SDS(k.shape, BF16) for k in self.keep]
        self.keep = self.step(token, add_kernel, "pair_add", None, same, hint)
        self.swap(self.level if self.level < len(self.orders[0]) else 1, self.keep)
        self.level += 1
        return self.keep[0]

    def join(self, token, hint=SHORT):
        n, d = self.keep[0].shape
        self.keep = self.step(token, join_kernel, "join", None, [SDS((2 * n, d), BF16)] * len(self.keep), hint)
        self.swap(0, self.keep)
        return self.keep[0]

    def place(self, token, pieces, hint=SHORT):
        n, d = self.keep[0].shape
        rows = 2 * n * len(self.keep) // pieces
        return self.step(token, place_kernel, "place", self.bits, [SDS((rows, d), F32)] * pieces, hint)


def per_device(
    n_tensor,
    n_dp,
    tokens,
    timesteps,
    piece_starts,
    step_table,
    first_gain,
    first_shift,
    w_query,
    b_query,
    w_key,
    w_value,
    b_value,
    w_out,
    b_out,
    second_gain,
    second_shift,
    w_in,
    b_in,
    w_down,
    b_down,
    cotangent,
):
    length, d = tokens.shape[1:]
    c = w_query.shape[1]
    rank = lax.axis_index("tensor").astype(jnp.int32)
    me = lax.axis_index("dp").astype(jnp.int32)
    over_x = [(i, i ^ 2) for i in range(n_tensor)]
    over_core = [(i, i ^ 1) for i in range(n_tensor)]
    swap_x = lambda v: lax.ppermute(v, "tensor", over_x)
    swap_core = lambda v: lax.ppermute(v, "tensor", over_core)
    n_bits = n_dp.bit_length() - 1
    orders = (list(range(n_bits)), list(range(1, n_bits)) + [0])
    bit = lambda b: (me >> b) & 1
    bits = jnp.stack([bit(orders[0][0]), bit(orders[1][0]), bit(orders[0][1]), bit(orders[1][1])])
    scal = jnp.stack([me, timesteps[0]])
    core = (rank & 1)[None]
    tok, bits, scal, core, starts = lax.optimization_barrier((tokens[0], bits, scal, core, piece_starts[0]))
    cot = cotangent[0]
    wq, wk, wv = w_query.T, w_key.T, w_value.T

    top = length // WIN - 1
    groups = [[top], list(range(top - 1, -1, -1))]
    row0s = [top * WIN, 0]
    hbm = lambda v: pltpu.with_memory_space_constraint(v, pltpu.HBM)

    n1, q, k, v, row = qkv_call(
        timesteps, *[hbm(z) for z in (tok, step_table, first_gain, first_shift, wq, wk, wv, b_query, b_value)]
    )
    wo0 = w_out
    wo2 = swap_x(after(n1, w_out))
    mix_a, lse_a = attn_fwd_call(starts, q, k, v, groups[0])
    wo1 = swap_core(after(mix_a, w_out))
    wo3 = swap_core(after(mix_a, wo2))
    wos = [wo0, wo2, wo1, wo3]
    m1_a, m2_a = swap_core(mix_a), swap_x(mix_a)
    mix_b, lse_b = attn_fwd_call(starts, after(mix_a, q), k, v, groups[1])
    m3_a = swap_core(after(mix_b, m2_a))
    m2_b = swap_x(mix_b)

    def ffn_of(ms, n):
        return ffn_call(
            core, ms, tok, row, cot, wos, b_out, second_gain, second_shift, w_in, b_in, w_down, row0s[n]
        )

    hid_a, n2_a, act_a, gpre_a, keep_a, send_a = ffn_of([mix_a, m2_a, m1_a, m3_a], 0)
    got_a = swap_core(send_a)
    pair_b = stack_call(after(n2_a, mix_b), m2_b)
    far_b = swap_core(pair_b)
    two_a = half_sum(after(pair_b, keep_a), got_a, 0)
    twox_a = swap_x(two_a)
    mlp_a = half_sum(after(two_a, keep_a), got_a, 1)
    hid_b, n2_b, act_b, gpre_b, keep_b, send_b = ffn_of([after(mlp_a, mix_b), m2_b, far_b], 1)
    got_b = swap_core(send_b)
    gh_a, ghb_a, s2_a = norm_two_call(core, after(n2_b, two_a), twox_a, hid_a, cot, second_gain, row0s[0])
    gho_a = swap_core(ghb_a)
    mlpx_a = swap_x(after(ghb_a, mlp_a))
    ka, sa, kb, sb, ffn_sums = ffn_grad_call(
        bits, core, after(ghb_a, n2_a), n2_b, gpre_a, gpre_b, act_a, act_b, cot
    )
    gff = Spread(n_dp, bits, orders, [ka, kb], [sa, sb])
    two_b = half_sum(after(ka, keep_b), got_b, 0)
    twox_b = swap_x(two_b)
    *grads_a, dkf, dvf = attn_bwd_call(
        starts, core, after((two_b, mlpx_a), q), k, v, ghb_a, gho_a, w_out, lse_a, None, top, groups[0]
    )
    one_a, osend_a, so_a = one_call(core, [grads_a], wq, wk, wv)
    ogot_a = swap_core(osend_a)
    t = gff.halve(one_a)
    gh_b, ghb_b, s2_b = norm_two_call(core, after(t, two_b), twox_b, hid_b, cot, second_gain, row0s[1], LONG)
    gho_b = swap_core(ghb_b)
    os_a = half_sum(after(ghb_b, one_a), ogot_a, 0, LONG)
    ox_a = swap_x(os_a)
    mlp_b = half_sum(after(os_a, keep_b), got_b, 1)
    *grads_1, dkf, dvf = attn_bwd_call(
        starts, core, after(mlp_b, q), k, v, ghb_b, gho_b, w_out, lse_b, (dkf, dvf), 1, groups[1]
    )
    t = gff.exchange(grads_1[0])
    gt_a, s1_a = norm_one_call(core, after(t, os_a), ox_a, tok, row, gh_a, first_gain, row0s[0])
    mlpx_b = swap_x(after(gt_a, mlp_b))
    grads_0 = attn_bwd_call(
        starts, core, after(gt_a, q), k, v, ghb_b, gho_b, w_out, lse_b, (dkf, dvf), 0, groups[1]
    )
    one_b, osend_b, so_b = one_call(core, [grads_0, grads_1], wq, wk, wv)
    ogot_b = swap_core(osend_b)
    ka, sa, kb, sb = attn_grad_call(
        bits, core, after(one_b, n1), (mix_a, mix_b), ((ghb_a, gho_a), (ghb_b, gho_b)), grads_a, grads_0, grads_1
    )
    gat = Spread(n_dp, bits, orders, [ka, kb], [sa, sb])
    t = ka
    for _ in range(n_bits - 2):
        t = gff.exchange(t, LONG)
    os_b = half_sum(after(t, one_b), ogot_b, 0)
    ox_b = swap_x(os_b)
    t = gat.halve((os_b, mlpx_b))
    t = gff.join(t)
    t = gat.exchange(t)
    gt_b, s1_b = norm_one_call(core, after(t, os_b), ox_b, tok, row, gh_b, first_gain, row0s[1], LONG)
    small = pack_call(after(gt_b, scal), n_dp, s2_a, s2_b, s1_a, s1_b, so_a, so_b, ffn_sums)
    swapped = swap_core(small)
    t = small
    for _ in range(n_bits - 2):
        t = gat.exchange(t)
    small = small_add(after(t, small), swapped, True)
    swap_dp = lambda v, b: lax.ppermute(v, "dp", [(i, i ^ (1 << b)) for i in range(n_dp)])
    got = swap_dp(small, 0)
    g_in, g_down = gff.place(small, 2, LONG)
    small = small_add(after(g_in, small), got)
    got = swap_dp(small, 1)
    t = gat.join(small)
    o = out_call(after(t, mlp_b), mlpx_b, hid_b, mlp_a, mlpx_a, hid_a, b_down, LONG)
    oo, gto_a, gto_b = swap_core(o), swap_core(after(o, gt_a)), swap_core(after(o, gt_b))
    small = after(o, small)
    for b in range(2, n_bits):
        small = small_add(small, got)
        got = swap_dp(small, b)
    grad_tokens = rows_call(core, after(small, gt_a), gto_a, gt_b, gto_b)
    output = out_rows_call(core, after(grad_tokens, o), oo)
    g_table, g_sg, g_ss, g_bo, g_fg, g_fs, g_bi, g_bd, g_bq, g_bv = unpack_call(
        n_dp, step_table.shape[0], c, after(output, small), got
    )
    g_q, g_k, g_v, g_o = gat.place(g_sg, 4)
    return (
        output[None],
        grad_tokens[None],
        g_table,
        g_fg,
        g_fs,
        g_q.T,
        g_bq,
        g_k.T,
        g_v.T,
        g_bv,
        g_o,
        g_bo,
        g_sg,
        g_ss,
        g_in,
        g_bi,
        g_down,
        g_bd,
    )


def solution(mesh):
    in_specs = (
        P("dp", None, None),
        P("dp"),
        P("dp", None),
        P(),
        P(),
        P(),
        P(None, "tensor"),
        P("tensor"),
        P(None, "tensor"),
        P(None, "tensor"),
        P("tensor"),
        P("tensor", None),
        P(),
        P(),
        P(),
        P(None, "tensor"),
        P("tensor"),
        P("tensor", None),
        P(),
        P("dp", None, None),
    )
    out_specs = (
        P("dp", None, None),
        P("dp", None, None),
        P(),
        P(),
        P(),
        P(None, "tensor"),
        P("tensor"),
        P(None, "tensor"),
        P(None, "tensor"),
        P("tensor"),
        P("tensor", None),
        P(),
        P(),
        P(),
        P(None, "tensor"),
        P("tensor"),
        P("tensor", None),
        P(),
    )
    return jax.shard_map(
        functools.partial(per_device, mesh.shape["tensor"], mesh.shape["dp"]),
        mesh=mesh,
        in_specs=in_specs,
        out_specs=out_specs,
        check_vma=False,
    )
```

```python
import functools

import jax
import jax.numpy as jnp
from jax import lax
from jax.experimental import pallas as pl
from jax.experimental.pallas import tpu as pltpu
from jax.sharding import PartitionSpec as P

HD = 64
PIECE = 256
WIN = 2 * PIECE
EPS = 1e-05
BT = 256
F32 = jnp.float32
BF16 = jnp.bfloat16
SDS = jax.ShapeDtypeStruct
SCALE = HD ** (-0.5)
GELU_C = 0.7978845608028654


def nn(a, b):
    return lax.dot_general(a, b, (((1,), (0,)), ((), ())), preferred_element_type=F32)


def nt(a, b):
    return lax.dot_general(a, b, (((1,), (1,)), ((), ())), preferred_element_type=F32)


def tn(a, b):
    return lax.dot_general(a, b, (((0,), (0,)), ((), ())), preferred_element_type=F32)


def norm_parts(v):
    c = v - jnp.mean(v, axis=-1, keepdims=True)
    root = lax.rsqrt(jnp.mean(c * c, axis=-1, keepdims=True) + EPS)
    return c * root, root


def norm_back(e, hat, root):
    return root * (
        e - jnp.mean(e, axis=-1, keepdims=True) - hat * jnp.mean(e * hat, axis=-1, keepdims=True)
    )


def col_sum(v):
    return jnp.sum(v, axis=0, keepdims=True)


def whole(shape):
    return pl.BlockSpec(shape, lambda i, *_: (0,) * len(shape))


def rows_at(width, offset=0, block=BT):
    return pl.BlockSpec((block, width), lambda i, *_: (offset + i, 0))


LONG = pl.CostEstimate(flops=10**11, bytes_accessed=1000, transcendentals=0)
SHORT = pl.CostEstimate(flops=1000, bytes_accessed=1000, transcendentals=0)
GRAD_HINT = SHORT


def params(mib=12):
    return pltpu.CompilerParams(vmem_limit_bytes=mib * 1024 * 1024)


SMEM = pl.BlockSpec(memory_space=pltpu.SMEM)


def qkv_kernel(steps, tok, table, gain, shift, wq, wk, wv, bq, bv, n1, q, k, v, row):
    rows = table[...].astype(F32)
    at = lax.broadcasted_iota(jnp.int32, rows.shape, 0) == lax.rem(steps[0], 8)
    step_row = col_sum(jnp.where(at, rows, 0.0))
    row[...] = step_row
    hat, _ = norm_parts(tok[...].astype(F32) + step_row)
    n = (hat * gain[...] + shift[...]).astype(BF16)
    n1[...] = n
    q[...] = ((nt(n, wq[...]) + bq[...]) * SCALE).astype(BF16)
    k[...] = nt(n, wk[...]).astype(BF16)
    v[...] = (nt(n, wv[...]) + bv[...]).astype(BF16)


def qkv_call(steps, tok, table, gain, shift, wq, wk, wv, bq, bv):
    length, d = tok.shape
    c = wq.shape[0]
    return pl.pallas_call(
        qkv_kernel,
        grid_spec=pltpu.PrefetchScalarGridSpec(
            num_scalar_prefetch=1,
            grid=(length // WIN,),
            in_specs=[rows_at(d, block=WIN), pl.BlockSpec((8, d), lambda i, steps: (steps[0] // 8, 0))]
            + [whole((d,))] * 2
            + [whole((c, d))] * 3
            + [whole((c,))] * 2,
            out_specs=[rows_at(d, block=WIN)] + [rows_at(c, block=WIN)] * 3 + [whole((1, d))],
        ),
        out_shape=[SDS((length, d), BF16)] + [SDS((length, c), BF16)] * 3 + [SDS((1, d), F32)],
        cost_estimate=LONG,
        compiler_params=params(16),
        name="norm_qkv",
    )(steps, tok, table, gain, shift, wq, wk, wv, bq, bv)


def attn_fwd_window(win, nh, starts, q, k, v, mix, lse):
    base = win * WIN
    start = starts[win]
    qpos = base + lax.broadcasted_iota(jnp.int32, (WIN, 1), 0)
    limit = jnp.where((qpos >= start) & (qpos < start + PIECE), start + PIECE - 1, qpos)
    kpos = base + lax.broadcasted_iota(jnp.int32, (1, WIN), 1)
    allow = kpos <= limit
    for h in range(nh):
        cols = slice(h * HD, (h + 1) * HD)
        qh = q[:, cols]
        near = jnp.where(allow, nt(qh, k[base : base + WIN, cols]), -1e30)
        top = jnp.max(near, axis=-1, keepdims=True)
        if win:
            far = nt(qh, k[:base, cols])
            top = jnp.maximum(top, jnp.max(far, axis=-1, keepdims=True))
        pn = jnp.exp(near - top)
        total = jnp.sum(pn, axis=-1, keepdims=True)
        out = nn(pn.astype(BF16), v[base : base + WIN, cols])
        if win:
            pf = jnp.exp(far - top)
            total = total + jnp.sum(pf, axis=-1, keepdims=True)
            out = out + nn(pf.astype(BF16), v[:base, cols])
        mix[:, cols] = (out / total).astype(BF16)
        stat = jnp.broadcast_to(top + jnp.log(total), (WIN, 128))
        lse[h : h + 1, :] = jnp.transpose(stat)[0:1, :]


def attn_fwd_kernel(wins, nh, starts, *refs):
    for n, win in enumerate(wins):

        @pl.when(pl.program_id(0) == n)
        def _(win=win):
            attn_fwd_window(win, nh, starts, *refs)


def attn_fwd_call(starts, q, k, v, wins):
    c = q.shape[1]
    kv = (wins[0] + 1) * WIN
    n = len(wins) * WIN
    return pl.pallas_call(
        functools.partial(attn_fwd_kernel, wins, c // HD),
        grid=(len(wins),),
        in_specs=[SMEM, pl.BlockSpec((WIN, c), lambda i: (wins[0] - i, 0)), whole((kv, c)), whole((kv, c))],
        out_specs=[
            pl.BlockSpec((WIN, c), lambda i: (wins[0] - wins[-1] - i, 0)),
            pl.BlockSpec((8, WIN), lambda i: (0, wins[0] - wins[-1] - i)),
        ],
        out_shape=[SDS((n, c), BF16), SDS((8, n), F32)],
        cost_estimate=LONG,
        compiler_params=params(20),
        name="attn_fwd",
    )(starts, q, k, v)


def stack_kernel(a, b, out):
    c = a.shape[1]
    out[:, :c] = a[...]
    out[:, c:] = b[...]


def stack_call(a, b):
    n, c = a.shape
    return pl.pallas_call(
        stack_kernel,
        in_specs=[pl.BlockSpec((n, c))] * 2,
        out_specs=pl.BlockSpec((n, 2 * c)),
        out_shape=SDS((n, 2 * c), BF16),
        cost_estimate=LONG,
        compiler_params=params(6),
        name="stack",
    )(a, b)


def ffn_kernel(
    pieces, core, *refs
):
    kept, sent, wos = refs[:pieces], refs[pieces : 2 * pieces], refs[2 * pieces + 5 : 2 * pieces + 9]
    tok_k, tok_s, row, cot_k, cot_s = refs[2 * pieces : 2 * pieces + 5]
    b_out, gain, shift, w_in, b_in, w_down, hid, n2, act, gpre, keep, send = refs[2 * pieces + 9 :]
    rows = tok_k.shape[0]
    both = lambda a, b: jnp.concatenate([a[...], b[...]], axis=0)
    mixed = jnp.concatenate([both(a, b) for a, b in zip(kept, sent)], axis=1)
    attn = nn(mixed, jnp.concatenate([w[...] for w in wos], axis=0))
    h = both(tok_k, tok_s).astype(F32) + row[...] + attn + b_out[...]
    hid[...] = h[:rows]
    hat, _ = norm_parts(h)
    n = (hat * gain[...] + shift[...]).astype(BF16)
    z = nn(n, w_in[...]) + b_in[...]
    z2 = z * z
    th = jnp.tanh(z * (GELU_C + (GELU_C * 0.044715) * z2))
    half = 0.5 * (1.0 + th)
    a = (z * half).astype(BF16)
    slope = half + (0.5 * z) * (1.0 - th * th) * (GELU_C + (3.0 * 0.044715 * GELU_C) * z2)
    gp = (nt(both(cot_k, cot_s), w_down[...]) * slope).astype(BF16)
    mlp = nn(a, w_down[...]).astype(BF16)
    two = nt(gp, w_in[...]).astype(BF16)
    for part, at in enumerate((slice(0, rows), slice(rows, 2 * rows))):
        n2[part] = n[at]
        act[part] = a[at]
        gpre[part] = gp[at]
        out = send if part else keep
        out[0] = two[at]
        out[1] = mlp[at]


def half_spec(width, nb, own, offset=0):
    return pl.BlockSpec((BT, width), lambda i, core: (offset + (core[0] if own else 1 - core[0]) * nb + i, 0))


def stacked(width, block=BT):
    return pl.BlockSpec((2, block, width), lambda i, *_: (0, i, 0))


def ffn_call(core, ms, tok, row, cot, wos, b_out, gain, shift, w_in, b_in, w_down, row0):
    n = ms[0].shape[0]
    c, d = wos[0].shape
    u = w_in.shape[1]
    h = n // 2
    nb = h // BT
    off = row0 // BT
    kept = functools.partial(half_spec, nb=nb, own=True)
    sent = functools.partial(half_spec, nb=nb, own=False)
    return pl.pallas_call(
        functools.partial(ffn_kernel, len(ms)),
        grid_spec=pltpu.PrefetchScalarGridSpec(
            num_scalar_prefetch=1,
            grid=(nb,),
            in_specs=[kept(v.shape[1]) for v in ms]
            + [sent(v.shape[1]) for v in ms]
            + [kept(d, offset=off), sent(d, offset=off), whole((1, d)), kept(d, offset=off), sent(d, offset=off)]
            + [whole((c, d))] * 4
            + [whole((d,))] * 3
            + [whole((d, u)), whole((u,)), whole((u, d))],
            out_specs=[rows_at(d), stacked(d), stacked(u), stacked(u), stacked(d), stacked(d)],
        ),
        out_shape=[SDS((h, d), F32), SDS((2, h, d), BF16)]
        + [SDS((2, h, u), BF16)] * 2
        + [SDS((2, h, d), BF16)] * 2,
        cost_estimate=LONG,
        compiler_params=params(24),
        name="ffn",
    )(core, *ms, *ms, tok, tok, row, cot, cot, *wos, b_out, gain, shift, w_in, b_in, w_down)


def split_store(acc, first, rows, bit, keep, send):
    half = rows // 2
    keep[...] = acc[pl.ds(pl.multiple_of(first + bit * half, 16), half), :].astype(BF16)
    send[...] = acc[pl.ds(pl.multiple_of(first + (1 - bit) * half, 16), half), :].astype(BF16)


def halve_kernel(parts, bits, *refs):
    ins, outs, acc = refs[: 2 * parts], refs[2 * parts : 4 * parts], refs[4 * parts]
    for part in range(parts):
        acc[...] = ins[2 * part][...].astype(F32) + ins[2 * part + 1][...].astype(F32)
        split_store(acc, 0, acc.shape[0], bits[2 + part], outs[2 * part], outs[2 * part + 1])


def add_kernel(parts, *refs):
    for part in range(parts):
        k, r = refs[2 * part : 2 * part + 2]
        refs[2 * parts + part][...] = (k[...].astype(F32) + r[...].astype(F32)).astype(BF16)


def join_kernel(parts, *refs):
    for part in range(parts):
        s, r = refs[2 * part : 2 * part + 2]
        n = s.shape[0]
        refs[2 * parts + part][:n, :] = s[...]
        refs[2 * parts + part][n:, :] = r[...]


def place_kernel(parts, bits, *refs):
    outs = refs[2 * parts :]
    per = len(outs) // parts
    for part in range(parts):
        p, r = refs[2 * part : 2 * part + 2]
        n = p.shape[0] // 2
        b0, b1 = bits[part], bits[2 + part]
        for src, first in ((p, b0), (r, 1 - b0)):
            for which in range(2):

                @pl.when(first == which)
                def _(src=src, which=which):
                    out = outs[part if per == 1 else 2 * part + which]
                    for sub, second in ((0, b1), (1, 1 - b1)):
                        at = pl.multiple_of(second * n, 8) + (2 * n * which if per == 1 else 0)
                        out[pl.ds(at, n), :] = src[sub * n : (sub + 1) * n, :].astype(F32)


def step_call(kernel, name, bits, arrays, shapes, hint, scratch=()):
    parts = len(arrays) // 2
    return pl.pallas_call(
        functools.partial(kernel, parts),
        in_specs=([] if bits is None else [SMEM]) + [pl.BlockSpec(a.shape) for a in arrays],
        out_specs=[pl.BlockSpec(s.shape) for s in shapes],
        out_shape=shapes,
        scratch_shapes=scratch,
        cost_estimate=hint,
        compiler_params=params(14),
        name=name,
    )(*([] if bits is None else [bits]), *arrays)


def one_sum_kernel(keep, got, out):
    out[...] = (keep[...].astype(F32) + got[...].astype(F32)).astype(BF16)


def one_sum(keep, got, hint=SHORT):
    return pl.pallas_call(
        one_sum_kernel,
        in_specs=[pl.BlockSpec(keep.shape)] * 2,
        out_specs=pl.BlockSpec(keep.shape),
        out_shape=SDS(keep.shape, BF16),
        cost_estimate=hint,
        compiler_params=params(8),
        name="one_sum",
    )(keep, got)


def half_sum_kernel(keep, got, out):
    out[...] = (keep[0].astype(F32) + got[0].astype(F32)).astype(BF16)


def half_sum(keep, got, which, hint=SHORT):
    _, n, d = keep.shape
    part = pl.BlockSpec((1, n, d), lambda i: (which, 0, 0))
    return pl.pallas_call(
        half_sum_kernel,
        grid=(1,),
        in_specs=[part, part],
        out_specs=whole((n, d)),
        out_shape=SDS((n, d), BF16),
        cost_estimate=hint,
        compiler_params=params(8),
        name="half_sum",
    )(keep, got)


def ffn_grad_step(n2, gp, ac, cot_k, cot_s, acc_in, acc_down, sums):
    flat = lambda ref: ref[...].reshape(2 * ref.shape[1], ref.shape[2])
    cot = jnp.concatenate([cot_k[...], cot_s[...]], axis=0)
    g = flat(gp)
    acc_in[...] += tn(flat(n2), g)
    acc_down[...] += tn(flat(ac), cot)
    sums[0:1, :] += col_sum(g.astype(F32))
    sums[1:2, :] += col_sum(cot.astype(F32))


def ffn_grad_first_kernel(core, n2, gp, ac, cot_k, cot_s, acc_in, acc_down, sums):
    for ref in (acc_in, acc_down, sums):
        ref[...] = jnp.zeros_like(ref)
    ffn_grad_step(n2, gp, ac, cot_k, cot_s, acc_in, acc_down, sums)


def ffn_grad_last_kernel(bits, core, n2, gp, ac, cot_k, cot_s, in0, down0, sums0, ka, sa, kb, sb, sums, acc_in, acc_down):
    @pl.when(pl.program_id(0) == 0)
    def _():
        acc_in[...] = in0[...]
        acc_down[...] = down0[...]
        sums[...] = sums0[...]

    ffn_grad_step(n2, gp, ac, cot_k, cot_s, acc_in, acc_down, sums)

    @pl.when(pl.program_id(0) == pl.num_programs(0) - 1)
    def _():
        split_store(acc_in, 0, acc_in.shape[0], bits[0], ka, sa)
        split_store(acc_down, 0, acc_down.shape[0], bits[1], kb, sb)


def ffn_grad_call(bits, core, n2, gp, ac, cot, row0, before=None, hint=SHORT):
    _, h, d = n2.shape
    u = gp.shape[2]
    nb = h // BT
    block = lambda w: pl.BlockSpec((2, BT, w), lambda i, *_: (0, i, 0))

    def cot_spec(own):
        return pl.BlockSpec(
            (BT, d), lambda i, *s: (row0 // BT + (s[-1][0] if own else 1 - s[-1][0]) * nb + i, 0)
        )

    sums = [(d, u), (u, d), (8, d)]
    last = before is not None
    outs = [(d // 2, u)] * 2 + [(u // 2, d)] * 2 + [(8, d)] if last else sums
    types = [BF16] * 4 + [F32] if last else [F32] * 3
    return pl.pallas_call(
        ffn_grad_last_kernel if last else ffn_grad_first_kernel,
        grid_spec=pltpu.PrefetchScalarGridSpec(
            num_scalar_prefetch=2 if last else 1,
            grid=(nb,),
            in_specs=[block(d), block(u), block(u), cot_spec(True), cot_spec(False)]
            + ([whole(s) for s in sums] if last else []),
            out_specs=[whole(s) for s in outs],
            scratch_shapes=[pltpu.VMEM(s, F32) for s in sums[:2]] if last else [],
        ),
        out_shape=[SDS(s, t) for s, t in zip(outs, types)],
        cost_estimate=hint,
        compiler_params=params(24 if last else 16),
        name="ffn_grad",
    )(*([bits] if last else []), core, n2, gp, ac, cot, cot, *(before or ()))


def norm_two_kernel(core, s, x, hid, cot, gain, gh, ghb, sums):
    @pl.when(pl.program_id(0) == 0)
    def _():
        sums[...] = jnp.zeros_like(sums)

    two = s[...].astype(F32) + x[...].astype(F32)
    hat, root = norm_parts(hid[...])
    g = cot[...].astype(F32) + norm_back(two * gain[...], hat, root)
    gh[...] = g
    ghb[...] = g.astype(BF16)
    sums[0:1, :] += col_sum(two * hat)
    sums[1:2, :] += col_sum(two)
    sums[2:3, :] += col_sum(g)


def half_rows(d, n, row0):
    return pl.BlockSpec((BT, d), lambda i, core: (row0 // BT + core[0] * (n // BT) + i, 0))


def norm_two_call(core, s, x, hid, cot, gain, row0, hint=SHORT):
    n, d = hid.shape
    return pl.pallas_call(
        norm_two_kernel,
        grid_spec=pltpu.PrefetchScalarGridSpec(
            num_scalar_prefetch=1,
            grid=(n // BT,),
            in_specs=[rows_at(d)] * 3 + [half_rows(d, n, row0), whole((d,))],
            out_specs=[rows_at(d)] * 2 + [whole((8, d))],
        ),
        out_shape=[SDS((n, d), F32), SDS((n, d), BF16), SDS((8, d), F32)],
        cost_estimate=hint,
        compiler_params=params(16),
        name="norm_two_back",
    )(core, s, x, hid, cot, gain)


def attn_bwd_kernel(win, low, wins, nh, carried, starts, core, q, k, v, mine, other, w_out, lse, *rest):
    if carried:
        dk0, dv0, rest = rest[0], rest[1], rest[2:]
    dq, dk, dv = rest[:3]
    gm = rest[-1]
    base = win * WIN
    near = slice(base, base + WIN)
    grad = lambda ref: nt(ref[...], w_out[...]).astype(BF16)
    if wins == 1:
        half = WIN // 2
        gm[pl.ds(pl.multiple_of(core[0] * half, half), half), :] = grad(mine)
        gm[pl.ds(pl.multiple_of((1 - core[0]) * half, half), half), :] = grad(other)
    else:

        @pl.when(core[0] == win - low)
        def _():
            gm[...] = grad(mine)

        @pl.when(core[0] != win - low)
        def _():
            gm[...] = grad(other)

    start = starts[win]
    qpos = base + lax.broadcasted_iota(jnp.int32, (1, WIN), 1)
    limit = jnp.where((qpos >= start) & (qpos < start + PIECE), start + PIECE - 1, qpos)
    kpos = base + lax.broadcasted_iota(jnp.int32, (WIN, 1), 0)
    allow = kpos <= limit
    for h in range(nh):
        cols = slice(h * HD, (h + 1) * HD)
        qh = q[near, cols]
        gh = gm[:, cols]
        ls = lse[h : h + 1, (win - low) * WIN : (win - low + 1) * WIN]
        pn = jnp.exp(jnp.where(allow, nt(k[near, cols], qh), -1e30) - ls)
        dpn = nt(v[near, cols], gh)
        centre = col_sum(pn * dpn)
        if win:
            pf = jnp.exp(nt(k[:base, cols], qh) - ls)
            dpf = nt(v[:base, cols], gh)
            centre = centre + col_sum(pf * dpf)
        dsn = (pn * (dpn - centre)).astype(BF16)
        dqt = tn(k[near, cols], dsn)
        dkn = nn(dsn, qh)
        dvn = nn(pn.astype(BF16), gh)
        if carried:
            dkn = dkn + dk0[near, cols]
            dvn = dvn + dv0[near, cols]
        dk[:, cols] = dkn.astype(BF16)
        dv[:, cols] = dvn.astype(BF16)
        if win:
            dsf = (pf * (dpf - centre)).astype(BF16)
            dqt = dqt + tn(k[:base, cols], dsf)
            dkf = nn(dsf, qh)
            dvf = nn(pf.astype(BF16), gh)
            if carried:
                dkf = dkf + dk0[:base, cols]
                dvf = dvf + dv0[:base, cols]
            rest[3][:, cols] = dkf
            rest[4][:, cols] = dvf
        dq[:, cols] = jnp.transpose((dqt.astype(BF16).astype(F32) * SCALE)).astype(BF16)


def attn_bwd_call(starts, core, q, k, v, mine, other, w_out, lse, carry, win, group, hint=LONG):
    c, d = w_out.shape
    carried = carry is not None
    kv = (win + 1) * WIN
    full = lambda a: pl.BlockSpec(a.shape, lambda *_: (0,) * a.ndim)
    first = pl.BlockSpec((kv, c), lambda *_: (0, 0))
    shapes = [SDS((WIN, c), BF16)] * 3 + ([SDS((win * WIN, c), F32)] * 2 if win else [])
    return pl.pallas_call(
        functools.partial(attn_bwd_kernel, win, group[-1], len(group), c // HD, carried),
        grid=(1,),
        in_specs=[SMEM, SMEM, first, first, first, full(mine), full(other), full(w_out), full(lse)]
        + ([first] * 2 if carried else []),
        out_specs=[full(s) for s in shapes],
        out_shape=shapes,
        scratch_shapes=[pltpu.VMEM((WIN, c), BF16)],
        cost_estimate=hint,
        compiler_params=params(24),
        name="attn_bwd",
    )(starts, core, q, k, v, mine, other, w_out, lse, *(carry if carried else ()))


def one_kernel(core, *refs):
    wq, wk, wv, keep, send, sums, buf = refs[9:]
    c = core[0]
    n = buf.shape[0]
    half = n // 2
    weights = jnp.concatenate([wq[...], wk[...], wv[...]], axis=0)
    for w in range(3):
        dq, dk, dv = refs[3 * w : 3 * w + 3]
        part = nn(jnp.concatenate([dq[...], dk[...], dv[...]], axis=1), weights).astype(BF16)
        for at, g in enumerate((dq, dv)):
            total = col_sum(g[...].astype(F32))
            sums[at : at + 1, :] = total if w == 0 else sums[at : at + 1, :] + total
        if w == 2:
            buf[...] = part
            keep[n:, :] = buf[pl.ds(pl.multiple_of(c * half, half), half), :]
            send[n:, :] = buf[pl.ds(pl.multiple_of((1 - c) * half, half), half), :]
        else:

            @pl.when(c == w)
            def _():
                keep[:n, :] = part

            @pl.when(c != w)
            def _():
                send[:n, :] = part


def one_call(core, grads, wq, wk, wv):
    c, d = wq.shape
    rows = 3 * WIN // 2
    return pl.pallas_call(
        one_kernel,
        in_specs=[SMEM] + [pl.BlockSpec((WIN, c))] * 9 + [pl.BlockSpec((c, d))] * 3,
        out_specs=[pl.BlockSpec((rows, d))] * 2 + [pl.BlockSpec((8, c))],
        out_shape=[SDS((rows, d), BF16)] * 2 + [SDS((8, c), F32)],
        scratch_shapes=[pltpu.VMEM((WIN, d), BF16)],
        cost_estimate=SHORT,
        compiler_params=params(18),
        name="grad_one",
    )(core, *[g for window in grads for g in window], wq, wk, wv)


def attn_grad_kernel(bits, core, n1a, n1b, mxa, mxb, ga0, ga1, gb0, gb1, *refs):
    i = pl.program_id(0)
    c = mxa.shape[1]
    lowers = (refs[3:6], refs[6:9])
    ka, sa, kb, sb, acc = refs[9:]

    @pl.when(i == 0)
    def _():
        acc[...] = jnp.zeros_like(acc)

    def step(n1, grads, mx, gh):
        acc[: 3 * c, :] += tn(jnp.concatenate([g[...] for g in grads], axis=1), n1[...])
        acc[3 * c :, :] += tn(mx[...], gh[...])

    for at, gh in enumerate((ga0, ga1)):

        @pl.when(i == at)
        def _(gh=gh):
            step(n1a, refs[:3], mxa, gh)

    for at, gh in enumerate((gb0, gb1)):
        for w in range(2):

            @pl.when((i == 2 + at) & (lax.rem(at + core[0], 2) == w))
            def _(gh=gh, w=w):
                step(n1b, lowers[w], mxb, gh)

    @pl.when(i == 3)
    def _():
        rows = acc.shape[0] // 2
        split_store(acc, 0, rows, bits[0], ka, sa)
        split_store(acc, rows, rows, bits[1], kb, sb)


def attn_grad_call(bits, core, n1, mxs, ghs, grads_a, grads_0, grads_1):
    d = n1.shape[1]
    c = mxs[0].shape[1]
    na, nb = mxs[0].shape[0] // 2, mxs[1].shape[0] // 2
    fa = lambda w, o=0: pl.BlockSpec((na, w), lambda i, bits, core: (o + lax.rem(jnp.minimum(i, 1) + core[0], 2), 0))
    fb = lambda w: pl.BlockSpec((nb, w), lambda i, bits, core: (lax.rem(jnp.maximum(i - 2, 0) + core[0], 2), 0))
    return pl.pallas_call(
        attn_grad_kernel,
        grid_spec=pltpu.PrefetchScalarGridSpec(
            num_scalar_prefetch=2,
            grid=(4,),
            in_specs=[fa(d, 2 * nb // na), fb(d), fa(c), fb(c)]
            + [whole((na, d))] * 2
            + [whole((nb, d))] * 2
            + [fa(c)] * 3
            + [whole((nb, c))] * 6,
            out_specs=[whole((c, d))] * 4,
            scratch_shapes=[pltpu.VMEM((4 * c, d), F32)],
        ),
        out_shape=[SDS((c, d), BF16)] * 4,
        cost_estimate=GRAD_HINT,
        compiler_params=params(18),
        name="attn_grad",
    )(bits, core, n1, n1, *mxs, *ghs[0], *ghs[1], *grads_a, *grads_0, *grads_1)


def norm_one_kernel(nb, core, s, x, tok, row, gh_b, gh_a, gain, out, sums):
    i = pl.program_id(0)

    @pl.when(i == 0)
    def _():
        sums[...] = jnp.zeros_like(sums)

    one = s[...].astype(F32) + x[...].astype(F32)
    hat, root = norm_parts(tok[...].astype(F32) + row[...])
    g = jnp.where(i < nb, gh_b[...], gh_a[...]) + norm_back(one * gain[...], hat, root)
    out[...] = g.astype(BF16)
    sums[0:1, :] += col_sum(one * hat)
    sums[1:2, :] += col_sum(one)
    sums[2:3, :] += col_sum(g)


def lower_upper(d, nb):
    lower = pl.BlockSpec((BT, d), lambda i, *_: (jnp.minimum(i, nb - 1), 0))
    upper = pl.BlockSpec((BT, d), lambda i, *_: (jnp.maximum(i - nb, 0), 0))
    return lower, upper


def norm_one_call(core, s, x, tok, row, gh_b, gh_a, gain, hint=SHORT):
    n, d = s.shape
    nb, na = gh_b.shape[0] // BT, gh_a.shape[0] // BT
    at = lambda i, core: jnp.where(i < nb, core[0] * nb + i, 2 * nb + core[0] * na + i - nb)
    return pl.pallas_call(
        functools.partial(norm_one_kernel, nb),
        grid_spec=pltpu.PrefetchScalarGridSpec(
            num_scalar_prefetch=1,
            grid=(nb + na,),
            in_specs=[rows_at(d)] * 2
            + [pl.BlockSpec((BT, d), lambda i, core: (at(i, core), 0)), whole((1, d))]
            + [*lower_upper(d, nb), whole((d,))],
            out_specs=[rows_at(d), whole((8, d))],
        ),
        out_shape=[SDS((n, d), BF16), SDS((8, d), F32)],
        cost_estimate=hint,
        compiler_params=params(16),
        name="norm_one_back",
    )(core, s, x, tok, row, gh_b, gh_a, gain)


def out_kernel(nb, sb, xb, hid_b, sa, xa, hid_a, b_down, out):
    def store(s, x, hid):
        out[...] = (hid[...] + s[...].astype(F32) + x[...].astype(F32) + b_down[...]).astype(BF16)

    @pl.when(pl.program_id(0) < nb)
    def _():
        store(sb, xb, hid_b)

    @pl.when(pl.program_id(0) >= nb)
    def _():
        store(sa, xa, hid_a)


def out_call(sb, xb, hid_b, sa, xa, hid_a, b_down, hint=SHORT):
    n, d = hid_b.shape
    nb, na = n // BT, hid_a.shape[0] // BT
    lower = pl.BlockSpec((BT, d), lambda i: (jnp.minimum(i, nb - 1), 0))
    upper = pl.BlockSpec((BT, d), lambda i: (jnp.maximum(i - nb, 0), 0))
    return pl.pallas_call(
        functools.partial(out_kernel, nb),
        grid=(nb + na,),
        in_specs=[lower] * 3 + [upper] * 3 + [whole((d,))],
        out_specs=rows_at(d),
        out_shape=SDS(((nb + na) * BT, d), BF16),
        cost_estimate=hint,
        compiler_params=params(16),
        name="layer_out",
    )(sb, xb, hid_b, sa, xa, hid_a, b_down)


def out_rows_kernel(core, own, other, out):
    na = WIN // 2
    nb = own.shape[0] - na
    c = core[0]
    for src, half in ((own, c), (other, 1 - c)):
        out[pl.ds(pl.multiple_of(half * nb, 16), nb), :] = src[:nb, :]
        out[pl.ds(pl.multiple_of(2 * nb + half * na, 16), na), :] = src[nb:, :]


def out_rows_call(core, own, other, hint=SHORT):
    n, d = own.shape
    return pl.pallas_call(
        out_rows_kernel,
        in_specs=[SMEM] + [pl.BlockSpec((n, d))] * 2,
        out_specs=pl.BlockSpec((2 * n, d)),
        out_shape=SDS((2 * n, d), BF16),
        cost_estimate=hint,
        compiler_params=params(12),
        name="in_order",
    )(core, own, other)


VALUE_AT = 256
STEP_AT = 512


def pack_kernel(scal, s2a, s2b, s1, so, ffn, out):
    me, step = scal[0], scal[1]
    c = so.shape[1]
    n = out.shape[0] - 8
    out[0:3, :] = s2a[0:3, :] + s2b[0:3, :]
    out[3:5, :] = s1[0:2, :]
    out[5:7, :] = ffn[0:2, :]
    out[7:8, :] = jnp.zeros((1, out.shape[1]), F32)
    out[7:8, 0:c] = so[0:1, :]
    out[7:8, VALUE_AT : VALUE_AT + c] = so[1:2, :]
    lane = lax.broadcasted_iota(jnp.int32, (1, out.shape[1] - STEP_AT), 1)
    out[7:8, STEP_AT:] = jnp.where(lane == me, step.astype(F32), 0.0)
    spot = lax.broadcasted_iota(jnp.int32, (n, 1), 0) == me
    out[8:, :] = jnp.where(spot, s1[2:3, :], 0.0)


def pack_call(scal, n_dp, s2a, s2b, s1, so, ffn, hint=SHORT):
    d = ffn.shape[1]
    rows = 8 + -(-n_dp // 8) * 8
    return pl.pallas_call(
        pack_kernel,
        in_specs=[SMEM] + [pl.BlockSpec(v.shape) for v in (s2a, s2b, s1, so, ffn)],
        out_specs=pl.BlockSpec((rows, d)),
        out_shape=SDS((rows, d), F32),
        cost_estimate=hint,
        compiler_params=params(4),
        name="pack",
    )(scal, s2a, s2b, s1, so, ffn)


def small_add_kernel(own_rows, a, b, out):
    out[...] = a[...] + b[...]
    if own_rows:
        out[5:8, :] = a[5:8, :]


def small_add(a, b, own_rows=False):
    return pl.pallas_call(
        functools.partial(small_add_kernel, own_rows),
        in_specs=[pl.BlockSpec(a.shape)] * 2,
        out_specs=pl.BlockSpec(a.shape),
        out_shape=SDS(a.shape, F32),
        cost_estimate=SHORT,
        compiler_params=params(4),
        name="small_add",
    )(a, b)


def unpack_kernel(n_dp, small, got, *outs):
    table, vecs, bq, bv, full = outs[0], outs[1:8], outs[8], outs[9], outs[10]
    full[...] = small[...] + got[...]
    for n, vec in enumerate(vecs):
        vec[...] = full[n, :]
    c = bq.shape[0]
    bq[...] = full[7, 0:c]
    bv[...] = full[7, VALUE_AT : VALUE_AT + c]
    table[...] = jnp.zeros_like(table)
    steps = full[7:8, STEP_AT:]
    lane = lax.broadcasted_iota(jnp.int32, steps.shape, 1)
    for n in range(n_dp):
        at = jnp.sum(jnp.where(lane == n, steps, 0.0)).astype(jnp.int32)
        table[pl.ds(at, 1), :] += full[8 + n : 9 + n, :]


def unpack_call(n_dp, table_rows, c, small, got):
    rows, d = small.shape
    shapes = [(table_rows, d)] + [(d,)] * 7 + [(c,)] * 2
    return pl.pallas_call(
        functools.partial(unpack_kernel, n_dp),
        in_specs=[pl.BlockSpec(small.shape)] * 2,
        out_specs=[pl.BlockSpec(s) for s in shapes],
        out_shape=[SDS(s, F32) for s in shapes],
        scratch_shapes=[pltpu.VMEM(small.shape, F32)],
        cost_estimate=SHORT,
        compiler_params=params(10),
        name="unpack",
    )(small, got)


def after(token, value):
    return lax.optimization_barrier((token, value))[1]


class Spread:
    def __init__(self, n_dp, bits, orders, keep, send):
        self.n_dp, self.bits, self.orders, self.level = n_dp, bits, orders, 2
        self.keep = keep
        self.swap(0, send)

    def swap(self, level, values):
        self.got = [
            lax.ppermute(v, "dp", [(i, i ^ (1 << order[level])) for i in range(self.n_dp)])
            for v, order in zip(values, self.orders)
        ]

    def step(self, token, kernel, name, bits, shapes, hint, scratch=()):
        keep = [after(token, self.keep[0]), *self.keep[1:]]
        arrays = [a for pair in zip(keep, self.got) for a in pair]
        return step_call(kernel, name, bits, arrays, shapes, hint, scratch)

    def halve(self, token, hint=SHORT):
        n, d = self.keep[0].shape
        half = [SDS((n // 2, d), BF16)] * (2 * len(self.keep))
        out = self.step(token, halve_kernel, "halve", self.bits, half, hint, [pltpu.VMEM((n, d), F32)])
        self.keep = out[0::2]
        self.swap(1, out[1::2])
        return self.keep[0]

    def exchange(self, token, hint=SHORT):
        same = [SDS(k.shape, BF16) for k in self.keep]
        self.keep = self.step(token, add_kernel, "pair_add", None, same, hint)
        self.swap(self.level if self.level < len(self.orders[0]) else 1, self.keep)
        self.level += 1
        return self.keep[0]

    def join(self, token, hint=SHORT):
        n, d = self.keep[0].shape
        self.keep = self.step(token, join_kernel, "join", None, [SDS((2 * n, d), BF16)] * len(self.keep), hint)
        self.swap(0, self.keep)
        return self.keep[0]

    def place(self, token, pieces, hint=SHORT):
        n, d = self.keep[0].shape
        rows = 2 * n * len(self.keep) // pieces
        return self.step(token, place_kernel, "place", self.bits, [SDS((rows, d), F32)] * pieces, hint)


def per_device(
    n_tensor,
    n_dp,
    tokens,
    timesteps,
    piece_starts,
    step_table,
    first_gain,
    first_shift,
    w_query,
    b_query,
    w_key,
    w_value,
    b_value,
    w_out,
    b_out,
    second_gain,
    second_shift,
    w_in,
    b_in,
    w_down,
    b_down,
    cotangent,
):
    length, d = tokens.shape[1:]
    c = w_query.shape[1]
    rank = lax.axis_index("tensor").astype(jnp.int32)
    me = lax.axis_index("dp").astype(jnp.int32)
    over_x = [(i, i ^ 2) for i in range(n_tensor)]
    over_core = [(i, i ^ 1) for i in range(n_tensor)]
    swap_x = lambda v: lax.ppermute(v, "tensor", over_x)
    swap_core = lambda v: lax.ppermute(v, "tensor", over_core)
    n_bits = n_dp.bit_length() - 1
    orders = (list(range(n_bits)), list(range(1, n_bits)) + [0])
    bit = lambda b: (me >> b) & 1
    bits = jnp.stack([bit(orders[0][0]), bit(orders[1][0]), bit(orders[0][1]), bit(orders[1][1])])
    scal = jnp.stack([me, timesteps[0]])
    core = (rank & 1)[None]
    tok, bits, scal, core, starts = lax.optimization_barrier((tokens[0], bits, scal, core, piece_starts[0]))
    cot = cotangent[0]
    wq, wk, wv = w_query.T, w_key.T, w_value.T

    top = length // WIN - 1
    groups = [[top], list(range(top - 1, -1, -1))]
    row0s = [top * WIN, 0]
    hbm = lambda v: pltpu.with_memory_space_constraint(v, pltpu.HBM)

    n1, q, k, v, row = qkv_call(
        timesteps, *[hbm(z) for z in (tok, step_table, first_gain, first_shift, wq, wk, wv, b_query, b_value)]
    )
    wo0 = w_out
    wo2 = swap_x(after(n1, w_out))
    mix_a, lse_a = attn_fwd_call(starts, q, k, v, groups[0])
    wo1 = swap_core(after(mix_a, w_out))
    wo3 = swap_core(after(mix_a, wo2))
    wos = [wo0, wo2, wo1, wo3]
    m1_a, m2_a = swap_core(mix_a), swap_x(mix_a)
    mix_b, lse_b = attn_fwd_call(starts, after(mix_a, q), k, v, groups[1])
    m3_a = swap_core(after(mix_b, m2_a))
    m2_b = swap_x(mix_b)

    def ffn_of(ms, n):
        return ffn_call(
            core, ms, tok, row, cot, wos, b_out, second_gain, second_shift, w_in, b_in, w_down, row0s[n]
        )

    hid_a, n2_a, act_a, gpre_a, keep_a, send_a = ffn_of([mix_a, m2_a, m1_a, m3_a], 0)
    got_a = swap_core(send_a)
    first = ffn_grad_call(bits, core, n2_a, gpre_a, act_a, cot, row0s[0])
    pair_b = stack_call(after(first[2], mix_b), m2_b)
    far_b = swap_core(pair_b)
    two_a = half_sum(after(pair_b, keep_a), got_a, 0)
    twox_a = swap_x(two_a)
    mlp_a = half_sum(after(two_a, keep_a), got_a, 1)
    hid_b, n2_b, act_b, gpre_b, keep_b, send_b = ffn_of([after(mlp_a, mix_b), m2_b, far_b], 1)
    got_b = swap_core(send_b)
    gh_a, ghb_a, s2_a = norm_two_call(core, after(n2_b, two_a), twox_a, hid_a, cot, second_gain, row0s[0])
    gho_a = swap_core(ghb_a)
    mlpx_a = swap_x(after(twox_a, mlp_a))
    ka, sa, kb, sb, ffn_sums = ffn_grad_call(
        bits, core, after(ghb_a, n2_b), gpre_b, act_b, cot, row0s[1], first, LONG
    )
    gff = Spread(n_dp, bits, orders, [ka, kb], [sa, sb])
    two_b = half_sum(after(ka, keep_b), got_b, 0)
    twox_b = swap_x(two_b)
    *grads_a, dkf, dvf = attn_bwd_call(
        starts, core, after((two_b, mlpx_a), q), k, v, ghb_a, gho_a, w_out, lse_a, None, top, groups[0]
    )
    t = gff.halve(grads_a[0])
    gh_b, ghb_b, s2_b = norm_two_call(core, after(t, two_b), twox_b, hid_b, cot, second_gain, row0s[1], LONG)
    gho_b = swap_core(ghb_b)
    mlp_b = half_sum(after(ghb_b, keep_b), got_b, 1, LONG)
    mlpx_b = swap_x(mlp_b)
    *grads_1, dkf, dvf = attn_bwd_call(
        starts, core, after(mlp_b, q), k, v, ghb_b, gho_b, w_out, lse_b, (dkf, dvf), 1, groups[1]
    )
    t = gff.exchange(grads_1[0])
    grads_0 = attn_bwd_call(
        starts, core, after(t, q), k, v, ghb_b, gho_b, w_out, lse_b, (dkf, dvf), 0, groups[1], SHORT
    )
    one, osend, so = one_call(core, [grads_0, grads_1, grads_a], wq, wk, wv)
    ogot = swap_core(osend)
    ka, sa, kb, sb = attn_grad_call(
        bits, core, after(one, n1), (mix_a, mix_b), ((ghb_a, gho_a), (ghb_b, gho_b)), grads_a, grads_0, grads_1
    )
    gat = Spread(n_dp, bits, orders, [ka, kb], [sa, sb])
    t = (ka, mlpx_b)
    for _ in range(n_bits - 2):
        t = gff.exchange(t, LONG)
    os_b = one_sum(after(t, one), ogot)
    ox_b = swap_x(os_b)
    t = gat.halve(os_b)
    t = gff.join(t)
    t = gat.exchange(t)
    gt, s1 = norm_one_call(core, after(t, os_b), ox_b, tok, row, gh_b, gh_a, first_gain, LONG)
    small = pack_call(after(gt, scal), n_dp, s2_a, s2_b, s1, so, ffn_sums)
    swapped = swap_core(small)
    t = small
    for _ in range(n_bits - 2):
        t = gat.exchange(t)
    small = small_add(after(t, small), swapped, True)
    swap_dp = lambda v, b: lax.ppermute(v, "dp", [(i, i ^ (1 << b)) for i in range(n_dp)])
    got = swap_dp(small, 0)
    g_in, g_down = gff.place(small, 2, LONG)
    small = small_add(after(g_in, small), got)
    got = swap_dp(small, 1)
    t = gat.join(small, LONG)
    small = after(t, small)
    for b in range(2, n_bits):
        small = small_add(small, got)
        got = swap_dp(small, b)
    o = out_call(after(small, mlp_b), mlpx_b, hid_b, mlp_a, mlpx_a, hid_a, b_down, LONG)
    oo, gto = swap_core(o), swap_core(after(o, gt))
    grad_tokens = out_rows_call(core, gt, gto)
    output = out_rows_call(core, after(grad_tokens, o), oo)
    g_table, g_sg, g_ss, g_bo, g_fg, g_fs, g_bi, g_bd, g_bq, g_bv = unpack_call(
        n_dp, step_table.shape[0], c, after(output, small), got
    )
    g_q, g_k, g_v, g_o = gat.place(g_sg, 4)
    return (
        output[None],
        grad_tokens[None],
        g_table,
        g_fg,
        g_fs,
        g_q.T,
        g_bq,
        g_k.T,
        g_v.T,
        g_bv,
        g_o,
        g_bo,
        g_sg,
        g_ss,
        g_in,
        g_bi,
        g_down,
        g_bd,
    )


def solution(mesh):
    in_specs = (
        P("dp", None, None),
        P("dp"),
        P("dp", None),
        P(),
        P(),
        P(),
        P(None, "tensor"),
        P("tensor"),
        P(None, "tensor"),
        P(None, "tensor"),
        P("tensor"),
        P("tensor", None),
        P(),
        P(),
        P(),
        P(None, "tensor"),
        P("tensor"),
        P("tensor", None),
        P(),
        P("dp", None, None),
    )
    out_specs = (
        P("dp", None, None),
        P("dp", None, None),
        P(),
        P(),
        P(),
        P(None, "tensor"),
        P("tensor"),
        P(None, "tensor"),
        P(None, "tensor"),
        P("tensor"),
        P("tensor", None),
        P(),
        P(),
        P(),
        P(None, "tensor"),
        P("tensor"),
        P("tensor", None),
        P(),
    )
    return jax.shard_map(
        functools.partial(per_device, mesh.shape["tensor"], mesh.shape["dp"]),
        mesh=mesh,
        in_specs=in_specs,
        out_specs=out_specs,
        check_vma=False,
    )
```

```python
import functools

import jax
import jax.numpy as jnp
from jax import lax
from jax.experimental import pallas as pl
from jax.experimental.pallas import tpu as pltpu
from jax.sharding import PartitionSpec as P

HD = 64
PIECE = 256
WIN = 2 * PIECE
EPS = 1e-05
BT = 256
F32 = jnp.float32
BF16 = jnp.bfloat16
SDS = jax.ShapeDtypeStruct
SCALE = HD ** (-0.5)
GELU_C = 0.7978845608028654


def nn(a, b):
    return lax.dot_general(a, b, (((1,), (0,)), ((), ())), preferred_element_type=F32)


def nt(a, b):
    return lax.dot_general(a, b, (((1,), (1,)), ((), ())), preferred_element_type=F32)


def tn(a, b):
    return lax.dot_general(a, b, (((0,), (0,)), ((), ())), preferred_element_type=F32)


def norm_parts(v):
    c = v - jnp.mean(v, axis=-1, keepdims=True)
    root = lax.rsqrt(jnp.mean(c * c, axis=-1, keepdims=True) + EPS)
    return c * root, root


def norm_back(e, hat, root):
    return root * (
        e - jnp.mean(e, axis=-1, keepdims=True) - hat * jnp.mean(e * hat, axis=-1, keepdims=True)
    )


def col_sum(v):
    return jnp.sum(v, axis=0, keepdims=True)


def whole(shape):
    return pl.BlockSpec(shape, lambda i, *_: (0,) * len(shape))


def rows_at(width, offset=0, block=BT):
    return pl.BlockSpec((block, width), lambda i, *_: (offset + i, 0))


LONG = pl.CostEstimate(flops=10**11, bytes_accessed=1000, transcendentals=0)
SHORT = pl.CostEstimate(flops=1000, bytes_accessed=1000, transcendentals=0)
GRAD_HINT = LONG


def params(mib=12):
    return pltpu.CompilerParams(vmem_limit_bytes=mib * 1024 * 1024)


SMEM = pl.BlockSpec(memory_space=pltpu.SMEM)


def qkv_kernel(steps, tok, table, gain, shift, wq, wk, wv, bq, bv, n1, q, k, v, row):
    rows = table[...].astype(F32)
    at = lax.broadcasted_iota(jnp.int32, rows.shape, 0) == lax.rem(steps[0], 8)
    step_row = col_sum(jnp.where(at, rows, 0.0))
    row[...] = step_row
    hat, _ = norm_parts(tok[...].astype(F32) + step_row)
    n = (hat * gain[...] + shift[...]).astype(BF16)
    n1[...] = n
    q[...] = ((nt(n, wq[...]) + bq[...]) * SCALE).astype(BF16)
    k[...] = nt(n, wk[...]).astype(BF16)
    v[...] = (nt(n, wv[...]) + bv[...]).astype(BF16)


def qkv_call(steps, tok, table, gain, shift, wq, wk, wv, bq, bv):
    length, d = tok.shape
    c = wq.shape[0]
    return pl.pallas_call(
        qkv_kernel,
        grid_spec=pltpu.PrefetchScalarGridSpec(
            num_scalar_prefetch=1,
            grid=(length // WIN,),
            in_specs=[rows_at(d, block=WIN), pl.BlockSpec((8, d), lambda i, steps: (steps[0] // 8, 0))]
            + [whole((d,))] * 2
            + [whole((c, d))] * 3
            + [whole((c,))] * 2,
            out_specs=[rows_at(d, block=WIN)] + [rows_at(c, block=WIN)] * 3 + [whole((1, d))],
        ),
        out_shape=[SDS((length, d), BF16)] + [SDS((length, c), BF16)] * 3 + [SDS((1, d), F32)],
        cost_estimate=LONG,
        compiler_params=params(16),
        name="norm_qkv",
    )(steps, tok, table, gain, shift, wq, wk, wv, bq, bv)


def attn_fwd_window(win, nh, starts, q, k, v, mix, lse):
    base = win * WIN
    start = starts[win]
    qpos = base + lax.broadcasted_iota(jnp.int32, (WIN, 1), 0)
    limit = jnp.where((qpos >= start) & (qpos < start + PIECE), start + PIECE - 1, qpos)
    kpos = base + lax.broadcasted_iota(jnp.int32, (1, WIN), 1)
    allow = kpos <= limit
    for h in range(nh):
        cols = slice(h * HD, (h + 1) * HD)
        qh = q[:, cols]
        near = jnp.where(allow, nt(qh, k[base : base + WIN, cols]), -1e30)
        top = jnp.max(near, axis=-1, keepdims=True)
        if win:
            far = nt(qh, k[:base, cols])
            top = jnp.maximum(top, jnp.max(far, axis=-1, keepdims=True))
        pn = jnp.exp(near - top)
        total = jnp.sum(pn, axis=-1, keepdims=True)
        out = nn(pn.astype(BF16), v[base : base + WIN, cols])
        if win:
            pf = jnp.exp(far - top)
            total = total + jnp.sum(pf, axis=-1, keepdims=True)
            out = out + nn(pf.astype(BF16), v[:base, cols])
        mix[:, cols] = (out / total).astype(BF16)
        stat = jnp.broadcast_to(top + jnp.log(total), (WIN, 128))
        lse[h : h + 1, :] = jnp.transpose(stat)[0:1, :]


def attn_fwd_kernel(wins, nh, starts, *refs):
    for n, win in enumerate(wins):

        @pl.when(pl.program_id(0) == n)
        def _(win=win):
            attn_fwd_window(win, nh, starts, *refs)


def attn_fwd_call(starts, q, k, v, wins):
    c = q.shape[1]
    kv = (wins[0] + 1) * WIN
    n = len(wins) * WIN
    return pl.pallas_call(
        functools.partial(attn_fwd_kernel, wins, c // HD),
        grid=(len(wins),),
        in_specs=[SMEM, pl.BlockSpec((WIN, c), lambda i: (wins[0] - i, 0)), whole((kv, c)), whole((kv, c))],
        out_specs=[
            pl.BlockSpec((WIN, c), lambda i: (wins[0] - wins[-1] - i, 0)),
            pl.BlockSpec((8, WIN), lambda i: (0, wins[0] - wins[-1] - i)),
        ],
        out_shape=[SDS((n, c), BF16), SDS((8, n), F32)],
        cost_estimate=LONG,
        compiler_params=params(20),
        name="attn_fwd",
    )(starts, q, k, v)


def stack_kernel(a, b, out):
    c = a.shape[1]
    out[:, :c] = a[...]
    out[:, c:] = b[...]


def stack_call(a, b):
    n, c = a.shape
    return pl.pallas_call(
        stack_kernel,
        in_specs=[pl.BlockSpec((n, c))] * 2,
        out_specs=pl.BlockSpec((n, 2 * c)),
        out_shape=SDS((n, 2 * c), BF16),
        cost_estimate=LONG,
        compiler_params=params(6),
        name="stack",
    )(a, b)


def ffn_kernel(
    pieces, core, *refs
):
    kept, sent, wos = refs[:pieces], refs[pieces : 2 * pieces], refs[2 * pieces + 5 : 2 * pieces + 9]
    tok_k, tok_s, row, cot_k, cot_s = refs[2 * pieces : 2 * pieces + 5]
    b_out, gain, shift, w_in, b_in, w_down, hid, n2, act, gpre, keep, send = refs[2 * pieces + 9 :]
    rows = tok_k.shape[0]
    both = lambda a, b: jnp.concatenate([a[...], b[...]], axis=0)
    mixed = jnp.concatenate([both(a, b) for a, b in zip(kept, sent)], axis=1)
    attn = nn(mixed, jnp.concatenate([w[...] for w in wos], axis=0))
    h = both(tok_k, tok_s).astype(F32) + row[...] + attn + b_out[...]
    hid[...] = h[:rows]
    hat, _ = norm_parts(h)
    n = (hat * gain[...] + shift[...]).astype(BF16)
    z = nn(n, w_in[...]) + b_in[...]
    z2 = z * z
    th = jnp.tanh(z * (GELU_C + (GELU_C * 0.044715) * z2))
    half = 0.5 * (1.0 + th)
    a = (z * half).astype(BF16)
    slope = half + (0.5 * z) * (1.0 - th * th) * (GELU_C + (3.0 * 0.044715 * GELU_C) * z2)
    gp = (nt(both(cot_k, cot_s), w_down[...]) * slope).astype(BF16)
    mlp = nn(a, w_down[...]).astype(BF16)
    two = nt(gp, w_in[...]).astype(BF16)
    for part, at in enumerate((slice(0, rows), slice(rows, 2 * rows))):
        n2[part] = n[at]
        act[part] = a[at]
        gpre[part] = gp[at]
        out = send if part else keep
        out[0] = two[at]
        out[1] = mlp[at]


def half_spec(width, nb, own, offset=0):
    return pl.BlockSpec((BT, width), lambda i, core: (offset + (core[0] if own else 1 - core[0]) * nb + i, 0))


def stacked(width, block=BT):
    return pl.BlockSpec((2, block, width), lambda i, *_: (0, i, 0))


def ffn_call(core, ms, tok, row, cot, wos, b_out, gain, shift, w_in, b_in, w_down, row0):
    n = ms[0].shape[0]
    c, d = wos[0].shape
    u = w_in.shape[1]
    h = n // 2
    nb = h // BT
    off = row0 // BT
    kept = functools.partial(half_spec, nb=nb, own=True)
    sent = functools.partial(half_spec, nb=nb, own=False)
    return pl.pallas_call(
        functools.partial(ffn_kernel, len(ms)),
        grid_spec=pltpu.PrefetchScalarGridSpec(
            num_scalar_prefetch=1,
            grid=(nb,),
            in_specs=[kept(v.shape[1]) for v in ms]
            + [sent(v.shape[1]) for v in ms]
            + [kept(d, offset=off), sent(d, offset=off), whole((1, d)), kept(d, offset=off), sent(d, offset=off)]
            + [whole((c, d))] * 4
            + [whole((d,))] * 3
            + [whole((d, u)), whole((u,)), whole((u, d))],
            out_specs=[rows_at(d), stacked(d), stacked(u), stacked(u), stacked(d), stacked(d)],
        ),
        out_shape=[SDS((h, d), F32), SDS((2, h, d), BF16)]
        + [SDS((2, h, u), BF16)] * 2
        + [SDS((2, h, d), BF16)] * 2,
        cost_estimate=LONG,
        compiler_params=params(24),
        name="ffn",
    )(core, *ms, *ms, tok, tok, row, cot, cot, *wos, b_out, gain, shift, w_in, b_in, w_down)


def split_store(acc, first, rows, bit, keep, send):
    half = rows // 2
    keep[...] = acc[pl.ds(pl.multiple_of(first + bit * half, 16), half), :].astype(BF16)
    send[...] = acc[pl.ds(pl.multiple_of(first + (1 - bit) * half, 16), half), :].astype(BF16)


def halve_kernel(parts, bits, *refs):
    ins, outs, acc = refs[: 2 * parts], refs[2 * parts : 4 * parts], refs[4 * parts]
    for part in range(parts):
        acc[...] = ins[2 * part][...].astype(F32) + ins[2 * part + 1][...].astype(F32)
        split_store(acc, 0, acc.shape[0], bits[2 + part], outs[2 * part], outs[2 * part + 1])


def add_kernel(parts, *refs):
    for part in range(parts):
        k, r = refs[2 * part : 2 * part + 2]
        refs[2 * parts + part][...] = (k[...].astype(F32) + r[...].astype(F32)).astype(BF16)


def join_kernel(parts, *refs):
    for part in range(parts):
        s, r = refs[2 * part : 2 * part + 2]
        n = s.shape[0]
        refs[2 * parts + part][:n, :] = s[...]
        refs[2 * parts + part][n:, :] = r[...]


def place_kernel(parts, bits, *refs):
    outs = refs[2 * parts :]
    per = len(outs) // parts
    for part in range(parts):
        p, r = refs[2 * part : 2 * part + 2]
        n = p.shape[0] // 2
        b0, b1 = bits[part], bits[2 + part]
        for src, first in ((p, b0), (r, 1 - b0)):
            for which in range(2):

                @pl.when(first == which)
                def _(src=src, which=which):
                    out = outs[part if per == 1 else 2 * part + which]
                    for sub, second in ((0, b1), (1, 1 - b1)):
                        at = pl.multiple_of(second * n, 8) + (2 * n * which if per == 1 else 0)
                        out[pl.ds(at, n), :] = src[sub * n : (sub + 1) * n, :].astype(F32)


def step_call(kernel, name, bits, arrays, shapes, hint, scratch=()):
    parts = len(arrays) // 2
    return pl.pallas_call(
        functools.partial(kernel, parts),
        in_specs=([] if bits is None else [SMEM]) + [pl.BlockSpec(a.shape) for a in arrays],
        out_specs=[pl.BlockSpec(s.shape) for s in shapes],
        out_shape=shapes,
        scratch_shapes=scratch,
        cost_estimate=hint,
        compiler_params=params(14),
        name=name,
    )(*([] if bits is None else [bits]), *arrays)


def one_sum_kernel(keep, got, out):
    out[...] = (keep[...].astype(F32) + got[...].astype(F32)).astype(BF16)


def one_sum(keep, got, hint=SHORT):
    return pl.pallas_call(
        one_sum_kernel,
        in_specs=[pl.BlockSpec(keep.shape)] * 2,
        out_specs=pl.BlockSpec(keep.shape),
        out_shape=SDS(keep.shape, BF16),
        cost_estimate=hint,
        compiler_params=params(8),
        name="one_sum",
    )(keep, got)


def half_sum_kernel(keep, got, out):
    out[...] = (keep[0].astype(F32) + got[0].astype(F32)).astype(BF16)


def half_sum(keep, got, which, hint=SHORT):
    _, n, d = keep.shape
    part = pl.BlockSpec((1, n, d), lambda i: (which, 0, 0))
    return pl.pallas_call(
        half_sum_kernel,
        grid=(1,),
        in_specs=[part, part],
        out_specs=whole((n, d)),
        out_shape=SDS((n, d), BF16),
        cost_estimate=hint,
        compiler_params=params(8),
        name="half_sum",
    )(keep, got)


def ffn_grad_step(n2, gp, ac, cot_k, cot_s, acc_in, acc_down, sums):
    flat = lambda ref: ref[...].reshape(2 * ref.shape[1], ref.shape[2])
    cot = jnp.concatenate([cot_k[...], cot_s[...]], axis=0)
    g = flat(gp)
    acc_in[...] += tn(flat(n2), g)
    acc_down[...] += tn(flat(ac), cot)
    sums[0:1, :] += col_sum(g.astype(F32))
    sums[1:2, :] += col_sum(cot.astype(F32))


def ffn_grad_first_kernel(core, n2, gp, ac, cot_k, cot_s, acc_in, acc_down, sums):
    for ref in (acc_in, acc_down, sums):
        ref[...] = jnp.zeros_like(ref)
    ffn_grad_step(n2, gp, ac, cot_k, cot_s, acc_in, acc_down, sums)


def ffn_grad_last_kernel(bits, core, n2, gp, ac, cot_k, cot_s, in0, down0, sums0, ka, sa, kb, sb, sums, acc_in, acc_down):
    @pl.when(pl.program_id(0) == 0)
    def _():
        acc_in[...] = in0[...]
        acc_down[...] = down0[...]
        sums[...] = sums0[...]

    ffn_grad_step(n2, gp, ac, cot_k, cot_s, acc_in, acc_down, sums)

    @pl.when(pl.program_id(0) == pl.num_programs(0) - 1)
    def _():
        split_store(acc_in, 0, acc_in.shape[0], bits[0], ka, sa)
        split_store(acc_down, 0, acc_down.shape[0], bits[1], kb, sb)


def ffn_grad_call(bits, core, n2, gp, ac, cot, row0, before=None, hint=SHORT):
    _, h, d = n2.shape
    u = gp.shape[2]
    nb = h // BT
    block = lambda w: pl.BlockSpec((2, BT, w), lambda i, *_: (0, i, 0))

    def cot_spec(own):
        return pl.BlockSpec(
            (BT, d), lambda i, *s: (row0 // BT + (s[-1][0] if own else 1 - s[-1][0]) * nb + i, 0)
        )

    sums = [(d, u), (u, d), (8, d)]
    last = before is not None
    outs = [(d // 2, u)] * 2 + [(u // 2, d)] * 2 + [(8, d)] if last else sums
    types = [BF16] * 4 + [F32] if last else [F32] * 3
    return pl.pallas_call(
        ffn_grad_last_kernel if last else ffn_grad_first_kernel,
        grid_spec=pltpu.PrefetchScalarGridSpec(
            num_scalar_prefetch=2 if last else 1,
            grid=(nb,),
            in_specs=[block(d), block(u), block(u), cot_spec(True), cot_spec(False)]
            + ([whole(s) for s in sums] if last else []),
            out_specs=[whole(s) for s in outs],
            scratch_shapes=[pltpu.VMEM(s, F32) for s in sums[:2]] if last else [],
        ),
        out_shape=[SDS(s, t) for s, t in zip(outs, types)],
        cost_estimate=hint,
        compiler_params=params(24 if last else 16),
        name="ffn_grad",
    )(*([bits] if last else []), core, n2, gp, ac, cot, cot, *(before or ()))


def norm_two_kernel(core, s, x, hid, cot, gain, gh, ghb, sums):
    @pl.when(pl.program_id(0) == 0)
    def _():
        sums[...] = jnp.zeros_like(sums)

    two = s[...].astype(F32) + x[...].astype(F32)
    hat, root = norm_parts(hid[...])
    g = cot[...].astype(F32) + norm_back(two * gain[...], hat, root)
    gh[...] = g
    ghb[...] = g.astype(BF16)
    sums[0:1, :] += col_sum(two * hat)
    sums[1:2, :] += col_sum(two)
    sums[2:3, :] += col_sum(g)


def half_rows(d, n, row0):
    return pl.BlockSpec((BT, d), lambda i, core: (row0 // BT + core[0] * (n // BT) + i, 0))


def norm_two_call(core, s, x, hid, cot, gain, row0, hint=SHORT):
    n, d = hid.shape
    return pl.pallas_call(
        norm_two_kernel,
        grid_spec=pltpu.PrefetchScalarGridSpec(
            num_scalar_prefetch=1,
            grid=(n // BT,),
            in_specs=[rows_at(d)] * 3 + [half_rows(d, n, row0), whole((d,))],
            out_specs=[rows_at(d)] * 2 + [whole((8, d))],
        ),
        out_shape=[SDS((n, d), F32), SDS((n, d), BF16), SDS((8, d), F32)],
        cost_estimate=hint,
        compiler_params=params(16),
        name="norm_two_back",
    )(core, s, x, hid, cot, gain)


def attn_bwd_kernel(win, low, wins, nh, carried, starts, core, q, k, v, mine, other, w_out, lse, *rest):
    if carried:
        dk0, dv0, rest = rest[0], rest[1], rest[2:]
    dq, dk, dv = rest[:3]
    gm = rest[-1]
    base = win * WIN
    near = slice(base, base + WIN)
    grad = lambda ref: nt(ref[...], w_out[...]).astype(BF16)
    if wins == 1:
        half = WIN // 2
        gm[pl.ds(pl.multiple_of(core[0] * half, half), half), :] = grad(mine)
        gm[pl.ds(pl.multiple_of((1 - core[0]) * half, half), half), :] = grad(other)
    else:

        @pl.when(core[0] == win - low)
        def _():
            gm[...] = grad(mine)

        @pl.when(core[0] != win - low)
        def _():
            gm[...] = grad(other)

    start = starts[win]
    qpos = base + lax.broadcasted_iota(jnp.int32, (1, WIN), 1)
    limit = jnp.where((qpos >= start) & (qpos < start + PIECE), start + PIECE - 1, qpos)
    kpos = base + lax.broadcasted_iota(jnp.int32, (WIN, 1), 0)
    allow = kpos <= limit
    for h in range(nh):
        cols = slice(h * HD, (h + 1) * HD)
        qh = q[near, cols]
        gh = gm[:, cols]
        ls = lse[h : h + 1, (win - low) * WIN : (win - low + 1) * WIN]
        pn = jnp.exp(jnp.where(allow, nt(k[near, cols], qh), -1e30) - ls)
        dpn = nt(v[near, cols], gh)
        centre = col_sum(pn * dpn)
        if win:
            pf = jnp.exp(nt(k[:base, cols], qh) - ls)
            dpf = nt(v[:base, cols], gh)
            centre = centre + col_sum(pf * dpf)
        dsn = (pn * (dpn - centre)).astype(BF16)
        dqt = tn(k[near, cols], dsn)
        dkn = nn(dsn, qh)
        dvn = nn(pn.astype(BF16), gh)
        if carried:
            dkn = dkn + dk0[near, cols]
            dvn = dvn + dv0[near, cols]
        dk[:, cols] = dkn.astype(BF16)
        dv[:, cols] = dvn.astype(BF16)
        if win:
            dsf = (pf * (dpf - centre)).astype(BF16)
            dqt = dqt + tn(k[:base, cols], dsf)
            dkf = nn(dsf, qh)
            dvf = nn(pf.astype(BF16), gh)
            if carried:
                dkf = dkf + dk0[:base, cols]
                dvf = dvf + dv0[:base, cols]
            rest[3][:, cols] = dkf
            rest[4][:, cols] = dvf
        dq[:, cols] = jnp.transpose((dqt.astype(BF16).astype(F32) * SCALE)).astype(BF16)


def attn_bwd_call(starts, core, q, k, v, mine, other, w_out, lse, carry, win, group, hint=LONG):
    c, d = w_out.shape
    carried = carry is not None
    kv = (win + 1) * WIN
    full = lambda a: pl.BlockSpec(a.shape, lambda *_: (0,) * a.ndim)
    first = pl.BlockSpec((kv, c), lambda *_: (0, 0))
    shapes = [SDS((WIN, c), BF16)] * 3 + ([SDS((win * WIN, c), F32)] * 2 if win else [])
    return pl.pallas_call(
        functools.partial(attn_bwd_kernel, win, group[-1], len(group), c // HD, carried),
        grid=(1,),
        in_specs=[SMEM, SMEM, first, first, first, full(mine), full(other), full(w_out), full(lse)]
        + ([first] * 2 if carried else []),
        out_specs=[full(s) for s in shapes],
        out_shape=shapes,
        scratch_shapes=[pltpu.VMEM((WIN, c), BF16)],
        cost_estimate=hint,
        compiler_params=params(24),
        name="attn_bwd",
    )(starts, core, q, k, v, mine, other, w_out, lse, *(carry if carried else ()))


def one_kernel(core, *refs):
    wq, wk, wv, keep, send, sums, buf = refs[9:]
    c = core[0]
    n = buf.shape[0]
    half = n // 2
    weights = jnp.concatenate([wq[...], wk[...], wv[...]], axis=0)
    for w in range(3):
        dq, dk, dv = refs[3 * w : 3 * w + 3]
        part = nn(jnp.concatenate([dq[...], dk[...], dv[...]], axis=1), weights).astype(BF16)
        for at, g in enumerate((dq, dv)):
            total = col_sum(g[...].astype(F32))
            sums[at : at + 1, :] = total if w == 0 else sums[at : at + 1, :] + total
        if w == 2:
            buf[...] = part
            keep[n:, :] = buf[pl.ds(pl.multiple_of(c * half, half), half), :]
            send[n:, :] = buf[pl.ds(pl.multiple_of((1 - c) * half, half), half), :]
        else:

            @pl.when(c == w)
            def _():
                keep[:n, :] = part

            @pl.when(c != w)
            def _():
                send[:n, :] = part


def one_call(core, grads, wq, wk, wv):
    c, d = wq.shape
    rows = 3 * WIN // 2
    return pl.pallas_call(
        one_kernel,
        in_specs=[SMEM] + [pl.BlockSpec((WIN, c))] * 9 + [pl.BlockSpec((c, d))] * 3,
        out_specs=[pl.BlockSpec((rows, d))] * 2 + [pl.BlockSpec((8, c))],
        out_shape=[SDS((rows, d), BF16)] * 2 + [SDS((8, c), F32)],
        scratch_shapes=[pltpu.VMEM((WIN, d), BF16)],
        cost_estimate=SHORT,
        compiler_params=params(18),
        name="grad_one",
    )(core, *[g for window in grads for g in window], wq, wk, wv)


def attn_grad_kernel(bits, core, n1a, n1b, mxa, mxb, ga0, ga1, gb0, gb1, *refs):
    i = pl.program_id(0)
    c = mxa.shape[1]
    lowers = (refs[3:6], refs[6:9])
    ka, sa, kb, sb, acc = refs[9:]

    @pl.when(i == 0)
    def _():
        acc[...] = jnp.zeros_like(acc)

    def step(n1, grads, mx, gh):
        acc[: 3 * c, :] += tn(jnp.concatenate([g[...] for g in grads], axis=1), n1[...])
        acc[3 * c :, :] += tn(mx[...], gh[...])

    for at, gh in enumerate((ga0, ga1)):

        @pl.when(i == at)
        def _(gh=gh):
            step(n1a, refs[:3], mxa, gh)

    for at, gh in enumerate((gb0, gb1)):
        for w in range(2):

            @pl.when((i == 2 + at) & (lax.rem(at + core[0], 2) == w))
            def _(gh=gh, w=w):
                step(n1b, lowers[w], mxb, gh)

    @pl.when(i == 3)
    def _():
        rows = acc.shape[0] // 2
        split_store(acc, 0, rows, bits[0], ka, sa)
        split_store(acc, rows, rows, bits[1], kb, sb)


def attn_grad_call(bits, core, n1, mxs, ghs, grads_a, grads_0, grads_1):
    d = n1.shape[1]
    c = mxs[0].shape[1]
    na, nb = mxs[0].shape[0] // 2, mxs[1].shape[0] // 2
    fa = lambda w, o=0: pl.BlockSpec((na, w), lambda i, bits, core: (o + lax.rem(jnp.minimum(i, 1) + core[0], 2), 0))
    fb = lambda w: pl.BlockSpec((nb, w), lambda i, bits, core: (lax.rem(jnp.maximum(i - 2, 0) + core[0], 2), 0))
    return pl.pallas_call(
        attn_grad_kernel,
        grid_spec=pltpu.PrefetchScalarGridSpec(
            num_scalar_prefetch=2,
            grid=(4,),
            in_specs=[fa(d, 2 * nb // na), fb(d), fa(c), fb(c)]
            + [whole((na, d))] * 2
            + [whole((nb, d))] * 2
            + [fa(c)] * 3
            + [whole((nb, c))] * 6,
            out_specs=[whole((c, d))] * 4,
            scratch_shapes=[pltpu.VMEM((4 * c, d), F32)],
        ),
        out_shape=[SDS((c, d), BF16)] * 4,
        cost_estimate=GRAD_HINT,
        compiler_params=params(18),
        name="attn_grad",
    )(bits, core, n1, n1, *mxs, *ghs[0], *ghs[1], *grads_a, *grads_0, *grads_1)


def norm_one_kernel(nb, core, s, x, tok, row, gh_b, gh_a, gain, out, sums):
    i = pl.program_id(0)

    @pl.when(i == 0)
    def _():
        sums[...] = jnp.zeros_like(sums)

    one = s[...].astype(F32) + x[...].astype(F32)
    hat, root = norm_parts(tok[...].astype(F32) + row[...])
    g = jnp.where(i < nb, gh_b[...], gh_a[...]) + norm_back(one * gain[...], hat, root)
    out[...] = g.astype(BF16)
    sums[0:1, :] += col_sum(one * hat)
    sums[1:2, :] += col_sum(one)
    sums[2:3, :] += col_sum(g)


def lower_upper(d, nb):
    lower = pl.BlockSpec((BT, d), lambda i, *_: (jnp.minimum(i, nb - 1), 0))
    upper = pl.BlockSpec((BT, d), lambda i, *_: (jnp.maximum(i - nb, 0), 0))
    return lower, upper


def norm_one_call(core, s, x, tok, row, gh_b, gh_a, gain, hint=SHORT):
    n, d = s.shape
    nb, na = gh_b.shape[0] // BT, gh_a.shape[0] // BT
    at = lambda i, core: jnp.where(i < nb, core[0] * nb + i, 2 * nb + core[0] * na + i - nb)
    return pl.pallas_call(
        functools.partial(norm_one_kernel, nb),
        grid_spec=pltpu.PrefetchScalarGridSpec(
            num_scalar_prefetch=1,
            grid=(nb + na,),
            in_specs=[rows_at(d)] * 2
            + [pl.BlockSpec((BT, d), lambda i, core: (at(i, core), 0)), whole((1, d))]
            + [*lower_upper(d, nb), whole((d,))],
            out_specs=[rows_at(d), whole((8, d))],
        ),
        out_shape=[SDS((n, d), BF16), SDS((8, d), F32)],
        cost_estimate=hint,
        compiler_params=params(16),
        name="norm_one_back",
    )(core, s, x, tok, row, gh_b, gh_a, gain)


def out_kernel(nb, sb, xb, hid_b, sa, xa, hid_a, b_down, out):
    def store(s, x, hid):
        out[...] = (hid[...] + s[...].astype(F32) + x[...].astype(F32) + b_down[...]).astype(BF16)

    @pl.when(pl.program_id(0) < nb)
    def _():
        store(sb, xb, hid_b)

    @pl.when(pl.program_id(0) >= nb)
    def _():
        store(sa, xa, hid_a)


def out_call(sb, xb, hid_b, sa, xa, hid_a, b_down, hint=SHORT):
    n, d = hid_b.shape
    nb, na = n // BT, hid_a.shape[0] // BT
    lower = pl.BlockSpec((BT, d), lambda i: (jnp.minimum(i, nb - 1), 0))
    upper = pl.BlockSpec((BT, d), lambda i: (jnp.maximum(i - nb, 0), 0))
    return pl.pallas_call(
        functools.partial(out_kernel, nb),
        grid=(nb + na,),
        in_specs=[lower] * 3 + [upper] * 3 + [whole((d,))],
        out_specs=rows_at(d),
        out_shape=SDS(((nb + na) * BT, d), BF16),
        cost_estimate=hint,
        compiler_params=params(16),
        name="layer_out",
    )(sb, xb, hid_b, sa, xa, hid_a, b_down)


def out_rows_kernel(core, own, other, out):
    na = WIN // 2
    nb = own.shape[0] - na
    c = core[0]
    for src, half in ((own, c), (other, 1 - c)):
        out[pl.ds(pl.multiple_of(half * nb, 16), nb), :] = src[:nb, :]
        out[pl.ds(pl.multiple_of(2 * nb + half * na, 16), na), :] = src[nb:, :]


def out_rows_call(core, own, other, hint=SHORT):
    n, d = own.shape
    return pl.pallas_call(
        out_rows_kernel,
        in_specs=[SMEM] + [pl.BlockSpec((n, d))] * 2,
        out_specs=pl.BlockSpec((2 * n, d)),
        out_shape=SDS((2 * n, d), BF16),
        cost_estimate=hint,
        compiler_params=params(12),
        name="in_order",
    )(core, own, other)


VALUE_AT = 256
STEP_AT = 512


def pack_kernel(scal, s2a, s2b, s1, so, ffn, out):
    me, step = scal[0], scal[1]
    c = so.shape[1]
    n = out.shape[0] - 8
    out[0:3, :] = s2a[0:3, :] + s2b[0:3, :]
    out[3:5, :] = s1[0:2, :]
    out[5:7, :] = ffn[0:2, :]
    out[7:8, :] = jnp.zeros((1, out.shape[1]), F32)
    out[7:8, 0:c] = so[0:1, :]
    out[7:8, VALUE_AT : VALUE_AT + c] = so[1:2, :]
    lane = lax.broadcasted_iota(jnp.int32, (1, out.shape[1] - STEP_AT), 1)
    out[7:8, STEP_AT:] = jnp.where(lane == me, step.astype(F32), 0.0)
    spot = lax.broadcasted_iota(jnp.int32, (n, 1), 0) == me
    out[8:, :] = jnp.where(spot, s1[2:3, :], 0.0)


def pack_call(scal, n_dp, s2a, s2b, s1, so, ffn, hint=SHORT):
    d = ffn.shape[1]
    rows = 8 + -(-n_dp // 8) * 8
    return pl.pallas_call(
        pack_kernel,
        in_specs=[SMEM] + [pl.BlockSpec(v.shape) for v in (s2a, s2b, s1, so, ffn)],
        out_specs=pl.BlockSpec((rows, d)),
        out_shape=SDS((rows, d), F32),
        cost_estimate=hint,
        compiler_params=params(4),
        name="pack",
    )(scal, s2a, s2b, s1, so, ffn)


def small_add_kernel(own_rows, a, b, out):
    out[...] = a[...] + b[...]
    if own_rows:
        out[5:8, :] = a[5:8, :]


def small_add(a, b, own_rows=False):
    return pl.pallas_call(
        functools.partial(small_add_kernel, own_rows),
        in_specs=[pl.BlockSpec(a.shape)] * 2,
        out_specs=pl.BlockSpec(a.shape),
        out_shape=SDS(a.shape, F32),
        cost_estimate=SHORT,
        compiler_params=params(4),
        name="small_add",
    )(a, b)


def unpack_kernel(n_dp, small, got, *outs):
    table, vecs, bq, bv, full = outs[0], outs[1:8], outs[8], outs[9], outs[10]
    full[...] = small[...] + got[...]
    for n, vec in enumerate(vecs):
        vec[...] = full[n, :]
    c = bq.shape[0]
    bq[...] = full[7, 0:c]
    bv[...] = full[7, VALUE_AT : VALUE_AT + c]
    table[...] = jnp.zeros_like(table)
    steps = full[7:8, STEP_AT:]
    lane = lax.broadcasted_iota(jnp.int32, steps.shape, 1)
    for n in range(n_dp):
        at = jnp.sum(jnp.where(lane == n, steps, 0.0)).astype(jnp.int32)
        table[pl.ds(at, 1), :] += full[8 + n : 9 + n, :]


def unpack_call(n_dp, table_rows, c, small, got):
    rows, d = small.shape
    shapes = [(table_rows, d)] + [(d,)] * 7 + [(c,)] * 2
    return pl.pallas_call(
        functools.partial(unpack_kernel, n_dp),
        in_specs=[pl.BlockSpec(small.shape)] * 2,
        out_specs=[pl.BlockSpec(s) for s in shapes],
        out_shape=[SDS(s, F32) for s in shapes],
        scratch_shapes=[pltpu.VMEM(small.shape, F32)],
        cost_estimate=SHORT,
        compiler_params=params(10),
        name="unpack",
    )(small, got)


def after(token, value):
    return lax.optimization_barrier((token, value))[1]


class Spread:
    def __init__(self, n_dp, bits, orders, keep, send):
        self.n_dp, self.bits, self.orders, self.level = n_dp, bits, orders, 2
        self.keep = keep
        self.swap(0, send)

    def swap(self, level, values):
        self.got = [
            lax.ppermute(v, "dp", [(i, i ^ (1 << order[level])) for i in range(self.n_dp)])
            for v, order in zip(values, self.orders)
        ]

    def step(self, token, kernel, name, bits, shapes, hint, scratch=()):
        keep = [after(token, self.keep[0]), *self.keep[1:]]
        arrays = [a for pair in zip(keep, self.got) for a in pair]
        return step_call(kernel, name, bits, arrays, shapes, hint, scratch)

    def halve(self, token, hint=SHORT):
        n, d = self.keep[0].shape
        half = [SDS((n // 2, d), BF16)] * (2 * len(self.keep))
        out = self.step(token, halve_kernel, "halve", self.bits, half, hint, [pltpu.VMEM((n, d), F32)])
        self.keep = out[0::2]
        self.swap(1, out[1::2])
        return self.keep[0]

    def exchange(self, token, hint=SHORT):
        same = [SDS(k.shape, BF16) for k in self.keep]
        self.keep = self.step(token, add_kernel, "pair_add", None, same, hint)
        self.swap(self.level if self.level < len(self.orders[0]) else 1, self.keep)
        self.level += 1
        return self.keep[0]

    def join(self, token, hint=SHORT):
        n, d = self.keep[0].shape
        self.keep = self.step(token, join_kernel, "join", None, [SDS((2 * n, d), BF16)] * len(self.keep), hint)
        self.swap(0, self.keep)
        return self.keep[0]

    def place(self, token, pieces, hint=SHORT):
        n, d = self.keep[0].shape
        rows = 2 * n * len(self.keep) // pieces
        return self.step(token, place_kernel, "place", self.bits, [SDS((rows, d), F32)] * pieces, hint)


def per_device(
    n_tensor,
    n_dp,
    tokens,
    timesteps,
    piece_starts,
    step_table,
    first_gain,
    first_shift,
    w_query,
    b_query,
    w_key,
    w_value,
    b_value,
    w_out,
    b_out,
    second_gain,
    second_shift,
    w_in,
    b_in,
    w_down,
    b_down,
    cotangent,
):
    length, d = tokens.shape[1:]
    c = w_query.shape[1]
    rank = lax.axis_index("tensor").astype(jnp.int32)
    me = lax.axis_index("dp").astype(jnp.int32)
    over_x = [(i, i ^ 2) for i in range(n_tensor)]
    over_core = [(i, i ^ 1) for i in range(n_tensor)]
    swap_x = lambda v: lax.ppermute(v, "tensor", over_x)
    swap_core = lambda v: lax.ppermute(v, "tensor", over_core)
    n_bits = n_dp.bit_length() - 1
    orders = (list(range(n_bits)), list(range(1, n_bits)) + [0])
    bit = lambda b: (me >> b) & 1
    bits = jnp.stack([bit(orders[0][0]), bit(orders[1][0]), bit(orders[0][1]), bit(orders[1][1])])
    orders_q = (orders[0], [1, 0] + list(range(2, n_bits)))
    bits_q = jnp.stack([bit(orders_q[0][0]), bit(orders_q[1][0]), bit(orders_q[0][1]), bit(orders_q[1][1])])
    scal = jnp.stack([me, timesteps[0]])
    core = (rank & 1)[None]
    tok, bits, bits_q, scal, core, starts = lax.optimization_barrier(
        (tokens[0], bits, bits_q, scal, core, piece_starts[0])
    )
    cot = cotangent[0]
    wq, wk, wv = w_query.T, w_key.T, w_value.T

    top = length // WIN - 1
    groups = [[top], list(range(top - 1, -1, -1))]
    row0s = [top * WIN, 0]
    hbm = lambda v: pltpu.with_memory_space_constraint(v, pltpu.HBM)

    n1, q, k, v, row = qkv_call(
        timesteps, *[hbm(z) for z in (tok, step_table, first_gain, first_shift, wq, wk, wv, b_query, b_value)]
    )
    wo0 = w_out
    wo2 = swap_x(after(n1, w_out))
    mix_a, lse_a = attn_fwd_call(starts, q, k, v, groups[0])
    wo1 = swap_core(after(mix_a, w_out))
    wo3 = swap_core(after(mix_a, wo2))
    wos = [wo0, wo2, wo1, wo3]
    m1_a, m2_a = swap_core(mix_a), swap_x(mix_a)
    mix_b, lse_b = attn_fwd_call(starts, after(mix_a, q), k, v, groups[1])
    m3_a = swap_core(after(mix_b, m2_a))
    m2_b = swap_x(mix_b)

    def ffn_of(ms, n):
        return ffn_call(
            core, ms, tok, row, cot, wos, b_out, second_gain, second_shift, w_in, b_in, w_down, row0s[n]
        )

    hid_a, n2_a, act_a, gpre_a, keep_a, send_a = ffn_of([mix_a, m2_a, m1_a, m3_a], 0)
    got_a = swap_core(send_a)
    first = ffn_grad_call(bits, core, n2_a, gpre_a, act_a, cot, row0s[0])
    pair_b = stack_call(after(first[2], mix_b), m2_b)
    far_b = swap_core(pair_b)
    two_a = half_sum(after(pair_b, keep_a), got_a, 0)
    twox_a = swap_x(two_a)
    mlp_a = half_sum(after(two_a, keep_a), got_a, 1)
    hid_b, n2_b, act_b, gpre_b, keep_b, send_b = ffn_of([after(mlp_a, mix_b), m2_b, far_b], 1)
    got_b = swap_core(send_b)
    gh_a, ghb_a, s2_a = norm_two_call(core, after(n2_b, two_a), twox_a, hid_a, cot, second_gain, row0s[0])
    gho_a = swap_core(ghb_a)
    mlpx_a = swap_x(after(twox_a, mlp_a))
    ka, sa, kb, sb, ffn_sums = ffn_grad_call(
        bits, core, after(ghb_a, n2_b), gpre_b, act_b, cot, row0s[1], first, LONG
    )
    gff = Spread(n_dp, bits, orders, [ka, kb], [sa, sb])
    two_b = half_sum(after(ka, keep_b), got_b, 0)
    twox_b = swap_x(two_b)
    *grads_a, dkf, dvf = attn_bwd_call(
        starts, core, after((two_b, mlpx_a), q), k, v, ghb_a, gho_a, w_out, lse_a, None, top, groups[0]
    )
    t = gff.halve(grads_a[0])
    gh_b, ghb_b, s2_b = norm_two_call(core, after(t, two_b), twox_b, hid_b, cot, second_gain, row0s[1], LONG)
    gho_b = swap_core(ghb_b)
    mlp_b = half_sum(after(ghb_b, keep_b), got_b, 1, LONG)
    mlpx_b = swap_x(mlp_b)
    *grads_1, dkf, dvf = attn_bwd_call(
        starts, core, after(mlp_b, q), k, v, ghb_b, gho_b, w_out, lse_b, (dkf, dvf), 1, groups[1]
    )
    t = gff.exchange(grads_1[0])
    grads_0 = attn_bwd_call(
        starts, core, after(t, q), k, v, ghb_b, gho_b, w_out, lse_b, (dkf, dvf), 0, groups[1], SHORT
    )
    one, osend, so = one_call(core, [grads_0, grads_1, grads_a], wq, wk, wv)
    ogot = swap_core(osend)
    ka, sa, kb, sb = attn_grad_call(
        bits_q, core, after(one, n1), (mix_a, mix_b), ((ghb_a, gho_a), (ghb_b, gho_b)), grads_a, grads_0, grads_1
    )
    gat = Spread(n_dp, bits_q, orders_q, [ka, kb], [sa, sb])
    os_b = one_sum(after(ka, one), ogot)
    ox_b = swap_x(os_b)
    t = (os_b, mlpx_b)
    for _ in range(n_bits - 2):
        t = gff.exchange(t, LONG)
    t = gat.halve(t)
    t = gff.join(t)
    t = gat.exchange(t)
    gt, s1 = norm_one_call(core, after(t, os_b), ox_b, tok, row, gh_b, gh_a, first_gain, LONG)
    small = pack_call(after(gt, scal), n_dp, s2_a, s2_b, s1, so, ffn_sums)
    swapped = swap_core(small)
    t = small
    for _ in range(n_bits - 2):
        t = gat.exchange(t)
    small = small_add(after(t, small), swapped, True)
    swap_dp = lambda v, b: lax.ppermute(v, "dp", [(i, i ^ (1 << b)) for i in range(n_dp)])
    got = swap_dp(small, 0)
    g_in, g_down = gff.place(small, 2, LONG)
    small = small_add(after(g_in, small), got)
    got = swap_dp(small, 1)
    t = gat.join(small, LONG)
    small = after(t, small)
    for b in range(2, n_bits):
        small = small_add(small, got)
        got = swap_dp(small, b)
    o = out_call(after(small, mlp_b), mlpx_b, hid_b, mlp_a, mlpx_a, hid_a, b_down, LONG)
    oo, gto = swap_core(o), swap_core(after(o, gt))
    grad_tokens = out_rows_call(core, gt, gto)
    output = out_rows_call(core, after(grad_tokens, o), oo)
    g_table, g_sg, g_ss, g_bo, g_fg, g_fs, g_bi, g_bd, g_bq, g_bv = unpack_call(
        n_dp, step_table.shape[0], c, after(output, small), got
    )
    g_q, g_k, g_v, g_o = gat.place(g_sg, 4)
    return (
        output[None],
        grad_tokens[None],
        g_table,
        g_fg,
        g_fs,
        g_q.T,
        g_bq,
        g_k.T,
        g_v.T,
        g_bv,
        g_o,
        g_bo,
        g_sg,
        g_ss,
        g_in,
        g_bi,
        g_down,
        g_bd,
    )


def solution(mesh):
    in_specs = (
        P("dp", None, None),
        P("dp"),
        P("dp", None),
        P(),
        P(),
        P(),
        P(None, "tensor"),
        P("tensor"),
        P(None, "tensor"),
        P(None, "tensor"),
        P("tensor"),
        P("tensor", None),
        P(),
        P(),
        P(),
        P(None, "tensor"),
        P("tensor"),
        P("tensor", None),
        P(),
        P("dp", None, None),
    )
    out_specs = (
        P("dp", None, None),
        P("dp", None, None),
        P(),
        P(),
        P(),
        P(None, "tensor"),
        P("tensor"),
        P(None, "tensor"),
        P(None, "tensor"),
        P("tensor"),
        P("tensor", None),
        P(),
        P(),
        P(),
        P(None, "tensor"),
        P("tensor"),
        P("tensor", None),
        P(),
    )
    return jax.shard_map(
        functools.partial(per_device, mesh.shape["tensor"], mesh.shape["dp"]),
        mesh=mesh,
        in_specs=in_specs,
        out_specs=out_specs,
        check_vma=False,
    )
```

```python
import functools

import jax
import jax.numpy as jnp
from jax import lax
from jax.experimental import pallas as pl
from jax.experimental.pallas import tpu as pltpu
from jax.sharding import PartitionSpec as P

HD = 64
PIECE = 256
WIN = 2 * PIECE
EPS = 1e-05
BT = 256
F32 = jnp.float32
BF16 = jnp.bfloat16
SDS = jax.ShapeDtypeStruct
SCALE = HD ** (-0.5)
GELU_C = 0.7978845608028654


def nn(a, b):
    return lax.dot_general(a, b, (((1,), (0,)), ((), ())), preferred_element_type=F32)


def nt(a, b):
    return lax.dot_general(a, b, (((1,), (1,)), ((), ())), preferred_element_type=F32)


def tn(a, b):
    return lax.dot_general(a, b, (((0,), (0,)), ((), ())), preferred_element_type=F32)


def norm_parts(v):
    c = v - jnp.mean(v, axis=-1, keepdims=True)
    root = lax.rsqrt(jnp.mean(c * c, axis=-1, keepdims=True) + EPS)
    return c * root, root


def norm_back(e, hat, root):
    return root * (
        e - jnp.mean(e, axis=-1, keepdims=True) - hat * jnp.mean(e * hat, axis=-1, keepdims=True)
    )


def col_sum(v):
    return jnp.sum(v, axis=0, keepdims=True)


def whole(shape):
    return pl.BlockSpec(shape, lambda i, *_: (0,) * len(shape))


def rows_at(width, offset=0, block=BT):
    return pl.BlockSpec((block, width), lambda i, *_: (offset + i, 0))


LONG = pl.CostEstimate(flops=10**11, bytes_accessed=1000, transcendentals=0)
SHORT = pl.CostEstimate(flops=1000, bytes_accessed=1000, transcendentals=0)
GRAD_HINT = LONG


def params(mib=12):
    return pltpu.CompilerParams(vmem_limit_bytes=mib * 1024 * 1024)


SMEM = pl.BlockSpec(memory_space=pltpu.SMEM)


def qkv_kernel(steps, tok, table, gain, shift, wq, wk, wv, bq, bv, n1, q, k, v, row):
    rows = table[...].astype(F32)
    at = lax.broadcasted_iota(jnp.int32, rows.shape, 0) == lax.rem(steps[0], 8)
    step_row = col_sum(jnp.where(at, rows, 0.0))
    row[...] = step_row
    hat, _ = norm_parts(tok[...].astype(F32) + step_row)
    n = (hat * gain[...] + shift[...]).astype(BF16)
    n1[...] = n
    q[...] = ((nt(n, wq[...]) + bq[...]) * SCALE).astype(BF16)
    k[...] = nt(n, wk[...]).astype(BF16)
    v[...] = (nt(n, wv[...]) + bv[...]).astype(BF16)


def qkv_call(steps, tok, table, gain, shift, wq, wk, wv, bq, bv):
    length, d = tok.shape
    c = wq.shape[0]
    return pl.pallas_call(
        qkv_kernel,
        grid_spec=pltpu.PrefetchScalarGridSpec(
            num_scalar_prefetch=1,
            grid=(length // WIN,),
            in_specs=[rows_at(d, block=WIN), pl.BlockSpec((8, d), lambda i, steps: (steps[0] // 8, 0))]
            + [whole((d,))] * 2
            + [whole((c, d))] * 3
            + [whole((c,))] * 2,
            out_specs=[rows_at(d, block=WIN)] + [rows_at(c, block=WIN)] * 3 + [whole((1, d))],
        ),
        out_shape=[SDS((length, d), BF16)] + [SDS((length, c), BF16)] * 3 + [SDS((1, d), F32)],
        cost_estimate=LONG,
        compiler_params=params(16),
        name="norm_qkv",
    )(steps, tok, table, gain, shift, wq, wk, wv, bq, bv)


def attn_fwd_window(win, nh, starts, q, k, v, mix, lse):
    base = win * WIN
    start = starts[win]
    qpos = base + lax.broadcasted_iota(jnp.int32, (WIN, 1), 0)
    limit = jnp.where((qpos >= start) & (qpos < start + PIECE), start + PIECE - 1, qpos)
    kpos = base + lax.broadcasted_iota(jnp.int32, (1, WIN), 1)
    allow = kpos <= limit
    for h in range(nh):
        cols = slice(h * HD, (h + 1) * HD)
        qh = q[:, cols]
        near = jnp.where(allow, nt(qh, k[base : base + WIN, cols]), -1e30)
        top = jnp.max(near, axis=-1, keepdims=True)
        if win:
            far = nt(qh, k[:base, cols])
            top = jnp.maximum(top, jnp.max(far, axis=-1, keepdims=True))
        pn = jnp.exp(near - top)
        total = jnp.sum(pn, axis=-1, keepdims=True)
        out = nn(pn.astype(BF16), v[base : base + WIN, cols])
        if win:
            pf = jnp.exp(far - top)
            total = total + jnp.sum(pf, axis=-1, keepdims=True)
            out = out + nn(pf.astype(BF16), v[:base, cols])
        mix[:, cols] = (out / total).astype(BF16)
        stat = jnp.broadcast_to(top + jnp.log(total), (WIN, 128))
        lse[h : h + 1, :] = jnp.transpose(stat)[0:1, :]


def attn_fwd_kernel(wins, nh, starts, *refs):
    for n, win in enumerate(wins):

        @pl.when(pl.program_id(0) == n)
        def _(win=win):
            attn_fwd_window(win, nh, starts, *refs)


def attn_fwd_call(starts, q, k, v, wins):
    c = q.shape[1]
    kv = (wins[0] + 1) * WIN
    n = len(wins) * WIN
    return pl.pallas_call(
        functools.partial(attn_fwd_kernel, wins, c // HD),
        grid=(len(wins),),
        in_specs=[SMEM, pl.BlockSpec((WIN, c), lambda i: (wins[0] - i, 0)), whole((kv, c)), whole((kv, c))],
        out_specs=[
            pl.BlockSpec((WIN, c), lambda i: (wins[0] - wins[-1] - i, 0)),
            pl.BlockSpec((8, WIN), lambda i: (0, wins[0] - wins[-1] - i)),
        ],
        out_shape=[SDS((n, c), BF16), SDS((8, n), F32)],
        cost_estimate=LONG,
        compiler_params=params(20),
        name="attn_fwd",
    )(starts, q, k, v)


def stack_kernel(a, b, out):
    c = a.shape[1]
    out[:, :c] = a[...]
    out[:, c:] = b[...]


def stack_call(a, b):
    n, c = a.shape
    return pl.pallas_call(
        stack_kernel,
        in_specs=[pl.BlockSpec((n, c))] * 2,
        out_specs=pl.BlockSpec((n, 2 * c)),
        out_shape=SDS((n, 2 * c), BF16),
        cost_estimate=LONG,
        compiler_params=params(6),
        name="stack",
    )(a, b)


def ffn_kernel(
    pieces, core, *refs
):
    kept, sent, wos = refs[:pieces], refs[pieces : 2 * pieces], refs[2 * pieces + 5 : 2 * pieces + 9]
    tok_k, tok_s, row, cot_k, cot_s = refs[2 * pieces : 2 * pieces + 5]
    b_out, gain, shift, w_in, b_in, w_down, hid, n2, act, gpre, keep, send = refs[2 * pieces + 9 :]
    rows = tok_k.shape[0]
    both = lambda a, b: jnp.concatenate([a[...], b[...]], axis=0)
    mixed = jnp.concatenate([both(a, b) for a, b in zip(kept, sent)], axis=1)
    attn = nn(mixed, jnp.concatenate([w[...] for w in wos], axis=0))
    h = both(tok_k, tok_s).astype(F32) + row[...] + attn + b_out[...]
    hid[...] = h[:rows]
    hat, _ = norm_parts(h)
    n = (hat * gain[...] + shift[...]).astype(BF16)
    z = nn(n, w_in[...]) + b_in[...]
    z2 = z * z
    th = jnp.tanh(z * (GELU_C + (GELU_C * 0.044715) * z2))
    half = 0.5 * (1.0 + th)
    a = (z * half).astype(BF16)
    slope = half + (0.5 * z) * (1.0 - th * th) * (GELU_C + (3.0 * 0.044715 * GELU_C) * z2)
    gp = (nt(both(cot_k, cot_s), w_down[...]) * slope).astype(BF16)
    mlp = nn(a, w_down[...]).astype(BF16)
    two = nt(gp, w_in[...]).astype(BF16)
    for part, at in enumerate((slice(0, rows), slice(rows, 2 * rows))):
        n2[part] = n[at]
        act[part] = a[at]
        gpre[part] = gp[at]
        out = send if part else keep
        out[0] = two[at]
        out[1] = mlp[at]


def half_spec(width, nb, own, offset=0):
    return pl.BlockSpec((BT, width), lambda i, core: (offset + (core[0] if own else 1 - core[0]) * nb + i, 0))


def stacked(width, block=BT):
    return pl.BlockSpec((2, block, width), lambda i, *_: (0, i, 0))


def ffn_call(core, ms, tok, row, cot, wos, b_out, gain, shift, w_in, b_in, w_down, row0):
    n = ms[0].shape[0]
    c, d = wos[0].shape
    u = w_in.shape[1]
    h = n // 2
    nb = h // BT
    off = row0 // BT
    kept = functools.partial(half_spec, nb=nb, own=True)
    sent = functools.partial(half_spec, nb=nb, own=False)
    return pl.pallas_call(
        functools.partial(ffn_kernel, len(ms)),
        grid_spec=pltpu.PrefetchScalarGridSpec(
            num_scalar_prefetch=1,
            grid=(nb,),
            in_specs=[kept(v.shape[1]) for v in ms]
            + [sent(v.shape[1]) for v in ms]
            + [kept(d, offset=off), sent(d, offset=off), whole((1, d)), kept(d, offset=off), sent(d, offset=off)]
            + [whole((c, d))] * 4
            + [whole((d,))] * 3
            + [whole((d, u)), whole((u,)), whole((u, d))],
            out_specs=[rows_at(d), stacked(d), stacked(u), stacked(u), stacked(d), stacked(d)],
        ),
        out_shape=[SDS((h, d), F32), SDS((2, h, d), BF16)]
        + [SDS((2, h, u), BF16)] * 2
        + [SDS((2, h, d), BF16)] * 2,
        cost_estimate=LONG,
        compiler_params=params(24),
        name="ffn",
    )(core, *ms, *ms, tok, tok, row, cot, cot, *wos, b_out, gain, shift, w_in, b_in, w_down)


def split_store(acc, first, rows, bit, keep, send):
    half = rows // 2
    keep[...] = acc[pl.ds(pl.multiple_of(first + bit * half, 16), half), :].astype(BF16)
    send[...] = acc[pl.ds(pl.multiple_of(first + (1 - bit) * half, 16), half), :].astype(BF16)


def halve_kernel(parts, bits, *refs):
    ins, outs, acc = refs[: 2 * parts], refs[2 * parts : 4 * parts], refs[4 * parts]
    for part in range(parts):
        acc[...] = ins[2 * part][...].astype(F32) + ins[2 * part + 1][...].astype(F32)
        split_store(acc, 0, acc.shape[0], bits[2 + part], outs[2 * part], outs[2 * part + 1])


def add_kernel(parts, *refs):
    for part in range(parts):
        k, r = refs[2 * part : 2 * part + 2]
        refs[2 * parts + part][...] = (k[...].astype(F32) + r[...].astype(F32)).astype(BF16)


def join_kernel(parts, *refs):
    for part in range(parts):
        s, r = refs[2 * part : 2 * part + 2]
        n = s.shape[0]
        refs[2 * parts + part][:n, :] = s[...]
        refs[2 * parts + part][n:, :] = r[...]


def place_kernel(parts, bits, *refs):
    outs = refs[2 * parts :]
    per = len(outs) // parts
    for part in range(parts):
        p, r = refs[2 * part : 2 * part + 2]
        n = p.shape[0] // 2
        b0, b1 = bits[part], bits[2 + part]
        for src, first in ((p, b0), (r, 1 - b0)):
            for which in range(2):

                @pl.when(first == which)
                def _(src=src, which=which):
                    out = outs[part if per == 1 else 2 * part + which]
                    for sub, second in ((0, b1), (1, 1 - b1)):
                        at = pl.multiple_of(second * n, 8) + (2 * n * which if per == 1 else 0)
                        out[pl.ds(at, n), :] = src[sub * n : (sub + 1) * n, :].astype(F32)


def step_call(kernel, name, bits, arrays, shapes, hint, scratch=()):
    parts = len(arrays) // 2
    return pl.pallas_call(
        functools.partial(kernel, parts),
        in_specs=([] if bits is None else [SMEM]) + [pl.BlockSpec(a.shape) for a in arrays],
        out_specs=[pl.BlockSpec(s.shape) for s in shapes],
        out_shape=shapes,
        scratch_shapes=scratch,
        cost_estimate=hint,
        compiler_params=params(14),
        name=name,
    )(*([] if bits is None else [bits]), *arrays)


def one_sum_kernel(keep, got, out):
    out[...] = (keep[...].astype(F32) + got[...].astype(F32)).astype(BF16)


def one_sum(keep, got, hint=SHORT):
    return pl.pallas_call(
        one_sum_kernel,
        in_specs=[pl.BlockSpec(keep.shape)] * 2,
        out_specs=pl.BlockSpec(keep.shape),
        out_shape=SDS(keep.shape, BF16),
        cost_estimate=hint,
        compiler_params=params(8),
        name="one_sum",
    )(keep, got)


def half_sum_kernel(keep, got, out):
    out[...] = (keep[0].astype(F32) + got[0].astype(F32)).astype(BF16)


def half_sum(keep, got, which, hint=SHORT):
    _, n, d = keep.shape
    part = pl.BlockSpec((1, n, d), lambda i: (which, 0, 0))
    return pl.pallas_call(
        half_sum_kernel,
        grid=(1,),
        in_specs=[part, part],
        out_specs=whole((n, d)),
        out_shape=SDS((n, d), BF16),
        cost_estimate=hint,
        compiler_params=params(8),
        name="half_sum",
    )(keep, got)


def ffn_grad_step(n2, gp, ac, cot_k, cot_s, acc_in, acc_down, sums):
    flat = lambda ref: ref[...].reshape(2 * ref.shape[1], ref.shape[2])
    cot = jnp.concatenate([cot_k[...], cot_s[...]], axis=0)
    g = flat(gp)
    acc_in[...] += tn(flat(n2), g)
    acc_down[...] += tn(flat(ac), cot)
    sums[0:1, :] += col_sum(g.astype(F32))
    sums[1:2, :] += col_sum(cot.astype(F32))


def ffn_grad_first_kernel(core, n2, gp, ac, cot_k, cot_s, acc_in, acc_down, sums):
    for ref in (acc_in, acc_down, sums):
        ref[...] = jnp.zeros_like(ref)
    ffn_grad_step(n2, gp, ac, cot_k, cot_s, acc_in, acc_down, sums)


def ffn_grad_last_kernel(bits, core, n2, gp, ac, cot_k, cot_s, in0, down0, sums0, ka, sa, kb, sb, sums, acc_in, acc_down):
    @pl.when(pl.program_id(0) == 0)
    def _():
        acc_in[...] = in0[...]
        acc_down[...] = down0[...]
        sums[...] = sums0[...]

    ffn_grad_step(n2, gp, ac, cot_k, cot_s, acc_in, acc_down, sums)

    @pl.when(pl.program_id(0) == pl.num_programs(0) - 1)
    def _():
        split_store(acc_in, 0, acc_in.shape[0], bits[0], ka, sa)
        split_store(acc_down, 0, acc_down.shape[0], bits[1], kb, sb)


def ffn_grad_call(bits, core, n2, gp, ac, cot, row0, before=None, hint=SHORT):
    _, h, d = n2.shape
    u = gp.shape[2]
    nb = h // BT
    block = lambda w: pl.BlockSpec((2, BT, w), lambda i, *_: (0, i, 0))

    def cot_spec(own):
        return pl.BlockSpec(
            (BT, d), lambda i, *s: (row0 // BT + (s[-1][0] if own else 1 - s[-1][0]) * nb + i, 0)
        )

    sums = [(d, u), (u, d), (8, d)]
    last = before is not None
    outs = [(d // 2, u)] * 2 + [(u // 2, d)] * 2 + [(8, d)] if last else sums
    types = [BF16] * 4 + [F32] if last else [F32] * 3
    return pl.pallas_call(
        ffn_grad_last_kernel if last else ffn_grad_first_kernel,
        grid_spec=pltpu.PrefetchScalarGridSpec(
            num_scalar_prefetch=2 if last else 1,
            grid=(nb,),
            in_specs=[block(d), block(u), block(u), cot_spec(True), cot_spec(False)]
            + ([whole(s) for s in sums] if last else []),
            out_specs=[whole(s) for s in outs],
            scratch_shapes=[pltpu.VMEM(s, F32) for s in sums[:2]] if last else [],
        ),
        out_shape=[SDS(s, t) for s, t in zip(outs, types)],
        cost_estimate=hint,
        compiler_params=params(24 if last else 16),
        name="ffn_grad",
    )(*([bits] if last else []), core, n2, gp, ac, cot, cot, *(before or ()))


def norm_two_kernel(core, s, x, hid, cot, gain, gh, ghb, sums):
    @pl.when(pl.program_id(0) == 0)
    def _():
        sums[...] = jnp.zeros_like(sums)

    two = s[...].astype(F32) + x[...].astype(F32)
    hat, root = norm_parts(hid[...])
    g = cot[...].astype(F32) + norm_back(two * gain[...], hat, root)
    gh[...] = g
    ghb[...] = g.astype(BF16)
    sums[0:1, :] += col_sum(two * hat)
    sums[1:2, :] += col_sum(two)
    sums[2:3, :] += col_sum(g)


def half_rows(d, n, row0):
    return pl.BlockSpec((BT, d), lambda i, core: (row0 // BT + core[0] * (n // BT) + i, 0))


def norm_two_call(core, s, x, hid, cot, gain, row0, hint=SHORT):
    n, d = hid.shape
    return pl.pallas_call(
        norm_two_kernel,
        grid_spec=pltpu.PrefetchScalarGridSpec(
            num_scalar_prefetch=1,
            grid=(n // BT,),
            in_specs=[rows_at(d)] * 3 + [half_rows(d, n, row0), whole((d,))],
            out_specs=[rows_at(d)] * 2 + [whole((8, d))],
        ),
        out_shape=[SDS((n, d), F32), SDS((n, d), BF16), SDS((8, d), F32)],
        cost_estimate=hint,
        compiler_params=params(16),
        name="norm_two_back",
    )(core, s, x, hid, cot, gain)


def attn_bwd_kernel(win, low, wins, nh, carried, starts, core, q, k, v, mine, other, w_out, lse, *rest):
    if carried:
        dk0, dv0, rest = rest[0], rest[1], rest[2:]
    dq, dk, dv = rest[:3]
    gm = rest[-1]
    base = win * WIN
    near = slice(base, base + WIN)
    grad = lambda ref: nt(ref[...], w_out[...]).astype(BF16)
    if wins == 1:
        half = WIN // 2
        gm[pl.ds(pl.multiple_of(core[0] * half, half), half), :] = grad(mine)
        gm[pl.ds(pl.multiple_of((1 - core[0]) * half, half), half), :] = grad(other)
    else:

        @pl.when(core[0] == win - low)
        def _():
            gm[...] = grad(mine)

        @pl.when(core[0] != win - low)
        def _():
            gm[...] = grad(other)

    start = starts[win]
    qpos = base + lax.broadcasted_iota(jnp.int32, (1, WIN), 1)
    limit = jnp.where((qpos >= start) & (qpos < start + PIECE), start + PIECE - 1, qpos)
    kpos = base + lax.broadcasted_iota(jnp.int32, (WIN, 1), 0)
    allow = kpos <= limit
    for h in range(nh):
        cols = slice(h * HD, (h + 1) * HD)
        qh = q[near, cols]
        gh = gm[:, cols]
        ls = lse[h : h + 1, (win - low) * WIN : (win - low + 1) * WIN]
        pn = jnp.exp(jnp.where(allow, nt(k[near, cols], qh), -1e30) - ls)
        dpn = nt(v[near, cols], gh)
        centre = col_sum(pn * dpn)
        if win:
            pf = jnp.exp(nt(k[:base, cols], qh) - ls)
            dpf = nt(v[:base, cols], gh)
            centre = centre + col_sum(pf * dpf)
        dsn = (pn * (dpn - centre)).astype(BF16)
        dqt = tn(k[near, cols], dsn)
        dkn = nn(dsn, qh)
        dvn = nn(pn.astype(BF16), gh)
        if carried:
            dkn = dkn + dk0[near, cols]
            dvn = dvn + dv0[near, cols]
        dk[:, cols] = dkn.astype(BF16)
        dv[:, cols] = dvn.astype(BF16)
        if win:
            dsf = (pf * (dpf - centre)).astype(BF16)
            dqt = dqt + tn(k[:base, cols], dsf)
            dkf = nn(dsf, qh)
            dvf = nn(pf.astype(BF16), gh)
            if carried:
                dkf = dkf + dk0[:base, cols]
                dvf = dvf + dv0[:base, cols]
            rest[3][:, cols] = dkf
            rest[4][:, cols] = dvf
        dq[:, cols] = jnp.transpose((dqt.astype(BF16).astype(F32) * SCALE)).astype(BF16)


def attn_bwd_call(starts, core, q, k, v, mine, other, w_out, lse, carry, win, group, hint=LONG):
    c, d = w_out.shape
    carried = carry is not None
    kv = (win + 1) * WIN
    full = lambda a: pl.BlockSpec(a.shape, lambda *_: (0,) * a.ndim)
    first = pl.BlockSpec((kv, c), lambda *_: (0, 0))
    shapes = [SDS((WIN, c), BF16)] * 3 + ([SDS((win * WIN, c), F32)] * 2 if win else [])
    return pl.pallas_call(
        functools.partial(attn_bwd_kernel, win, group[-1], len(group), c // HD, carried),
        grid=(1,),
        in_specs=[SMEM, SMEM, first, first, first, full(mine), full(other), full(w_out), full(lse)]
        + ([first] * 2 if carried else []),
        out_specs=[full(s) for s in shapes],
        out_shape=shapes,
        scratch_shapes=[pltpu.VMEM((WIN, c), BF16)],
        cost_estimate=hint,
        compiler_params=params(24),
        name="attn_bwd",
    )(starts, core, q, k, v, mine, other, w_out, lse, *(carry if carried else ()))


def one_kernel(core, *refs):
    wq, wk, wv, keep, send, sums, buf = refs[9:]
    c = core[0]
    n = buf.shape[0]
    half = n // 2
    weights = jnp.concatenate([wq[...], wk[...], wv[...]], axis=0)
    for w in range(3):
        dq, dk, dv = refs[3 * w : 3 * w + 3]
        part = nn(jnp.concatenate([dq[...], dk[...], dv[...]], axis=1), weights).astype(BF16)
        for at, g in enumerate((dq, dv)):
            total = col_sum(g[...].astype(F32))
            sums[at : at + 1, :] = total if w == 0 else sums[at : at + 1, :] + total
        if w == 2:
            buf[...] = part
            keep[n:, :] = buf[pl.ds(pl.multiple_of(c * half, half), half), :]
            send[n:, :] = buf[pl.ds(pl.multiple_of((1 - c) * half, half), half), :]
        else:

            @pl.when(c == w)
            def _():
                keep[:n, :] = part

            @pl.when(c != w)
            def _():
                send[:n, :] = part


def one_call(core, grads, wq, wk, wv):
    c, d = wq.shape
    rows = 3 * WIN // 2
    return pl.pallas_call(
        one_kernel,
        in_specs=[SMEM] + [pl.BlockSpec((WIN, c))] * 9 + [pl.BlockSpec((c, d))] * 3,
        out_specs=[pl.BlockSpec((rows, d))] * 2 + [pl.BlockSpec((8, c))],
        out_shape=[SDS((rows, d), BF16)] * 2 + [SDS((8, c), F32)],
        scratch_shapes=[pltpu.VMEM((WIN, d), BF16)],
        cost_estimate=SHORT,
        compiler_params=params(18),
        name="grad_one",
    )(core, *[g for window in grads for g in window], wq, wk, wv)


def attn_grad_kernel(bits, core, n1a, n1b, mxa, mxb, ga0, ga1, gb0, gb1, *refs):
    i = pl.program_id(0)
    c = mxa.shape[1]
    lowers = (refs[3:6], refs[6:9])
    ka, sa, kb, sb, acc = refs[9:]

    @pl.when(i == 0)
    def _():
        acc[...] = jnp.zeros_like(acc)

    def step(n1, grads, mx, gh):
        acc[: 3 * c, :] += tn(jnp.concatenate([g[...] for g in grads], axis=1), n1[...])
        acc[3 * c :, :] += tn(mx[...], gh[...])

    for at, gh in enumerate((ga0, ga1)):

        @pl.when(i == at)
        def _(gh=gh):
            step(n1a, refs[:3], mxa, gh)

    for at, gh in enumerate((gb0, gb1)):
        for w in range(2):

            @pl.when((i == 2 + at) & (lax.rem(at + core[0], 2) == w))
            def _(gh=gh, w=w):
                step(n1b, lowers[w], mxb, gh)

    @pl.when(i == 3)
    def _():
        rows = acc.shape[0] // 2
        split_store(acc, 0, rows, bits[0], ka, sa)
        split_store(acc, rows, rows, bits[1], kb, sb)


def attn_grad_call(bits, core, n1, mxs, ghs, grads_a, grads_0, grads_1):
    d = n1.shape[1]
    c = mxs[0].shape[1]
    na, nb = mxs[0].shape[0] // 2, mxs[1].shape[0] // 2
    fa = lambda w, o=0: pl.BlockSpec((na, w), lambda i, bits, core: (o + lax.rem(jnp.minimum(i, 1) + core[0], 2), 0))
    fb = lambda w: pl.BlockSpec((nb, w), lambda i, bits, core: (lax.rem(jnp.maximum(i - 2, 0) + core[0], 2), 0))
    return pl.pallas_call(
        attn_grad_kernel,
        grid_spec=pltpu.PrefetchScalarGridSpec(
            num_scalar_prefetch=2,
            grid=(4,),
            in_specs=[fa(d, 2 * nb // na), fb(d), fa(c), fb(c)]
            + [whole((na, d))] * 2
            + [whole((nb, d))] * 2
            + [fa(c)] * 3
            + [whole((nb, c))] * 6,
            out_specs=[whole((c, d))] * 4,
            scratch_shapes=[pltpu.VMEM((4 * c, d), F32)],
        ),
        out_shape=[SDS((c, d), BF16)] * 4,
        cost_estimate=GRAD_HINT,
        compiler_params=params(18),
        name="attn_grad",
    )(bits, core, n1, n1, *mxs, *ghs[0], *ghs[1], *grads_a, *grads_0, *grads_1)


def norm_one_kernel(nb, core, s, x, tok, row, gh_b, gh_a, gain, out, sums):
    i = pl.program_id(0)

    @pl.when(i == 0)
    def _():
        sums[...] = jnp.zeros_like(sums)

    one = s[...].astype(F32) + x[...].astype(F32)
    hat, root = norm_parts(tok[...].astype(F32) + row[...])
    g = jnp.where(i < nb, gh_b[...], gh_a[...]) + norm_back(one * gain[...], hat, root)
    out[...] = g.astype(BF16)
    sums[0:1, :] += col_sum(one * hat)
    sums[1:2, :] += col_sum(one)
    sums[2:3, :] += col_sum(g)


def lower_upper(d, nb):
    lower = pl.BlockSpec((BT, d), lambda i, *_: (jnp.minimum(i, nb - 1), 0))
    upper = pl.BlockSpec((BT, d), lambda i, *_: (jnp.maximum(i - nb, 0), 0))
    return lower, upper


def norm_one_call(core, s, x, tok, row, gh_b, gh_a, gain, hint=SHORT):
    n, d = s.shape
    nb, na = gh_b.shape[0] // BT, gh_a.shape[0] // BT
    at = lambda i, core: jnp.where(i < nb, core[0] * nb + i, 2 * nb + core[0] * na + i - nb)
    return pl.pallas_call(
        functools.partial(norm_one_kernel, nb),
        grid_spec=pltpu.PrefetchScalarGridSpec(
            num_scalar_prefetch=1,
            grid=(nb + na,),
            in_specs=[rows_at(d)] * 2
            + [pl.BlockSpec((BT, d), lambda i, core: (at(i, core), 0)), whole((1, d))]
            + [*lower_upper(d, nb), whole((d,))],
            out_specs=[rows_at(d), whole((8, d))],
        ),
        out_shape=[SDS((n, d), BF16), SDS((8, d), F32)],
        cost_estimate=hint,
        compiler_params=params(16),
        name="norm_one_back",
    )(core, s, x, tok, row, gh_b, gh_a, gain)


def out_kernel(nb, sb, xb, hid_b, sa, xa, hid_a, b_down, out):
    def store(s, x, hid):
        out[...] = (hid[...] + s[...].astype(F32) + x[...].astype(F32) + b_down[...]).astype(BF16)

    @pl.when(pl.program_id(0) < nb)
    def _():
        store(sb, xb, hid_b)

    @pl.when(pl.program_id(0) >= nb)
    def _():
        store(sa, xa, hid_a)


def out_call(sb, xb, hid_b, sa, xa, hid_a, b_down, hint=SHORT):
    n, d = hid_b.shape
    nb, na = n // BT, hid_a.shape[0] // BT
    lower = pl.BlockSpec((BT, d), lambda i: (jnp.minimum(i, nb - 1), 0))
    upper = pl.BlockSpec((BT, d), lambda i: (jnp.maximum(i - nb, 0), 0))
    return pl.pallas_call(
        functools.partial(out_kernel, nb),
        grid=(nb + na,),
        in_specs=[lower] * 3 + [upper] * 3 + [whole((d,))],
        out_specs=rows_at(d),
        out_shape=SDS(((nb + na) * BT, d), BF16),
        cost_estimate=hint,
        compiler_params=params(16),
        name="layer_out",
    )(sb, xb, hid_b, sa, xa, hid_a, b_down)


def out_rows_kernel(core, own, other, out):
    na = WIN // 2
    nb = own.shape[0] - na
    c = core[0]
    for src, half in ((own, c), (other, 1 - c)):
        out[pl.ds(pl.multiple_of(half * nb, 16), nb), :] = src[:nb, :]
        out[pl.ds(pl.multiple_of(2 * nb + half * na, 16), na), :] = src[nb:, :]


def out_rows_call(core, own, other, hint=SHORT):
    n, d = own.shape
    return pl.pallas_call(
        out_rows_kernel,
        in_specs=[SMEM] + [pl.BlockSpec((n, d))] * 2,
        out_specs=pl.BlockSpec((2 * n, d)),
        out_shape=SDS((2 * n, d), BF16),
        cost_estimate=hint,
        compiler_params=params(12),
        name="in_order",
    )(core, own, other)


VALUE_AT = 256
STEP_AT = 512


def pack_kernel(scal, s2a, s2b, s1, so, ffn, out):
    me, step = scal[0], scal[1]
    c = so.shape[1]
    n = out.shape[0] - 8
    out[0:3, :] = s2a[0:3, :] + s2b[0:3, :]
    out[3:5, :] = s1[0:2, :]
    out[5:7, :] = ffn[0:2, :]
    out[7:8, :] = jnp.zeros((1, out.shape[1]), F32)
    out[7:8, 0:c] = so[0:1, :]
    out[7:8, VALUE_AT : VALUE_AT + c] = so[1:2, :]
    lane = lax.broadcasted_iota(jnp.int32, (1, out.shape[1] - STEP_AT), 1)
    out[7:8, STEP_AT:] = jnp.where(lane == me, step.astype(F32), 0.0)
    spot = lax.broadcasted_iota(jnp.int32, (n, 1), 0) == me
    out[8:, :] = jnp.where(spot, s1[2:3, :], 0.0)


def pack_call(scal, n_dp, s2a, s2b, s1, so, ffn, hint=SHORT):
    d = ffn.shape[1]
    rows = 8 + -(-n_dp // 8) * 8
    return pl.pallas_call(
        pack_kernel,
        in_specs=[SMEM] + [pl.BlockSpec(v.shape) for v in (s2a, s2b, s1, so, ffn)],
        out_specs=pl.BlockSpec((rows, d)),
        out_shape=SDS((rows, d), F32),
        cost_estimate=hint,
        compiler_params=params(4),
        name="pack",
    )(scal, s2a, s2b, s1, so, ffn)


def small_add_kernel(own_rows, a, b, out):
    out[...] = a[...] + b[...]
    if own_rows:
        out[5:8, :] = a[5:8, :]


def small_add(a, b, own_rows=False):
    return pl.pallas_call(
        functools.partial(small_add_kernel, own_rows),
        in_specs=[pl.BlockSpec(a.shape)] * 2,
        out_specs=pl.BlockSpec(a.shape),
        out_shape=SDS(a.shape, F32),
        cost_estimate=SHORT,
        compiler_params=params(4),
        name="small_add",
    )(a, b)


def unpack_kernel(n_dp, small, got, *outs):
    table, vecs, bq, bv, full = outs[0], outs[1:8], outs[8], outs[9], outs[10]
    full[...] = small[...] + got[...]
    for n, vec in enumerate(vecs):
        vec[...] = full[n, :]
    c = bq.shape[0]
    bq[...] = full[7, 0:c]
    bv[...] = full[7, VALUE_AT : VALUE_AT + c]
    table[...] = jnp.zeros_like(table)
    steps = full[7:8, STEP_AT:]
    lane = lax.broadcasted_iota(jnp.int32, steps.shape, 1)
    for n in range(n_dp):
        at = jnp.sum(jnp.where(lane == n, steps, 0.0)).astype(jnp.int32)
        table[pl.ds(at, 1), :] += full[8 + n : 9 + n, :]


def unpack_call(n_dp, table_rows, c, small, got):
    rows, d = small.shape
    shapes = [(table_rows, d)] + [(d,)] * 7 + [(c,)] * 2
    return pl.pallas_call(
        functools.partial(unpack_kernel, n_dp),
        in_specs=[pl.BlockSpec(small.shape)] * 2,
        out_specs=[pl.BlockSpec(s) for s in shapes],
        out_shape=[SDS(s, F32) for s in shapes],
        scratch_shapes=[pltpu.VMEM(small.shape, F32)],
        cost_estimate=SHORT,
        compiler_params=params(10),
        name="unpack",
    )(small, got)


def after(token, value):
    return lax.optimization_barrier((token, value))[1]


class Spread:
    def __init__(self, n_dp, bits, orders, keep, send):
        self.n_dp, self.bits, self.orders, self.level = n_dp, bits, orders, 2
        self.keep = keep
        self.swap(0, send)

    def swap(self, level, values):
        self.got = [
            lax.ppermute(v, "dp", [(i, i ^ (1 << order[level])) for i in range(self.n_dp)])
            for v, order in zip(values, self.orders)
        ]

    def step(self, token, kernel, name, bits, shapes, hint, scratch=()):
        keep = [after(token, self.keep[0]), *self.keep[1:]]
        arrays = [a for pair in zip(keep, self.got) for a in pair]
        return step_call(kernel, name, bits, arrays, shapes, hint, scratch)

    def halve(self, token, hint=SHORT):
        n, d = self.keep[0].shape
        half = [SDS((n // 2, d), BF16)] * (2 * len(self.keep))
        out = self.step(token, halve_kernel, "halve", self.bits, half, hint, [pltpu.VMEM((n, d), F32)])
        self.keep = out[0::2]
        self.swap(1, out[1::2])
        return self.keep[0]

    def exchange(self, token, hint=SHORT):
        same = [SDS(k.shape, BF16) for k in self.keep]
        self.keep = self.step(token, add_kernel, "pair_add", None, same, hint)
        self.swap(self.level if self.level < len(self.orders[0]) else 1, self.keep)
        self.level += 1
        return self.keep[0]

    def join(self, token, hint=SHORT):
        n, d = self.keep[0].shape
        self.keep = self.step(token, join_kernel, "join", None, [SDS((2 * n, d), BF16)] * len(self.keep), hint)
        self.swap(0, self.keep)
        return self.keep[0]

    def place(self, token, pieces, hint=SHORT):
        n, d = self.keep[0].shape
        rows = 2 * n * len(self.keep) // pieces
        return self.step(token, place_kernel, "place", self.bits, [SDS((rows, d), F32)] * pieces, hint)


def per_device(
    n_tensor,
    n_dp,
    tokens,
    timesteps,
    piece_starts,
    step_table,
    first_gain,
    first_shift,
    w_query,
    b_query,
    w_key,
    w_value,
    b_value,
    w_out,
    b_out,
    second_gain,
    second_shift,
    w_in,
    b_in,
    w_down,
    b_down,
    cotangent,
):
    length, d = tokens.shape[1:]
    c = w_query.shape[1]
    rank = lax.axis_index("tensor").astype(jnp.int32)
    me = lax.axis_index("dp").astype(jnp.int32)
    over_x = [(i, i ^ 2) for i in range(n_tensor)]
    over_core = [(i, i ^ 1) for i in range(n_tensor)]
    swap_x = lambda v: lax.ppermute(v, "tensor", over_x)
    swap_core = lambda v: lax.ppermute(v, "tensor", over_core)
    n_bits = n_dp.bit_length() - 1
    orders = (list(range(n_bits)), list(range(1, n_bits)) + [0])
    bit = lambda b: (me >> b) & 1
    bits = jnp.stack([bit(orders[0][0]), bit(orders[1][0]), bit(orders[0][1]), bit(orders[1][1])])
    orders_q = (orders[0], [1, 0] + list(range(2, n_bits)))
    bits_q = jnp.stack([bit(orders_q[0][0]), bit(orders_q[1][0]), bit(orders_q[0][1]), bit(orders_q[1][1])])
    scal = jnp.stack([me, timesteps[0]])
    core = (rank & 1)[None]
    tok, bits, bits_q, scal, core, starts = lax.optimization_barrier(
        (tokens[0], bits, bits_q, scal, core, piece_starts[0])
    )
    cot = cotangent[0]
    wq, wk, wv = w_query.T, w_key.T, w_value.T

    top = length // WIN - 1
    groups = [[top], list(range(top - 1, -1, -1))]
    row0s = [top * WIN, 0]
    hbm = lambda v: pltpu.with_memory_space_constraint(v, pltpu.HBM)

    n1, q, k, v, row = qkv_call(
        timesteps, *[hbm(z) for z in (tok, step_table, first_gain, first_shift, wq, wk, wv, b_query, b_value)]
    )
    wo0 = w_out
    wo2 = swap_x(after(n1, w_out))
    mix_a, lse_a = attn_fwd_call(starts, q, k, v, groups[0])
    wo1 = swap_core(after(mix_a, w_out))
    wo3 = swap_core(after(mix_a, wo2))
    wos = [wo0, wo2, wo1, wo3]
    m1_a, m2_a = swap_core(mix_a), swap_x(mix_a)
    mix_b, lse_b = attn_fwd_call(starts, after(mix_a, q), k, v, groups[1])
    m3_a = swap_core(after(mix_b, m2_a))
    m2_b = swap_x(mix_b)

    def ffn_of(ms, n):
        return ffn_call(
            core, ms, tok, row, cot, wos, b_out, second_gain, second_shift, w_in, b_in, w_down, row0s[n]
        )

    hid_a, n2_a, act_a, gpre_a, keep_a, send_a = ffn_of([mix_a, m2_a, m1_a, m3_a], 0)
    got_a = swap_core(send_a)
    first = ffn_grad_call(bits, core, n2_a, gpre_a, act_a, cot, row0s[0])
    pair_b = stack_call(after(first[2], mix_b), m2_b)
    far_b = swap_core(pair_b)
    two_a = half_sum(after(pair_b, keep_a), got_a, 0)
    twox_a = swap_x(two_a)
    mlp_a = half_sum(after(two_a, keep_a), got_a, 1)
    hid_b, n2_b, act_b, gpre_b, keep_b, send_b = ffn_of([after(mlp_a, mix_b), m2_b, far_b], 1)
    got_b = swap_core(send_b)
    gh_a, ghb_a, s2_a = norm_two_call(core, after(n2_b, two_a), twox_a, hid_a, cot, second_gain, row0s[0])
    gho_a = swap_core(ghb_a)
    mlpx_a = swap_x(after(twox_a, mlp_a))
    ka, sa, kb, sb, ffn_sums = ffn_grad_call(
        bits, core, after(ghb_a, n2_b), gpre_b, act_b, cot, row0s[1], first, LONG
    )
    gff = Spread(n_dp, bits, orders, [ka, kb], [sa, sb])
    two_b = half_sum(after(ka, keep_b), got_b, 0)
    twox_b = swap_x(two_b)
    *grads_a, dkf, dvf = attn_bwd_call(
        starts, core, after((two_b, mlpx_a), q), k, v, ghb_a, gho_a, w_out, lse_a, None, top, groups[0]
    )
    t = gff.halve(grads_a[0])
    gh_b, ghb_b, s2_b = norm_two_call(core, after(t, two_b), twox_b, hid_b, cot, second_gain, row0s[1], LONG)
    gho_b = swap_core(ghb_b)
    mlp_b = half_sum(after(ghb_b, keep_b), got_b, 1, LONG)
    mlpx_b = swap_x(mlp_b)
    *grads_1, dkf, dvf = attn_bwd_call(
        starts, core, after(mlp_b, q), k, v, ghb_b, gho_b, w_out, lse_b, (dkf, dvf), 1, groups[1]
    )
    t = gff.exchange(grads_1[0])
    grads_0 = attn_bwd_call(
        starts, core, after(t, q), k, v, ghb_b, gho_b, w_out, lse_b, (dkf, dvf), 0, groups[1], SHORT
    )
    one, osend, so = one_call(core, [grads_0, grads_1, grads_a], wq, wk, wv)
    ogot = swap_core(osend)
    ka, sa, kb, sb = attn_grad_call(
        bits_q, core, after(one, n1), (mix_a, mix_b), ((ghb_a, gho_a), (ghb_b, gho_b)), grads_a, grads_0, grads_1
    )
    gat = Spread(n_dp, bits_q, orders_q, [ka, kb], [sa, sb])
    os_b = one_sum(after(ka, one), ogot)
    ox_b = swap_x(os_b)
    t = (os_b, mlpx_b)
    for _ in range(n_bits - 2):
        t = gff.exchange(t, LONG)
    t = gat.halve(t)
    t = gff.join(t)
    t = gat.exchange(t)
    gt, s1 = norm_one_call(core, after(t, os_b), ox_b, tok, row, gh_b, gh_a, first_gain, LONG)
    small = pack_call(after(gt, scal), n_dp, s2_a, s2_b, s1, so, ffn_sums)
    swapped = swap_core(small)
    t = small
    for _ in range(n_bits - 2):
        t = gat.exchange(t)
    small = small_add(after(t, small), swapped, True)
    swap_dp = lambda v, b: lax.ppermute(v, "dp", [(i, i ^ (1 << b)) for i in range(n_dp)])
    got = swap_dp(small, 0)
    g_in, g_down = gff.place(small, 2, LONG)
    small = small_add(after(g_in, small), got)
    got = swap_dp(small, 1)
    t = gat.join(small, LONG)
    small = after(t, small)
    for b in range(2, n_bits):
        small = small_add(small, got)
        got = swap_dp(small, b)
    o = out_call(after(small, mlp_b), mlpx_b, hid_b, mlp_a, mlpx_a, hid_a, b_down, LONG)
    oo, gto = swap_core(o), swap_core(after(o, gt))
    grad_tokens = out_rows_call(core, gt, gto)
    output = out_rows_call(core, after(grad_tokens, o), oo)
    g_q, g_k, g_v, g_o = gat.place(output, 4)
    g_table, g_sg, g_ss, g_bo, g_fg, g_fs, g_bi, g_bd, g_bq, g_bv = unpack_call(
        n_dp, step_table.shape[0], c, after(g_q, small), got
    )
    return (
        output[None],
        grad_tokens[None],
        g_table,
        g_fg,
        g_fs,
        g_q.T,
        g_bq,
        g_k.T,
        g_v.T,
        g_bv,
        g_o,
        g_bo,
        g_sg,
        g_ss,
        g_in,
        g_bi,
        g_down,
        g_bd,
    )


def solution(mesh):
    in_specs = (
        P("dp", None, None),
        P("dp"),
        P("dp", None),
        P(),
        P(),
        P(),
        P(None, "tensor"),
        P("tensor"),
        P(None, "tensor"),
        P(None, "tensor"),
        P("tensor"),
        P("tensor", None),
        P(),
        P(),
        P(),
        P(None, "tensor"),
        P("tensor"),
        P("tensor", None),
        P(),
        P("dp", None, None),
    )
    out_specs = (
        P("dp", None, None),
        P("dp", None, None),
        P(),
        P(),
        P(),
        P(None, "tensor"),
        P("tensor"),
        P(None, "tensor"),
        P(None, "tensor"),
        P("tensor"),
        P("tensor", None),
        P(),
        P(),
        P(),
        P(None, "tensor"),
        P("tensor"),
        P("tensor", None),
        P(),
    )
    return jax.shard_map(
        functools.partial(per_device, mesh.shape["tensor"], mesh.shape["dp"]),
        mesh=mesh,
        in_specs=in_specs,
        out_specs=out_specs,
        check_vma=False,
    )
```
